256 devices in a mesh: seq: 16 (over x, z_lo), ch: 16 (over z_hi, y, core).
Axes of the slice: x: 4, y: 4, z: 8 (z_hi: 2, z_lo: 4; z = z_hi * 4 + z_lo), core: 2. Of those that a mesh axis runs over, the one named last changes fastest.
Arguments:
- signal: bfloat16 [8192, 2048], P('seq', 'ch'), may hold values from -6 to 6
- filter_raw: bfloat16 [8192, 2048], P('seq', 'ch'), may hold values from -6 to 6
- gate: bfloat16 [8192, 2048], P('seq', 'ch'), may hold values from -6 to 6
- d_out: bfloat16 [8192, 2048], P('seq', 'ch'), may hold values from -6 to 6
- w_first: bfloat16 [32, 64, 64], P('ch'), may hold values from -0.75 to 0.75
- w_second: bfloat16 [64, 32, 32], P('ch'), may hold values from -1 to 1
Outputs:
- grad_signal: bfloat16 [8192, 2048], P('seq', 'ch')
- grad_filter: bfloat16 [8192, 2048], P('seq', 'ch')
- grad_gate: bfloat16 [8192, 2048], P('seq', 'ch')
- grad_first: float32 [32, 64, 64], P('ch', 'seq')
- grad_second: float32 [64, 32, 32], P('ch', 'seq')
The draws below stay inside these ranges and needn't reach their ends.
All inputs are finite; a program needn't handle non-finite values.
Results may differ from the reference program's by a relative error of at most 0.02.
Values may be sent and summed in bfloat16 or wider, within the bound.
No kernel may reach another device: no remote copies, remote signals or barrier semaphores. Data moves between devices by JAX's collectives and lax.ppermute only.
A program may use at most 64 MiB of HBM per device.

```python
import jax
import jax.numpy as jnp
from jax import lax

WIDTH = 2048
BLOCK = 64
BLOCKS = 32
SEQ = 8192


def steps_of(own_key, extent, shards, low, high):
    loudness = 1.0
    for dim, shards_of in shards:
        heights = jax.random.uniform(jax.random.fold_in(jax.random.fold_in(own_key, 6), dim), (shards_of,), jnp.float32, low / len(shards), high / len(shards))
        loudness = loudness * jnp.repeat(jnp.exp(heights), extent[dim] // shards_of).reshape((-1,) + (1,) * (len(extent) - 1 - dim))
    return loudness


def noise(rng, extent, width, most, split=(), kind=jnp.bfloat16):
    level = steps_of(rng, extent, split, -0.22, 0.18) if split else 1.0
    entries = jax.random.normal(rng, extent, jnp.float32) * width * level
    return jnp.minimum(jnp.maximum(entries, -most), most).astype(kind)


def setup_inputs(seed: int = 0) -> dict:
    seeds = jax.random.split(jax.random.key(seed), 7)
    return {
        "signal": noise(seeds[0], (SEQ, WIDTH), 1.0, 6.0, ((0, 16), (1, 16))),
        "filter_raw": noise(seeds[1], (SEQ, WIDTH), 1.0, 6.0, ((0, 16), (1, 16))),
        "gate": noise(seeds[2], (SEQ, WIDTH), 1.0, 6.0, ((0, 16), (1, 16))),
        "d_out": noise(seeds[3], (SEQ, WIDTH), 1.0, 6.0, ((0, 16), (1, 16))),
        "w_first": noise(seeds[4], (BLOCKS, BLOCK, BLOCK), BLOCK ** -0.5, 0.75, ((0, 16),)),
        "w_second": noise(seeds[5], (BLOCK, BLOCKS, BLOCKS), BLOCKS ** -0.5, 1.0, ((0, 16),)),
    }


def block_conv(pair):
    values, kernel = pair
    count = values.shape[0]
    length = 2 * count
    spectrum = jnp.fft.rfft(values, n=length, axis=0) * jnp.fft.rfft(kernel, n=length, axis=0)
    return jnp.fft.irfft(spectrum, n=length, axis=0)[:count]


def block_adjoint(triple):
    values, kernel, incoming = triple
    count = values.shape[0]
    length = 2 * count
    incoming_spec = jnp.fft.rfft(incoming, n=length, axis=0)
    toward_signal = jnp.fft.irfft(jnp.conj(jnp.fft.rfft(kernel, n=length, axis=0)) * incoming_spec, n=length, axis=0)[:count]
    toward_filter = jnp.fft.irfft(jnp.conj(jnp.fft.rfft(values, n=length, axis=0)) * incoming_spec, n=length, axis=0)[:count]
    return toward_signal, toward_filter


def by_blocks(array):
    return jnp.transpose(array.reshape(SEQ, BLOCKS, BLOCK), (1, 0, 2))


def from_blocks(array):
    return jnp.transpose(array, (1, 0, 2)).reshape(SEQ, WIDTH)


def reference(signal, filter_raw, gate, d_out, w_first, w_second):
    scale = float(SEQ) ** -0.5
    signal_wide = signal.astype(jnp.float32)
    kernel = filter_raw.astype(jnp.float32) * scale
    conv = from_blocks(lax.map(block_conv, (by_blocks(signal_wide), by_blocks(kernel)))).astype(jnp.bfloat16)
    gate_wide = gate.astype(jnp.float32)
    product = (conv.astype(jnp.float32) * gate_wide).astype(jnp.bfloat16)
    product_blocks = product.reshape(SEQ, BLOCKS, BLOCK).astype(jnp.float32)
    first_wide = w_first.astype(jnp.float32)
    second_wide = w_second.astype(jnp.float32)
    first_mix = jnp.einsum("tij,ijk->tik", product_blocks, first_wide).astype(jnp.bfloat16)
    incoming = d_out.reshape(SEQ, BLOCK, BLOCKS).astype(jnp.float32)
    second_back = jnp.einsum("tko,kio->tki", incoming, second_wide).astype(jnp.bfloat16)
    grad_second = jnp.einsum("tik,tko->kio", first_mix.astype(jnp.float32), incoming)
    back_wide = second_back.astype(jnp.float32)
    grad_product = jnp.einsum("tki,ijk->tij", back_wide, first_wide).reshape(SEQ, WIDTH)
    grad_first = jnp.einsum("tij,tki->ijk", product_blocks, back_wide)
    grad_gate = (grad_product * conv.astype(jnp.float32)).astype(jnp.bfloat16)
    grad_conv = grad_product * gate_wide
    toward_signal, toward_filter = lax.map(block_adjoint, (by_blocks(signal_wide), by_blocks(kernel), by_blocks(grad_conv)))
    grad_signal = from_blocks(toward_signal).astype(jnp.bfloat16)
    grad_filter = (from_blocks(toward_filter) * scale).astype(jnp.bfloat16)
    return grad_signal, grad_filter, grad_gate, grad_first, grad_second
```

```python
import math

import jax
import jax.numpy as jnp
import numpy as np
from jax import lax
from jax.experimental import pallas as pl
from jax.experimental.pallas import tpu as pltpu
from jax.sharding import PartitionSpec as P

F32 = jnp.float32
BF16 = jnp.bfloat16
HIGHEST = lax.Precision.HIGHEST
NN = (((1,), (0,)), ((), ()))
NT = (((1,), (1,)), ((), ()))
TN = (((0,), (0,)), ((), ()))


def dot(a, b, form=NN):
    return lax.dot_general(a, b, form, preferred_element_type=F32)


def exact_dot(a, b, form=NN):
    return lax.dot_general(a, b, form, preferred_element_type=F32, precision=HIGHEST)


def halves(table):
    high = table.astype(BF16)
    return high, (table - high.astype(np.float32)).astype(BF16)


def tables(devices, rows):
    lanes = 128
    length = 2 * devices * rows
    steps = devices * rows // lanes
    split = rows // lanes
    place = (np.arange(steps) % devices) * split + np.arange(steps) // devices
    turn = 2.0 * math.pi
    freq = np.arange(steps) + 0.5
    angle = turn * freq[:, None] * place[None, :] / (2 * steps)
    outer = np.concatenate([np.cos(angle), -np.sin(angle)], 0)
    scale = float(devices * rows) ** -0.5 * 2.0 / length
    back = scale * np.concatenate([np.cos(angle.T), -np.sin(angle.T)], 1)
    angle = turn * freq[:, None] * np.arange(lanes)[None, :] / length
    twiddle = np.concatenate([np.cos(angle), -np.sin(angle)], 1)
    angle = turn * (np.arange(lanes)[:, None] * np.arange(lanes)[None, :] % lanes) / lanes
    cosine, sine = np.cos(angle), np.sin(angle)
    inner = np.concatenate(
        [np.concatenate([cosine, -sine], 1), np.concatenate([sine, cosine], 1)], 0
    )
    outer_high, outer_low = halves(outer.astype(np.float32))
    back_high, back_low = halves(back.astype(np.float32))
    inner_high, inner_low = halves(inner.astype(np.float32))
    return (
        np.concatenate([outer_high, outer_low], 1),
        np.stack([back_high, back_low]),
        twiddle.astype(np.float32),
        np.stack([inner_high, inner_low]),
    )


def iotas(rows, cols):
    return (
        lax.broadcasted_iota(jnp.int32, (rows, cols), 0),
        lax.broadcasted_iota(jnp.int32, (rows, cols), 1),
    )


def ones_where(mask):
    return jnp.where(mask, 1.0, 0.0).astype(BF16)


def pair_order():
    row, col = iotas(256, 256)
    return ones_where((row // 16 == col % 128 // 8) & (row // 8 % 2 == col // 128) & (row % 8 == col % 8))


def unit():
    row, col = iotas(128, 128)
    return ones_where(row == col)


def first_blocks(w_first_ref):
    flat = w_first_ref[...].reshape(128, 64)
    row, col = iotas(64, 128)
    spread = dot(flat, ones_where(row == col // 8 * 4 + col % 4))
    row, col = iotas(128, 128)
    return jnp.where(row // 64 == col // 4 % 2, spread, 0.0).astype(BF16)


def entry_kernel(signal_ref, filter_ref, d_out_ref, w_second_ref, pair_ref, back_ref):
    flat = w_second_ref[...].reshape(128, 32)
    row, col = iotas(32, 128)
    spread = dot(flat, ones_where(row == col % 32))
    row, col = iotas(128, 128)
    spread = jnp.where(row // 32 == col // 32, spread, 0.0).astype(BF16)
    order = ones_where((row // 4 == col % 32) & (row % 4 == col // 32))
    weights = dot(order, spread).astype(BF16)
    back_ref[...] = dot(weights, d_out_ref[...], NT).astype(BF16)
    both = jnp.concatenate([signal_ref[...], filter_ref[...]], axis=1)
    pair_ref[...] = dot(pair_order(), both, NT).astype(BF16)


def gate_kernel(returned_ref, w_first_ref, gate_ref, incoming_ref):
    grad_product = dot(first_blocks(w_first_ref), returned_ref[...])
    gate = dot(unit(), gate_ref[...], NT)
    incoming_ref[...] = (grad_product * gate).astype(BF16)


def split(value):
    high = value.astype(BF16)
    return high, (value - high.astype(F32)).astype(BF16)


def by_channel(wide_ref, first, stride):
    columns = [wide_ref[pl.ds(first + c, 64, stride=stride), :] for c in range(8)]
    return jnp.concatenate(columns, axis=1).astype(BF16)


def by_slab(wide_ref, value, first, stride):
    for c in range(8):
        wide_ref[pl.ds(first + c, 64, stride=stride), :] = value[:, 128 * c : 128 * c + 128]


def unroll(wide_ref, value):
    rows = value.shape[0]
    for th in range(4):
        wide_ref[rows * th : rows * th + rows, :] = value[:, 128 * th : 128 * th + 128].astype(F32)


def enroll(wide_ref):
    rows = wide_ref.shape[0] // 4
    pieces = [wide_ref[rows * th : rows * th + rows, :].astype(BF16) for th in range(4)]
    return jnp.concatenate(pieces, axis=1)


def transform(values, outer_ref, twiddle_ref, inner_ref):
    stage = dot(outer_ref[...], jnp.concatenate([values, values], axis=0))
    cosine, sine = twiddle_ref[:, 0:128], twiddle_ref[:, 128:256]
    rows = []
    for c in range(8):
        real = stage[0:64, 128 * c : 128 * c + 128]
        imag = stage[64:128, 128 * c : 128 * c + 128]
        rows.append(
            jnp.concatenate([real * cosine - imag * sine, real * sine + imag * cosine], axis=1)
        )
    high, low = split(jnp.concatenate(rows, axis=0))
    return dot(high, inner_ref[0]) + dot(low, inner_ref[0]) + dot(high, inner_ref[1])


def restore(real, imag, back_ref, twiddle_ref, inner_ref):
    high, low = split(jnp.concatenate([real, imag], axis=1))
    stage = dot(high, inner_ref[0], NT) + dot(low, inner_ref[0], NT) + dot(high, inner_ref[1], NT)
    cosine, sine = twiddle_ref[:, 0:128], twiddle_ref[:, 128:256]
    columns = []
    for c in range(8):
        real = stage[64 * c : 64 * c + 64, 0:128]
        imag = stage[64 * c : 64 * c + 64, 128:256]
        columns.append(
            jnp.concatenate([real * cosine + imag * sine, imag * cosine - real * sine], axis=0)
        )
    high, low = split(jnp.concatenate(columns, axis=1))
    return dot(back_ref[0], high) + dot(back_ref[0], low) + dot(back_ref[1], high)


def conv_kernel(
    pair_ref, outer_ref, back_ref, twiddle_ref, inner_ref, conv_ref, spectra_ref, wide_ref, out_ref
):
    unroll(wide_ref, pair_ref[...])
    signal = transform(by_channel(wide_ref, 0, 16), outer_ref, twiddle_ref, inner_ref)
    kernel = transform(by_channel(wide_ref, 8, 16), outer_ref, twiddle_ref, inner_ref)
    spectra_ref[0] = signal
    spectra_ref[1] = kernel
    sr, si = signal[:, 0:128], signal[:, 128:256]
    kr, ki = kernel[:, 0:128], kernel[:, 128:256]
    result = restore(sr * kr - si * ki, sr * ki + si * kr, back_ref, twiddle_ref, inner_ref)
    by_slab(out_ref, result, 0, 8)
    conv_ref[...] = enroll(out_ref)


def adjoint_kernel(
    incoming_ref, spectra_ref, outer_ref, back_ref, twiddle_ref, inner_ref, pair_ref, wide_ref, out_ref
):
    unroll(wide_ref, incoming_ref[...])
    spectrum = transform(by_channel(wide_ref, 0, 8), outer_ref, twiddle_ref, inner_ref)
    gr, gi = spectrum[:, 0:128], spectrum[:, 128:256]
    for field in range(2):
        real, imag = spectra_ref[1 - field, :, 0:128], spectra_ref[1 - field, :, 128:256]
        result = restore(
            gr * real + gi * imag, gi * real - gr * imag, back_ref, twiddle_ref, inner_ref
        )
        by_slab(out_ref, result, 8 * field, 16)
    pair_ref[...] = enroll(out_ref)


def mix_kernel(conv_ref, gate_ref, w_first_ref, mix_ref):
    gate = dot(unit(), gate_ref[...], NT)
    product = (conv_ref[...].astype(F32) * gate).astype(BF16)
    mix_ref[...] = dot(first_blocks(w_first_ref), product, TN).astype(BF16)


def first_kernel(conv_ref, gate_ref, returned_ref, w_first_ref, grad_gate_ref, partial_ref):
    gate = dot(unit(), gate_ref[...], NT)
    conv = conv_ref[...].astype(F32)
    product = (conv * gate).astype(BF16)
    returned = returned_ref[...]
    grad_product = dot(first_blocks(w_first_ref), returned)
    grad_gate = (grad_product * conv).astype(BF16)
    grad_gate_ref[...] = dot(grad_gate, unit(), TN).astype(BF16)
    row, col = iotas(128, 128)
    grad = jnp.where(row // 64 == col // 4 % 2, dot(product, returned, NT), 0.0)
    order = jnp.where(
        (row // 8 == col % 64 // 4) & (row // 4 % 2 == col // 64) & (row % 4 == col % 4), 1.0, 0.0
    )
    row, col = iotas(128, 64)
    fold = jnp.where(row // 8 * 4 + row % 4 == col, 1.0, 0.0)
    partial_ref[...] = exact_dot(order, exact_dot(grad, fold))


def exit_kernel(pair_ref, signal_ref, filter_ref):
    both = dot(pair_ref[...], pair_order(), TN).astype(BF16)
    signal_ref[...] = both[:, 0:128]
    filter_ref[...] = both[:, 128:256]


def second_kernel(received_ref, d_out_ref, partial_ref, sums_ref):
    row, col = iotas(128, 128)
    grad = jnp.where(row % 4 == col // 32, dot(received_ref[...], d_out_ref[...]), 0.0)
    row, col = iotas(128, 64)
    fold = jnp.where(row % 32 == col, 1.0, 0.0)
    sums_ref[...] = jnp.concatenate([partial_ref[...], exact_dot(grad, fold)], axis=1)


def sum_kernel(sums_ref, first_ref, second_ref):
    total = sums_ref[0:8, :]
    for s in range(1, 16):
        total = total + sums_ref[8 * s : 8 * s + 8, :]
    for i in range(2):
        first_ref[i] = total[4 * i : 4 * i + 4, 0:64]
        for k in range(4):
            second_ref[k, i : i + 1, :] = total[4 * i + k : 4 * i + k + 1, 64:96]


def call(body, outs, scratch=(), flops=1 << 26, moved=1 << 19):
    return pl.pallas_call(
        body,
        out_shape=[jax.ShapeDtypeStruct(shape, kind) for shape, kind in outs],
        scratch_shapes=list(scratch),
        compiler_params=pltpu.CompilerParams(vmem_limit_bytes=32 << 20),
        cost_estimate=pl.CostEstimate(flops=flops, bytes_accessed=moved, transcendentals=0),
    )


def exchange(value, axis):
    rows, cols = value.shape
    pieces = value.reshape(16, rows // 16, cols)
    return lax.all_to_all(pieces, axis, split_axis=0, concat_axis=0, tiled=True).reshape(rows, cols)


def shards(signal, filter_raw, gate, d_out, w_first, w_second):
    rows, width = signal.shape
    outer, back, twiddle, inner = (jnp.asarray(t) for t in tables(lax.axis_size("seq"), rows))
    pair, second_back = call(
        entry_kernel, [((2 * width, rows), BF16), ((width, rows), BF16)]
    )(signal, filter_raw, d_out, w_second)
    returned = exchange(second_back, "ch")
    pair = exchange(pair, "seq")
    conv, spectra = call(
        conv_kernel,
        [((width, rows), BF16), ((2, 512, 256), F32)],
        [pltpu.VMEM((2 * width * 4, 128), F32), pltpu.VMEM((width * 4, 128), F32)],
        flops=1 << 30,
    )(pair, outer, back, twiddle, inner)
    conv = exchange(conv, "seq")
    incoming = call(gate_kernel, [((width, rows), BF16)])(returned, w_first, gate)[0]
    incoming = exchange(incoming, "seq")
    grads = call(
        adjoint_kernel,
        [((2 * width, rows), BF16)],
        [pltpu.VMEM((width * 4, 128), F32), pltpu.VMEM((2 * width * 4, 128), F32)],
        flops=1 << 30,
    )(incoming, spectra, outer, back, twiddle, inner)[0]
    grads = exchange(grads, "seq")
    mix = call(mix_kernel, [((width, rows), BF16)])(conv, gate, w_first)[0]
    received = exchange(mix, "ch")
    grad_gate, partial = call(first_kernel, [((rows, width), BF16), ((width, 64), F32)])(
        conv, gate, returned, w_first
    )
    grad_signal, grad_filter = call(exit_kernel, [((rows, width), BF16), ((rows, width), BF16)])(grads)
    sums = call(second_kernel, [((width, 128), F32)])(received, d_out, partial)[0]
    sums = exchange(sums, "seq")
    grad_first, grad_second = call(sum_kernel, [((2, 4, 64), F32), ((4, 2, 32), F32)])(sums)
    return (grad_signal, grad_filter, grad_gate, grad_first, grad_second)


def solution(mesh):
    in_specs = (
        P("seq", "ch"),
        P("seq", "ch"),
        P("seq", "ch"),
        P("seq", "ch"),
        P("ch", None, None),
        P("ch", None, None),
    )
    out_specs = (
        P("seq", "ch"),
        P("seq", "ch"),
        P("seq", "ch"),
        P("ch", "seq", None),
        P("ch", "seq", None),
    )
    return jax.shard_map(shards, mesh=mesh, in_specs=in_specs, out_specs=out_specs, check_vma=False)
```

```python
import math

import jax
import jax.numpy as jnp
import numpy as np
from jax import lax
from jax.experimental import pallas as pl
from jax.experimental.pallas import tpu as pltpu
from jax.sharding import PartitionSpec as P

F32 = jnp.float32
BF16 = jnp.bfloat16
NN = (((1,), (0,)), ((), ()))
NT = (((1,), (1,)), ((), ()))
TN = (((0,), (0,)), ((), ()))


def dot(a, b, form=NN):
    return lax.dot_general(a, b, form, preferred_element_type=F32)


def halves(table):
    high = table.astype(BF16)
    return high, (table - high.astype(np.float32)).astype(BF16)


def tables(devices, rows):
    lanes = 128
    length = 2 * devices * rows
    steps = devices * rows // lanes
    split = rows // lanes
    place = (np.arange(steps) % devices) * split + np.arange(steps) // devices
    turn = 2.0 * math.pi
    freq = np.arange(steps) + 0.5
    angle = turn * freq[:, None] * place[None, :] / (2 * steps)
    outer = np.concatenate([np.cos(angle), -np.sin(angle)], 0)
    scale = float(devices * rows) ** -0.5 * 2.0 / length
    back = scale * np.concatenate([np.cos(angle.T), -np.sin(angle.T)], 1)
    angle = turn * freq[:, None] * np.arange(lanes)[None, :] / length
    twiddle = np.concatenate([np.cos(angle), -np.sin(angle)], 1)
    angle = turn * (np.arange(lanes)[:, None] * np.arange(lanes)[None, :] % lanes) / lanes
    cosine, sine = np.cos(angle), np.sin(angle)
    inner = np.concatenate(
        [np.concatenate([cosine, -sine], 1), np.concatenate([sine, cosine], 1)], 0
    )
    outer_high, outer_low = halves(outer.astype(np.float32))
    back_high, back_low = halves(back.astype(np.float32))
    inner_high, inner_low = halves(inner.astype(np.float32))
    return (
        np.concatenate([outer_high, outer_low], 1),
        np.stack([back_high, back_low]),
        twiddle.astype(np.float32),
        np.stack([inner_high, inner_low]),
    )


def iotas(rows, cols):
    return (
        lax.broadcasted_iota(jnp.int32, (rows, cols), 0),
        lax.broadcasted_iota(jnp.int32, (rows, cols), 1),
    )


def ones_where(mask):
    return jnp.where(mask, 1.0, 0.0).astype(BF16)


def pair_order():
    row, col = iotas(256, 256)
    return ones_where((row // 16 == col % 128 // 8) & (row // 8 % 2 == col // 128) & (row % 8 == col % 8))


def unit():
    row, col = iotas(128, 128)
    return ones_where(row == col)


def pair_kernel(signal_hbm, filter_hbm, pair_ref, both_ref, sems):
    copies = [
        pltpu.make_async_copy(source, both_ref.at[field], sems.at[field])
        for field, source in enumerate((signal_hbm, filter_hbm))
    ]
    for copy in copies:
        copy.start()
    order = pair_order()
    for copy in copies:
        copy.wait()
    both = jnp.concatenate([both_ref[0], both_ref[1]], axis=1)
    pair_ref[...] = dot(order, both, NT).astype(BF16)


def back_kernel(d_out_ref, w_second_ref, back_ref):
    flat = w_second_ref[...].reshape(128, 32)
    row, col = iotas(32, 128)
    spread = dot(flat, ones_where(row == col % 32))
    row, col = iotas(128, 128)
    spread = jnp.where(row // 32 == col // 32, spread, 0.0).astype(BF16)
    order = ones_where((row // 4 == col % 32) & (row % 4 == col // 32))
    weights = dot(order, spread).astype(BF16)
    back_ref[...] = dot(weights, d_out_ref[...], NT).astype(BF16)


def prepare_kernel(gate_ref, w_first_ref, gate_out_ref, blocks_ref):
    flat = w_first_ref[...].reshape(128, 64)
    row, col = iotas(64, 128)
    spread = dot(flat, ones_where(row == col // 8 * 4 + col % 4))
    row, col = iotas(128, 128)
    blocks_ref[...] = jnp.where(row // 64 == col // 4 % 2, spread, 0.0).astype(BF16)
    gate_out_ref[...] = dot(unit(), gate_ref[...], NT)


def gate_kernel(returned_ref, blocks_ref, gate_ref, conv_ref, pair_ref):
    incoming = dot(blocks_ref[...], returned_ref[...]) * gate_ref[...]
    rows = []
    for p in range(16):
        pieces = [conv_ref[128 * th + 8 * p : 128 * th + 8 * p + 8, :] for th in range(4)]
        rows.append(jnp.concatenate(pieces, axis=1))
        rows.append(incoming[8 * p : 8 * p + 8, :])
    pair_ref[...] = jnp.concatenate(rows, axis=0).astype(BF16)


def split(value):
    high = value.astype(BF16)
    return high, (value - high.astype(F32)).astype(BF16)


def by_channel(wide_ref, first, stride):
    columns = [wide_ref[pl.ds(first + c, 64, stride=stride), :] for c in range(8)]
    return jnp.concatenate(columns, axis=1).astype(BF16)


def by_slab(wide_ref, value, first, stride):
    for c in range(8):
        wide_ref[pl.ds(first + c, 64, stride=stride), :] = value[:, 128 * c : 128 * c + 128]


def unroll(wide_ref, value):
    rows = value.shape[0]
    for th in range(4):
        wide_ref[rows * th : rows * th + rows, :] = value[:, 128 * th : 128 * th + 128].astype(F32)


def enroll(wide_ref):
    rows = wide_ref.shape[0] // 4
    pieces = [wide_ref[rows * th : rows * th + rows, :].astype(BF16) for th in range(4)]
    return jnp.concatenate(pieces, axis=1)


def transform(values, outer_ref, twiddle_ref, inner_ref):
    stage = dot(outer_ref[...], jnp.concatenate([values, values], axis=0))
    cosine, sine = twiddle_ref[:, 0:128], twiddle_ref[:, 128:256]
    rows = []
    for c in range(8):
        real = stage[0:64, 128 * c : 128 * c + 128]
        imag = stage[64:128, 128 * c : 128 * c + 128]
        rows.append(
            jnp.concatenate([real * cosine - imag * sine, real * sine + imag * cosine], axis=1)
        )
    high, low = split(jnp.concatenate(rows, axis=0))
    return dot(high, inner_ref[0]) + dot(low, inner_ref[0]) + dot(high, inner_ref[1])


def restore(real, imag, back_ref, twiddle_ref, inner_ref):
    high, low = split(jnp.concatenate([real, imag], axis=1))
    stage = dot(high, inner_ref[0], NT) + dot(low, inner_ref[0], NT) + dot(high, inner_ref[1], NT)
    cosine, sine = twiddle_ref[:, 0:128], twiddle_ref[:, 128:256]
    columns = []
    for c in range(8):
        real = stage[64 * c : 64 * c + 64, 0:128]
        imag = stage[64 * c : 64 * c + 64, 128:256]
        columns.append(
            jnp.concatenate([real * cosine + imag * sine, imag * cosine - real * sine], axis=0)
        )
    high, low = split(jnp.concatenate(columns, axis=1))
    return dot(back_ref[0], high) + dot(back_ref[0], low) + dot(back_ref[1], high)


def conv_kernel(pair_ref, outer_ref, back_ref, twiddle_ref, inner_ref, conv_ref, spectra_ref, wide_ref):
    unroll(wide_ref, pair_ref[...])
    signal = transform(by_channel(wide_ref, 0, 16), outer_ref, twiddle_ref, inner_ref)
    kernel = transform(by_channel(wide_ref, 8, 16), outer_ref, twiddle_ref, inner_ref)
    spectra_ref[0] = signal
    spectra_ref[1] = kernel
    sr, si = signal[:, 0:128], signal[:, 128:256]
    kr, ki = kernel[:, 0:128], kernel[:, 128:256]
    result = restore(sr * kr - si * ki, sr * ki + si * kr, back_ref, twiddle_ref, inner_ref)
    by_slab(conv_ref, result, 0, 8)


def adjoint_kernel(
    pair_ref, spectra_ref, outer_ref, back_ref, twiddle_ref, inner_ref, grads_ref, wide_ref, out_ref
):
    unroll(wide_ref, pair_ref[...])
    spectrum = transform(by_channel(wide_ref, 8, 16), outer_ref, twiddle_ref, inner_ref)
    gr, gi = spectrum[:, 0:128], spectrum[:, 128:256]
    for field in range(2):
        real, imag = spectra_ref[1 - field, :, 0:128], spectra_ref[1 - field, :, 128:256]
        result = restore(
            gr * real + gi * imag, gi * real - gr * imag, back_ref, twiddle_ref, inner_ref
        )
        by_slab(out_ref, result, 8 * field, 16)
    grads_ref[...] = enroll(out_ref)


def conv_rows(pair_ref):
    wide = pair_ref[...].astype(F32)
    return jnp.concatenate([wide[16 * p : 16 * p + 8, :] for p in range(16)], axis=0)


def mix_kernel(pair_ref, gate_ref, blocks_ref, mix_ref):
    product = (conv_rows(pair_ref) * gate_ref[...]).astype(BF16)
    mix_ref[...] = dot(blocks_ref[...], product, TN).astype(BF16)


def first_kernel(pair_ref, gate_ref, returned_ref, blocks_ref, grad_gate_ref, partial_ref):
    conv = conv_rows(pair_ref)
    product = (conv * gate_ref[...]).astype(BF16)
    returned = returned_ref[...]
    grad_gate = (dot(blocks_ref[...], returned) * conv).astype(BF16)
    grad_gate_ref[...] = dot(grad_gate, unit(), TN).astype(BF16)
    row, col = iotas(128, 128)
    grad = jnp.where(row // 64 == col // 4 % 2, dot(product, returned, NT), 0.0)
    order = ones_where(
        (row // 8 == col % 64 // 4) & (row // 4 % 2 == col // 64) & (row % 4 == col % 4)
    )
    row, col = iotas(128, 64)
    fold = ones_where(row // 8 * 4 + row % 4 == col)
    for part, piece in enumerate(split(grad)):
        partial_ref[part] = dot(order, dot(piece, fold).astype(BF16))


def second_kernel(received_ref, d_out_ref, partial_ref, grads_ref, sums_ref):
    row, col = iotas(128, 128)
    grad = jnp.where(row % 4 == col // 32, dot(received_ref[...], d_out_ref[...]), 0.0)
    row, col = iotas(128, 64)
    fold = ones_where(row % 32 == col)
    high, low = [
        jnp.concatenate([partial_ref[part], dot(piece, fold)], axis=1)
        for part, piece in enumerate(split(grad))
    ]
    rows = []
    for p in range(16):
        rows.append(high[8 * p : 8 * p + 8, :])
        rows.append(low[8 * p : 8 * p + 8, :])
    sums_ref[:, 0:512] = grads_ref[...]
    sums_ref[:, 512:640] = jnp.concatenate(rows, axis=0).astype(BF16)


def exit_kernel(sums_ref, signal_ref, filter_ref, first_ref, second_ref):
    both = dot(sums_ref[:, 0:512], pair_order(), TN).astype(BF16)
    signal_ref[...] = both[:, 0:128]
    filter_ref[...] = both[:, 128:256]
    wide = sums_ref[:, 512:640].astype(F32)
    total = wide[0:16, :]
    for p in range(1, 16):
        total = total + wide[16 * p : 16 * p + 16, :]
    total = total[0:8, :] + total[8:16, :]
    for i in range(2):
        first_ref[i] = total[4 * i : 4 * i + 4, 0:64]
        for k in range(4):
            second_ref[k, i : i + 1, :] = total[4 * i + k : 4 * i + k + 1, 64:96]


def call(body, outs, scratch=(), flops=1 << 26, moved=1 << 19, held=None):
    extra = {}
    if held is not None:
        extra["in_specs"] = [pl.BlockSpec(memory_space=held[0])] * held[1]
    return pl.pallas_call(
        body,
        out_shape=[jax.ShapeDtypeStruct(shape, kind) for shape, kind in outs],
        scratch_shapes=list(scratch),
        compiler_params=pltpu.CompilerParams(vmem_limit_bytes=32 << 20),
        cost_estimate=pl.CostEstimate(flops=flops, bytes_accessed=moved, transcendentals=0),
        **extra,
    )


def exchange(value, axis):
    rows, cols = value.shape
    pieces = value.reshape(16, rows // 16, cols)
    return lax.all_to_all(pieces, axis, split_axis=0, concat_axis=0, tiled=True).reshape(rows, cols)


def shards(signal, filter_raw, gate, d_out, w_first, w_second):
    rows, width = signal.shape
    outer, back, twiddle, inner = (jnp.asarray(t) for t in tables(lax.axis_size("seq"), rows))
    single, double = ((width, rows), BF16), ((2 * width, rows), BF16)
    slab = ((rows, width), BF16)
    pair = call(
        pair_kernel,
        [double],
        [pltpu.VMEM((2, rows, width), BF16), pltpu.SemaphoreType.DMA((2,))],
        held=(pltpu.HBM, 2),
    )(signal, filter_raw)[0]
    pair = exchange(pair, "seq")
    second_back = call(back_kernel, [single])(d_out, w_second)[0]
    gate, blocks = call(prepare_kernel, [((width, rows), F32), ((128, 128), BF16)])(gate, w_first)
    returned = exchange(second_back, "ch")
    conv, spectra = call(
        conv_kernel,
        [((4 * width, 128), F32), ((2, 512, 256), F32)],
        [pltpu.VMEM((2 * width * 4, 128), F32)],
        flops=1 << 30,
    )(pair, outer, back, twiddle, inner)
    pair = call(gate_kernel, [double])(returned, blocks, gate, conv)[0]
    pair = exchange(pair, "seq")
    mix = call(mix_kernel, [single])(pair, gate, blocks)[0]
    received = exchange(mix, "ch")
    grads = call(
        adjoint_kernel,
        [double],
        [pltpu.VMEM((2 * width * 4, 128), F32), pltpu.VMEM((2 * width * 4, 128), F32)],
        flops=1 << 30,
    )(pair, spectra, outer, back, twiddle, inner)[0]
    grad_gate, partial = call(first_kernel, [slab, ((2, width, 64), F32)])(
        pair, gate, returned, blocks
    )
    sums = call(second_kernel, [((2 * width, rows + 128), BF16)])(received, d_out, partial, grads)[0]
    sums = exchange(sums, "seq")
    grad_signal, grad_filter, grad_first, grad_second = call(
        exit_kernel, [slab, slab, ((2, 4, 64), F32), ((4, 2, 32), F32)]
    )(sums)
    return (grad_signal, grad_filter, grad_gate, grad_first, grad_second)


def solution(mesh):
    in_specs = (
        P("seq", "ch"),
        P("seq", "ch"),
        P("seq", "ch"),
        P("seq", "ch"),
        P("ch", None, None),
        P("ch", None, None),
    )
    out_specs = (
        P("seq", "ch"),
        P("seq", "ch"),
        P("seq", "ch"),
        P("ch", "seq", None),
        P("ch", "seq", None),
    )
    return jax.shard_map(shards, mesh=mesh, in_specs=in_specs, out_specs=out_specs, check_vma=False)
```

```python
import math

import jax
import jax.numpy as jnp
import numpy as np
from jax import lax
from jax.experimental import pallas as pl
from jax.experimental.pallas import tpu as pltpu
from jax.sharding import PartitionSpec as P

F32 = jnp.float32
BF16 = jnp.bfloat16
NN = (((1,), (0,)), ((), ()))
NT = (((1,), (1,)), ((), ()))
TN = (((0,), (0,)), ((), ()))


def dot(a, b, form=NN):
    return lax.dot_general(a, b, form, preferred_element_type=F32)


def halves(table):
    high = table.astype(BF16)
    return high, (table - high.astype(np.float32)).astype(BF16)


def tables(devices, rows):
    lanes = 128
    length = 2 * devices * rows
    steps = devices * rows // lanes
    split = rows // lanes
    place = (np.arange(steps) % devices) * split + np.arange(steps) // devices
    turn = 2.0 * math.pi
    freq = np.arange(steps) + 0.5
    angle = turn * freq[:, None] * place[None, :] / (2 * steps)
    outer = np.concatenate([np.cos(angle), -np.sin(angle)], 0)
    scale = float(devices * rows) ** -0.5 * 2.0 / length
    back = scale * np.concatenate([np.cos(angle.T), -np.sin(angle.T)], 1)
    angle = turn * freq[:, None] * np.arange(lanes)[None, :] / length
    twiddle = np.concatenate([np.cos(angle), -np.sin(angle)], 1)
    angle = turn * (np.arange(lanes)[:, None] * np.arange(lanes)[None, :] % lanes) / lanes
    cosine, sine = np.cos(angle), np.sin(angle)
    inner = np.concatenate(
        [np.concatenate([cosine, -sine], 1), np.concatenate([sine, cosine], 1)], 0
    )
    outer_high, outer_low = halves(outer.astype(np.float32))
    back_high, back_low = halves(back.astype(np.float32))
    inner_high, inner_low = halves(inner.astype(np.float32))
    return (
        np.concatenate([outer_high, outer_low], 1),
        np.stack([back_high, back_low]),
        twiddle.astype(np.float32),
        np.stack([inner_high, inner_low]),
    )


def iotas(rows, cols):
    return (
        lax.broadcasted_iota(jnp.int32, (rows, cols), 0),
        lax.broadcasted_iota(jnp.int32, (rows, cols), 1),
    )


def ones_where(mask):
    return jnp.where(mask, 1.0, 0.0).astype(BF16)


def pair_order():
    row, col = iotas(256, 256)
    return ones_where((row // 16 == col % 128 // 8) & (row // 8 % 2 == col // 128) & (row % 8 == col % 8))


def unit():
    row, col = iotas(128, 128)
    return ones_where(row == col)


def pair_kernel(signal_hbm, filter_hbm, pair_ref, both_ref, sems):
    copies = [
        pltpu.make_async_copy(source, both_ref.at[field], sems.at[field])
        for field, source in enumerate((signal_hbm, filter_hbm))
    ]
    for copy in copies:
        copy.start()
    order = pair_order()
    for copy in copies:
        copy.wait()
    both = jnp.concatenate([both_ref[0], both_ref[1]], axis=1)
    pair_ref[...] = dot(order, both, NT).astype(BF16)


def place():
    index = lax.axis_index("ch")
    return index // 8, index // 2 % 4, index % 2


def partner(slot_y, slot_zc, step):
    z, y, core = place()
    z = (z + slot_zc // 2) % 2
    core = (core + slot_zc) % 2
    y = (y + 4 + step * slot_y) % 4
    return z * 8 + y * 2 + core


def back_kernel(d_out_ref, w_second_ref, near_ref, core_ref, far_ref, cross_ref):
    flat = w_second_ref[...].reshape(128, 32)
    row, col = iotas(32, 128)
    spread = dot(flat, ones_where(row == col % 32))
    row, col = iotas(128, 128)
    spread = jnp.where(row // 32 == col // 32, spread, 0.0).astype(BF16)
    block = 2 * partner(row // 8 % 4, row // 32, 1) + row // 4 % 2
    order = ones_where((block == col % 32) & (row % 4 == col // 32))
    weights = dot(order, spread).astype(BF16)
    result = dot(weights, d_out_ref[...], NT).astype(BF16)
    for zc, ref in enumerate((near_ref, core_ref, far_ref, cross_ref)):
        ref[...] = result[32 * zc : 32 * zc + 32, :]


def repack_kernel(*refs):
    values = [ref[...].astype(F32) for ref in refs[:4]]
    for y, ref in enumerate(refs[4:]):
        ref[...] = jnp.concatenate([v[8 * y : 8 * y + 8, :] for v in values], axis=0).astype(BF16)


def source(col):
    return partner(col // 32, col // 8 % 4, -1)


def prepare_kernel(gate_ref, w_first_ref, gate_out_ref, blocks_ref, own_ref):
    flat = w_first_ref[...].reshape(128, 64)
    row, col = iotas(64, 128)
    keep_row, keep_col = iotas(128, 128)
    keep = keep_row // 64 == keep_col // 4 % 2
    for ref, group in ((blocks_ref, col // 8), (own_ref, source(col))):
        spread = dot(flat, ones_where(row == group * 4 + col % 4))
        ref[...] = jnp.where(keep, spread, 0.0).astype(BF16)
    gate_out_ref[...] = dot(unit(), gate_ref[...], NT)


def gate_kernel(near_ref, first_ref, second_ref, third_ref, own_ref, gate_ref, conv_ref, pair_ref, returned_ref):
    pieces = [ref[...] for ref in (near_ref, first_ref, second_ref, third_ref)]
    returned = jnp.concatenate(pieces, axis=0)
    returned_ref[...] = returned
    incoming = dot(own_ref[...], returned) * gate_ref[...]
    rows = []
    for p in range(16):
        pieces = [conv_ref[128 * th + 8 * p : 128 * th + 8 * p + 8, :] for th in range(4)]
        rows.append(jnp.concatenate(pieces, axis=1))
        rows.append(incoming[8 * p : 8 * p + 8, :])
    pair_ref[...] = jnp.concatenate(rows, axis=0).astype(BF16)


def split(value):
    high = value.astype(BF16)
    return high, (value - high.astype(F32)).astype(BF16)


def by_channel(wide_ref, first, stride):
    columns = [wide_ref[pl.ds(first + c, 64, stride=stride), :] for c in range(8)]
    return jnp.concatenate(columns, axis=1).astype(BF16)


def by_slab(wide_ref, value, first, stride):
    for c in range(8):
        wide_ref[pl.ds(first + c, 64, stride=stride), :] = value[:, 128 * c : 128 * c + 128]


def unroll(wide_ref, value):
    rows = value.shape[0]
    for th in range(4):
        wide_ref[rows * th : rows * th + rows, :] = value[:, 128 * th : 128 * th + 128].astype(F32)


def enroll(wide_ref):
    rows = wide_ref.shape[0] // 4
    pieces = [wide_ref[rows * th : rows * th + rows, :].astype(BF16) for th in range(4)]
    return jnp.concatenate(pieces, axis=1)


def transform(values, outer_ref, twiddle_ref, inner_ref):
    stage = dot(outer_ref[...], jnp.concatenate([values, values], axis=0))
    cosine, sine = twiddle_ref[:, 0:128], twiddle_ref[:, 128:256]
    rows = []
    for c in range(8):
        real = stage[0:64, 128 * c : 128 * c + 128]
        imag = stage[64:128, 128 * c : 128 * c + 128]
        rows.append(
            jnp.concatenate([real * cosine - imag * sine, real * sine + imag * cosine], axis=1)
        )
    high, low = split(jnp.concatenate(rows, axis=0))
    return dot(high, inner_ref[0]) + dot(low, inner_ref[0]) + dot(high, inner_ref[1])


def restore(real, imag, back_ref, twiddle_ref, inner_ref):
    high, low = split(jnp.concatenate([real, imag], axis=1))
    stage = dot(high, inner_ref[0], NT) + dot(low, inner_ref[0], NT) + dot(high, inner_ref[1], NT)
    cosine, sine = twiddle_ref[:, 0:128], twiddle_ref[:, 128:256]
    columns = []
    for c in range(8):
        real = stage[64 * c : 64 * c + 64, 0:128]
        imag = stage[64 * c : 64 * c + 64, 128:256]
        columns.append(
            jnp.concatenate([real * cosine + imag * sine, imag * cosine - real * sine], axis=0)
        )
    high, low = split(jnp.concatenate(columns, axis=1))
    return dot(back_ref[0], high) + dot(back_ref[0], low) + dot(back_ref[1], high)


def conv_kernel(pair_ref, outer_ref, back_ref, twiddle_ref, inner_ref, conv_ref, spectra_ref, wide_ref):
    unroll(wide_ref, pair_ref[...])
    signal = transform(by_channel(wide_ref, 0, 16), outer_ref, twiddle_ref, inner_ref)
    kernel = transform(by_channel(wide_ref, 8, 16), outer_ref, twiddle_ref, inner_ref)
    spectra_ref[0] = signal
    spectra_ref[1] = kernel
    sr, si = signal[:, 0:128], signal[:, 128:256]
    kr, ki = kernel[:, 0:128], kernel[:, 128:256]
    result = restore(sr * kr - si * ki, sr * ki + si * kr, back_ref, twiddle_ref, inner_ref)
    by_slab(conv_ref, result, 0, 8)


def adjoint_kernel(
    pair_ref, spectra_ref, outer_ref, back_ref, twiddle_ref, inner_ref, grads_ref, wide_ref, out_ref
):
    unroll(wide_ref, pair_ref[...])
    spectrum = transform(by_channel(wide_ref, 8, 16), outer_ref, twiddle_ref, inner_ref)
    gr, gi = spectrum[:, 0:128], spectrum[:, 128:256]
    for field in range(2):
        real, imag = spectra_ref[1 - field, :, 0:128], spectra_ref[1 - field, :, 128:256]
        result = restore(
            gr * real + gi * imag, gi * real - gr * imag, back_ref, twiddle_ref, inner_ref
        )
        by_slab(out_ref, result, 8 * field, 16)
    grads_ref[...] = enroll(out_ref)


def conv_rows(pair_ref):
    wide = pair_ref[...].astype(F32)
    return jnp.concatenate([wide[16 * p : 16 * p + 8, :] for p in range(16)], axis=0)


def mix_kernel(pair_ref, gate_ref, blocks_ref, mix_ref):
    product = (conv_rows(pair_ref) * gate_ref[...]).astype(BF16)
    mix_ref[...] = dot(blocks_ref[...], product, TN).astype(BF16)


def first_kernel(pair_ref, gate_ref, returned_ref, own_ref, grad_gate_ref, partial_ref):
    conv = conv_rows(pair_ref)
    product = (conv * gate_ref[...]).astype(BF16)
    returned = returned_ref[...]
    grad_gate = (dot(own_ref[...], returned) * conv).astype(BF16)
    grad_gate_ref[...] = dot(grad_gate, unit(), TN).astype(BF16)
    row, col = iotas(128, 128)
    grad = jnp.where(row // 64 == col // 4 % 2, dot(product, returned, NT), 0.0)
    order = ones_where(
        (row // 8 == col % 64 // 4) & (row // 4 % 2 == col // 64) & (row % 4 == col % 4)
    )
    row, col = iotas(128, 64)
    fold = ones_where(source(row) * 4 + row % 4 == col)
    for part, piece in enumerate(split(grad)):
        partial_ref[part] = dot(order, dot(piece, fold).astype(BF16))


def second_kernel(received_ref, d_out_ref, partial_ref, grads_ref, sums_ref):
    row, col = iotas(128, 128)
    grad = jnp.where(row % 4 == col // 32, dot(received_ref[...], d_out_ref[...]), 0.0)
    row, col = iotas(128, 64)
    fold = ones_where(row % 32 == col)
    high, low = [
        jnp.concatenate([partial_ref[part], dot(piece, fold)], axis=1)
        for part, piece in enumerate(split(grad))
    ]
    rows = []
    for p in range(16):
        rows.append(high[8 * p : 8 * p + 8, :])
        rows.append(low[8 * p : 8 * p + 8, :])
    sums_ref[:, 0:512] = grads_ref[...]
    sums_ref[:, 512:640] = jnp.concatenate(rows, axis=0).astype(BF16)


def exit_kernel(sums_ref, signal_ref, filter_ref, first_ref, second_ref):
    both = dot(sums_ref[:, 0:512], pair_order(), TN).astype(BF16)
    signal_ref[...] = both[:, 0:128]
    filter_ref[...] = both[:, 128:256]
    wide = sums_ref[:, 512:640].astype(F32)
    total = wide[0:16, :]
    for p in range(1, 16):
        total = total + wide[16 * p : 16 * p + 16, :]
    total = total[0:8, :] + total[8:16, :]
    for i in range(2):
        first_ref[i] = total[4 * i : 4 * i + 4, 0:64]
        for k in range(4):
            second_ref[k, i : i + 1, :] = total[4 * i + k : 4 * i + k + 1, 64:96]


def call(body, outs, scratch=(), flops=1 << 26, moved=1 << 19, held=None, limit=32 << 20):
    extra = {}
    if held is not None:
        extra["in_specs"] = [pl.BlockSpec(memory_space=held[0])] * held[1]
    return pl.pallas_call(
        body,
        out_shape=[jax.ShapeDtypeStruct(shape, kind) for shape, kind in outs],
        scratch_shapes=list(scratch),
        compiler_params=pltpu.CompilerParams(vmem_limit_bytes=limit),
        cost_estimate=pl.CostEstimate(flops=flops, bytes_accessed=moved, transcendentals=0),
        **extra,
    )


def exchange(value, axis):
    rows, cols = value.shape
    pieces = value.reshape(16, rows // 16, cols)
    return lax.all_to_all(pieces, axis, split_axis=0, concat_axis=0, tiled=True).reshape(rows, cols)


def shift(value, y, zc):
    pairs = []
    for index in range(16):
        z, there, core = (index // 8 + zc // 2) % 2, (index // 2 + y) % 4, (index + zc) % 2
        pairs.append((index, z * 8 + there * 2 + core))
    return lax.ppermute(value, "ch", pairs)


def shards(signal, filter_raw, gate, d_out, w_first, w_second):
    rows, width = signal.shape
    outer, back, twiddle, inner = (jnp.asarray(t) for t in tables(lax.axis_size("seq"), rows))
    single, double = ((width, rows), BF16), ((2 * width, rows), BF16)
    slab = ((rows, width), BF16)
    pair = call(
        pair_kernel,
        [double],
        [pltpu.VMEM((2, rows, width), BF16), pltpu.SemaphoreType.DMA((2,))],
        held=(pl.ANY, 2),
        limit=60 << 20,
    )(signal, filter_raw)[0]
    pair = exchange(pair, "seq")
    quarter = ((width // 4, rows), BF16)
    near, *others = call(back_kernel, [quarter] * 4)(d_out, w_second)
    others = [shift(value, 0, zc) for zc, value in zip((1, 2, 3), others)]
    near, *others = call(repack_kernel, [quarter] * 4)(near, *others)
    others = [shift(value, y, 0) for y, value in zip((1, 2, 3), others)]
    square = ((128, 128), BF16)
    gate, blocks, own = call(prepare_kernel, [((width, rows), F32), square, square])(gate, w_first)
    conv, spectra = call(
        conv_kernel,
        [((4 * width, 128), F32), ((2, 512, 256), F32)],
        [pltpu.VMEM((2 * width * 4, 128), F32)],
        flops=1 << 30,
    )(pair, outer, back, twiddle, inner)
    pair, returned = call(gate_kernel, [double, single])(near, *others, own, gate, conv)
    pair = exchange(pair, "seq")
    mix = call(mix_kernel, [single])(pair, gate, blocks)[0]
    received = exchange(mix, "ch")
    grads = call(
        adjoint_kernel,
        [double],
        [pltpu.VMEM((2 * width * 4, 128), F32), pltpu.VMEM((2 * width * 4, 128), F32)],
        flops=1 << 30,
    )(pair, spectra, outer, back, twiddle, inner)[0]
    grad_gate, partial = call(first_kernel, [slab, ((2, width, 64), F32)])(
        pair, gate, returned, own
    )
    sums = call(second_kernel, [((2 * width, rows + 128), BF16)])(received, d_out, partial, grads)[0]
    sums = exchange(sums, "seq")
    grad_signal, grad_filter, grad_first, grad_second = call(
        exit_kernel, [slab, slab, ((2, 4, 64), F32), ((4, 2, 32), F32)]
    )(sums)
    return (grad_signal, grad_filter, grad_gate, grad_first, grad_second)


def solution(mesh):
    in_specs = (
        P("seq", "ch"),
        P("seq", "ch"),
        P("seq", "ch"),
        P("seq", "ch"),
        P("ch", None, None),
        P("ch", None, None),
    )
    out_specs = (
        P("seq", "ch"),
        P("seq", "ch"),
        P("seq", "ch"),
        P("ch", "seq", None),
        P("ch", "seq", None),
    )
    return jax.shard_map(shards, mesh=mesh, in_specs=in_specs, out_specs=out_specs, check_vma=False)
```

```python
import math

import jax
import jax.numpy as jnp
import numpy as np
from jax import lax
from jax.experimental import pallas as pl
from jax.experimental.pallas import tpu as pltpu
from jax.sharding import PartitionSpec as P

F32 = jnp.float32
BF16 = jnp.bfloat16
NN = (((1,), (0,)), ((), ()))
NT = (((1,), (1,)), ((), ()))
TN = (((0,), (0,)), ((), ()))


def dot(a, b, form=NN):
    return lax.dot_general(a, b, form, preferred_element_type=F32)


def halves(table):
    high = table.astype(BF16)
    return high, (table - high.astype(np.float32)).astype(BF16)


def tables(devices, rows):
    lanes = 128
    length = 2 * devices * rows
    steps = devices * rows // lanes
    split = rows // lanes
    place = (np.arange(steps) % devices) * split + np.arange(steps) // devices
    turn = 2.0 * math.pi
    freq = np.arange(steps) + 0.5
    angle = turn * freq[:, None] * place[None, :] / (2 * steps)
    outer = np.concatenate([np.cos(angle), -np.sin(angle)], 0)
    scale = float(devices * rows) ** -0.5 * 2.0 / length
    back = scale * np.concatenate([np.cos(angle.T), -np.sin(angle.T)], 1)
    angle = turn * freq[:, None] * np.arange(lanes)[None, :] / length
    twiddle = np.concatenate([np.cos(angle), -np.sin(angle)], 1)
    angle = turn * (np.arange(lanes)[:, None] * np.arange(lanes)[None, :] % lanes) / lanes
    cosine, sine = np.cos(angle), np.sin(angle)
    inner = np.concatenate(
        [np.concatenate([cosine, -sine], 1), np.concatenate([sine, cosine], 1)], 0
    )
    outer_high, outer_low = halves(outer.astype(np.float32))
    back_high, back_low = halves(back.astype(np.float32))
    inner_high, inner_low = halves(inner.astype(np.float32))
    return (
        np.concatenate([outer_high, outer_low], 1),
        np.stack([back_high, back_low]),
        twiddle.astype(np.float32),
        np.stack([inner_high, inner_low]),
    )


def iotas(rows, cols):
    return (
        lax.broadcasted_iota(jnp.int32, (rows, cols), 0),
        lax.broadcasted_iota(jnp.int32, (rows, cols), 1),
    )


def ones_where(mask):
    return jnp.where(mask, 1.0, 0.0).astype(BF16)


def pair_order():
    row, col = iotas(256, 256)
    return ones_where((row // 16 == col % 128 // 8) & (row // 8 % 2 == col // 128) & (row % 8 == col % 8))


def unit():
    row, col = iotas(128, 128)
    return ones_where(row == col)


def pair_kernel(signal_ref, filter_ref, pair_ref):
    both = jnp.concatenate([signal_ref[...], filter_ref[...]], axis=1)
    pair_ref[...] = dot(pair_order(), both, NT).astype(BF16)


def place():
    index = lax.axis_index("ch")
    return index // 8, index // 2 % 4, index % 2


def partner(slot_y, slot_zc, step):
    z, y, core = place()
    z = (z + slot_zc // 2) % 2
    core = (core + slot_zc) % 2
    y = (y + 4 + step * slot_y) % 4
    return z * 8 + y * 2 + core


def back_kernel(d_out_hbm, w_second_hbm, *refs):
    outs, (d_out_ref, w_second_ref, sems) = refs[:4], refs[4:]
    copies = [
        pltpu.make_async_copy(w_second_hbm, w_second_ref, sems.at[0]),
        pltpu.make_async_copy(d_out_hbm, d_out_ref, sems.at[1]),
    ]
    for copy in copies:
        copy.start()
    copies[0].wait()
    flat = w_second_ref[...].reshape(128, 32)
    row, col = iotas(32, 128)
    spread = dot(flat, ones_where(row == col % 32))
    row, col = iotas(128, 128)
    spread = jnp.where(row // 32 == col // 32, spread, 0.0).astype(BF16)
    block = 2 * partner(row // 8 % 4, row // 32, 1) + row // 4 % 2
    order = ones_where((block == col % 32) & (row % 4 == col // 32))
    weights = dot(order, spread).astype(BF16)
    copies[1].wait()
    result = dot(weights, d_out_ref[...], NT).astype(BF16)
    for zc, ref in enumerate(outs):
        ref[...] = result[32 * zc : 32 * zc + 32, :]


def repack_kernel(*refs):
    values = [ref[...].astype(F32) for ref in refs[:4]]
    for y, ref in enumerate(refs[4:]):
        ref[...] = jnp.concatenate([v[8 * y : 8 * y + 8, :] for v in values], axis=0).astype(BF16)


def source(col):
    return partner(col // 32, col // 8 % 4, -1)


def prepare_kernel(gate_ref, w_first_ref, gate_out_ref, blocks_ref, own_ref):
    flat = w_first_ref[...].reshape(128, 64)
    row, col = iotas(64, 128)
    keep_row, keep_col = iotas(128, 128)
    keep = keep_row // 64 == keep_col // 4 % 2
    for ref, group in ((blocks_ref, col // 8), (own_ref, source(col))):
        spread = dot(flat, ones_where(row == group * 4 + col % 4))
        ref[...] = jnp.where(keep, spread, 0.0).astype(BF16)
    gate_out_ref[...] = dot(unit(), gate_ref[...], NT)


def slab(slot_x, slot_z, step):
    index = lax.axis_index("seq")
    return (index // 4 + 4 + step * slot_x) % 4 * 4 + (index % 4 + 4 + step * slot_z) % 4


def gate_kernel(*refs):
    pieces, (own_ref, gate_ref), outs, returned_ref = refs[:4], refs[4:6], refs[6:10], refs[10]
    returned = jnp.concatenate([ref[...] for ref in pieces], axis=0)
    returned_ref[...] = returned
    incoming = (dot(own_ref[...], returned) * gate_ref[...]).astype(BF16)
    row, col = iotas(128, 128)
    order = ones_where(slab(row // 32, row // 8 % 4, 1) * 8 + row % 8 == col)
    result = dot(order, incoming).astype(BF16)
    for x, ref in enumerate(outs):
        ref[...] = result[32 * x : 32 * x + 32, :]


def split(value):
    high = value.astype(BF16)
    return high, (value - high.astype(F32)).astype(BF16)


def by_channel(wide_ref, first, stride):
    columns = [wide_ref[pl.ds(first + c, 64, stride=stride), :] for c in range(8)]
    return jnp.concatenate(columns, axis=1).astype(BF16)


def by_slab(wide_ref, value, first, stride):
    for c in range(8):
        wide_ref[pl.ds(first + c, 64, stride=stride), :] = value[:, 128 * c : 128 * c + 128]


def unroll(wide_ref, value):
    rows = value.shape[0]
    for th in range(4):
        wide_ref[rows * th : rows * th + rows, :] = value[:, 128 * th : 128 * th + 128].astype(F32)


def enroll(wide_ref):
    rows = wide_ref.shape[0] // 4
    pieces = [wide_ref[rows * th : rows * th + rows, :].astype(BF16) for th in range(4)]
    return jnp.concatenate(pieces, axis=1)


def transform(values, outer, twiddle_ref, inner_ref):
    stage = dot(outer, jnp.concatenate([values, values], axis=0))
    cosine, sine = twiddle_ref[:, 0:128], twiddle_ref[:, 128:256]
    rows = []
    for c in range(8):
        real = stage[0:64, 128 * c : 128 * c + 128]
        imag = stage[64:128, 128 * c : 128 * c + 128]
        rows.append(
            jnp.concatenate([real * cosine - imag * sine, real * sine + imag * cosine], axis=1)
        )
    high, low = split(jnp.concatenate(rows, axis=0))
    return dot(high, inner_ref[0]) + dot(low, inner_ref[0]) + dot(high, inner_ref[1])


def restore(real, imag, back_ref, twiddle_ref, inner_ref):
    high, low = split(jnp.concatenate([real, imag], axis=1))
    stage = dot(high, inner_ref[0], NT) + dot(low, inner_ref[0], NT) + dot(high, inner_ref[1], NT)
    cosine, sine = twiddle_ref[:, 0:128], twiddle_ref[:, 128:256]
    columns = []
    for c in range(8):
        real = stage[64 * c : 64 * c + 64, 0:128]
        imag = stage[64 * c : 64 * c + 64, 128:256]
        columns.append(
            jnp.concatenate([real * cosine + imag * sine, imag * cosine - real * sine], axis=0)
        )
    high, low = split(jnp.concatenate(columns, axis=1))
    return dot(back_ref[0], high) + dot(back_ref[0], low) + dot(back_ref[1], high)


def conv_kernel(
    pair_ref, outer_ref, back_ref, twiddle_ref, inner_ref, conv_ref, spectra_ref, wide_ref, out_ref
):
    unroll(wide_ref, pair_ref[...])
    signal = transform(by_channel(wide_ref, 0, 16), outer_ref[...], twiddle_ref, inner_ref)
    kernel = transform(by_channel(wide_ref, 8, 16), outer_ref[...], twiddle_ref, inner_ref)
    spectra_ref[0] = signal
    spectra_ref[1] = kernel
    sr, si = signal[:, 0:128], signal[:, 128:256]
    kr, ki = kernel[:, 0:128], kernel[:, 128:256]
    result = restore(sr * kr - si * ki, sr * ki + si * kr, back_ref, twiddle_ref, inner_ref)
    by_slab(out_ref, result, 0, 8)
    conv_ref[...] = enroll(out_ref)


def adjoint_kernel(*refs):
    pieces, (spectra_ref, outer_ref, back_ref, twiddle_ref, inner_ref) = refs[:4], refs[4:9]
    grads_ref, wide_ref, out_ref = refs[9:]
    unroll(wide_ref, jnp.concatenate([ref[...] for ref in pieces], axis=0))
    row, col = iotas(128, 128)
    order = ones_where(row == col // 16 * 16 + slab(col % 4, col // 4 % 4, -1))
    outer = dot(outer_ref[...], order).astype(BF16)
    spectrum = transform(by_channel(wide_ref, 0, 8), outer, twiddle_ref, inner_ref)
    gr, gi = spectrum[:, 0:128], spectrum[:, 128:256]
    for field in range(2):
        real, imag = spectra_ref[1 - field, :, 0:128], spectra_ref[1 - field, :, 128:256]
        result = restore(
            gr * real + gi * imag, gi * real - gr * imag, back_ref, twiddle_ref, inner_ref
        )
        by_slab(out_ref, result, 8 * field, 16)
    grads_ref[...] = enroll(out_ref)


def mix_kernel(conv_ref, gate_ref, blocks_ref, mix_ref):
    product = (conv_ref[...].astype(F32) * gate_ref[...]).astype(BF16)
    mix_ref[...] = dot(blocks_ref[...], product, TN).astype(BF16)


def first_kernel(conv_ref, gate_ref, returned_ref, own_ref, grad_gate_ref, partial_ref):
    conv = conv_ref[...].astype(F32)
    product = (conv * gate_ref[...]).astype(BF16)
    returned = returned_ref[...]
    grad_gate = (dot(own_ref[...], returned) * conv).astype(BF16)
    grad_gate_ref[...] = dot(grad_gate, unit(), TN).astype(BF16)
    row, col = iotas(128, 128)
    grad = jnp.where(row // 64 == col // 4 % 2, dot(product, returned, NT), 0.0)
    order = ones_where(
        (row // 8 == col % 64 // 4) & (row // 4 % 2 == col // 64) & (row % 4 == col % 4)
    )
    row, col = iotas(128, 64)
    fold = ones_where(source(row) * 4 + row % 4 == col)
    for part, piece in enumerate(split(grad)):
        partial_ref[part] = dot(order, dot(piece, fold).astype(BF16))


def second_kernel(received_ref, d_out_ref, partial_ref, grads_ref, sums_ref):
    row, col = iotas(128, 128)
    grad = jnp.where(row % 4 == col // 32, dot(received_ref[...], d_out_ref[...]), 0.0)
    row, col = iotas(128, 64)
    fold = ones_where(row % 32 == col)
    high, low = [
        jnp.concatenate([partial_ref[part], dot(piece, fold)], axis=1)
        for part, piece in enumerate(split(grad))
    ]
    rows = []
    for p in range(16):
        rows.append(high[8 * p : 8 * p + 8, :])
        rows.append(low[8 * p : 8 * p + 8, :])
    sums_ref[:, 0:512] = grads_ref[...]
    sums_ref[:, 512:640] = jnp.concatenate(rows, axis=0).astype(BF16)


def exit_kernel(sums_ref, signal_ref, filter_ref, first_ref, second_ref):
    both = dot(sums_ref[:, 0:512], pair_order(), TN).astype(BF16)
    signal_ref[...] = both[:, 0:128]
    filter_ref[...] = both[:, 128:256]
    wide = sums_ref[:, 512:640].astype(F32)
    total = wide[0:16, :]
    for p in range(1, 16):
        total = total + wide[16 * p : 16 * p + 16, :]
    total = total[0:8, :] + total[8:16, :]
    for i in range(2):
        first_ref[i] = total[4 * i : 4 * i + 4, 0:64]
        for k in range(4):
            second_ref[k, i : i + 1, :] = total[4 * i + k : 4 * i + k + 1, 64:96]


def call(body, outs, scratch=(), flops=1 << 26, moved=1 << 19, held=None, limit=32 << 20):
    extra = {}
    if held is not None:
        extra["in_specs"] = [pl.BlockSpec(memory_space=held[0])] * held[1]
    return pl.pallas_call(
        body,
        out_shape=[jax.ShapeDtypeStruct(shape, kind) for shape, kind in outs],
        scratch_shapes=list(scratch),
        compiler_params=pltpu.CompilerParams(vmem_limit_bytes=limit),
        cost_estimate=pl.CostEstimate(flops=flops, bytes_accessed=moved, transcendentals=0),
        **extra,
    )


def exchange(value, axis):
    rows, cols = value.shape
    pieces = value.reshape(16, rows // 16, cols)
    return lax.all_to_all(pieces, axis, split_axis=0, concat_axis=0, tiled=True).reshape(rows, cols)


def shift(value, y, zc):
    pairs = []
    for index in range(16):
        z, there, core = (index // 8 + zc // 2) % 2, (index // 2 + y) % 4, (index + zc) % 2
        pairs.append((index, z * 8 + there * 2 + core))
    return lax.ppermute(value, "ch", pairs)


def slide(value, x, z):
    pairs = [(index, (index // 4 + x) % 4 * 4 + (index + z) % 4) for index in range(16)]
    return lax.ppermute(value, "seq", pairs)


def after(value, *done):
    return lax.optimization_barrier((value, *done))[0]


def shards(signal, filter_raw, gate, d_out, w_first, w_second):
    rows, width = signal.shape
    outer, back, twiddle, inner = (jnp.asarray(t) for t in tables(lax.axis_size("seq"), rows))
    single, double = ((width, rows), BF16), ((2 * width, rows), BF16)
    slabs = ((rows, width), BF16)
    quarter, square = ((width // 4, rows), BF16), ((128, 128), BF16)
    near, *others = call(
        back_kernel,
        [quarter] * 4,
        [
            pltpu.VMEM(d_out.shape, BF16),
            pltpu.VMEM(w_second.shape, BF16),
            pltpu.SemaphoreType.DMA((2,)),
        ],
        held=(pl.ANY, 2),
        limit=60 << 20,
    )(d_out, w_second)
    others = [shift(value, 0, zc) for zc, value in zip((1, 2, 3), others)]
    pair = call(pair_kernel, [double])(signal, filter_raw)[0]
    pair = exchange(pair, "seq")
    near, *others = call(repack_kernel, [quarter] * 4, flops=1 << 35)(near, *others)
    pair = after(pair, near, *others)
    others = [shift(value, y, 0) for y, value in zip((1, 2, 3), others)]
    gate, blocks, own = call(prepare_kernel, [((width, rows), F32), square, square])(gate, w_first)
    conv, spectra = call(
        conv_kernel,
        [single, ((2, 512, 256), F32)],
        [pltpu.VMEM((2 * width * 4, 128), F32), pltpu.VMEM((width * 4, 128), F32)],
        flops=1 << 30,
    )(pair, outer, back, twiddle, inner)
    conv = exchange(after(conv, *others), "seq")
    near, *others, returned = call(gate_kernel, [quarter] * 4 + [single])(near, *others, own, gate)
    conv = after(conv, near, *others)
    others = [slide(value, x, 0) for x, value in zip((1, 2, 3), others)]
    mix = call(mix_kernel, [single])(conv, gate, blocks)[0]
    near, *others = call(repack_kernel, [quarter] * 4)(near, *others)
    received = exchange(after(mix, near, *others), "ch")
    others = [slide(value, 0, z) for z, value in zip((1, 2, 3), others)]
    grads = call(
        adjoint_kernel,
        [double],
        [pltpu.VMEM((width * 4, 128), F32), pltpu.VMEM((2 * width * 4, 128), F32)],
        flops=1 << 30,
    )(near, *others, spectra, outer, back, twiddle, inner)[0]
    grad_gate, partial = call(first_kernel, [slabs, ((2, width, 64), F32)])(
        conv, gate, returned, own
    )
    sums = call(second_kernel, [((2 * width, rows + 128), BF16)])(received, d_out, partial, grads)[0]
    sums = exchange(sums, "seq")
    grad_signal, grad_filter, grad_first, grad_second = call(
        exit_kernel, [slabs, slabs, ((2, 4, 64), F32), ((4, 2, 32), F32)]
    )(sums)
    return (grad_signal, grad_filter, grad_gate, grad_first, grad_second)


def solution(mesh):
    in_specs = (
        P("seq", "ch"),
        P("seq", "ch"),
        P("seq", "ch"),
        P("seq", "ch"),
        P("ch", None, None),
        P("ch", None, None),
    )
    out_specs = (
        P("seq", "ch"),
        P("seq", "ch"),
        P("seq", "ch"),
        P("ch", "seq", None),
        P("ch", "seq", None),
    )
    return jax.shard_map(shards, mesh=mesh, in_specs=in_specs, out_specs=out_specs, check_vma=False)
```

```python
import math

import jax
import jax.numpy as jnp
import numpy as np
from jax import lax
from jax.experimental import pallas as pl
from jax.experimental.pallas import tpu as pltpu
from jax.sharding import PartitionSpec as P

F32 = jnp.float32
BF16 = jnp.bfloat16
NN = (((1,), (0,)), ((), ()))
NT = (((1,), (1,)), ((), ()))
TN = (((0,), (0,)), ((), ()))


def dot(a, b, form=NN):
    return lax.dot_general(a, b, form, preferred_element_type=F32)


def halves(table):
    high = table.astype(BF16)
    return high, (table - high.astype(np.float32)).astype(BF16)


def tables(devices, rows):
    lanes = 128
    length = 2 * devices * rows
    steps = devices * rows // lanes
    split = rows // lanes
    place = (np.arange(steps) % devices) * split + np.arange(steps) // devices
    turn = 2.0 * math.pi
    freq = np.arange(steps) + 0.5
    angle = turn * freq[:, None] * place[None, :] / (2 * steps)
    outer = np.concatenate([np.cos(angle), -np.sin(angle)], 0)
    scale = float(devices * rows) ** -0.5 * 2.0 / length
    back = scale * np.concatenate([np.cos(angle.T), -np.sin(angle.T)], 1)
    angle = turn * freq[:, None] * np.arange(lanes)[None, :] / length
    twiddle = np.concatenate([np.cos(angle), -np.sin(angle)], 1)
    angle = turn * (np.arange(lanes)[:, None] * np.arange(lanes)[None, :] % lanes) / lanes
    cosine, sine = np.cos(angle), np.sin(angle)
    inner = np.concatenate(
        [np.concatenate([cosine, -sine], 1), np.concatenate([sine, cosine], 1)], 0
    )
    outer_high, outer_low = halves(outer.astype(np.float32))
    back_high, back_low = halves(back.astype(np.float32))
    inner_high, inner_low = halves(inner.astype(np.float32))
    return (
        np.concatenate([outer_high, outer_low], 1),
        np.stack([back_high, back_low]),
        twiddle.astype(np.float32),
        np.stack([inner_high, inner_low]),
    )


def iotas(rows, cols):
    return (
        lax.broadcasted_iota(jnp.int32, (rows, cols), 0),
        lax.broadcasted_iota(jnp.int32, (rows, cols), 1),
    )


def ones_where(mask):
    return jnp.where(mask, 1.0, 0.0).astype(BF16)


def pair_order():
    row, col = iotas(256, 256)
    return ones_where((row // 16 == col % 128 // 8) & (row // 8 % 2 == col // 128) & (row % 8 == col % 8))


def unit():
    row, col = iotas(128, 128)
    return ones_where(row == col)


def pair_kernel(signal_ref, filter_ref, pair_ref):
    both = jnp.concatenate([signal_ref[...], filter_ref[...]], axis=1)
    pair_ref[...] = dot(pair_order(), both, NT).astype(BF16)


def place():
    index = lax.axis_index("ch")
    return index // 8, index // 2 % 4, index % 2


def partner(slot_y, slot_zc, step):
    z, y, core = place()
    z = (z + slot_zc // 2) % 2
    core = (core + slot_zc) % 2
    y = (y + 4 + step * slot_y) % 4
    return z * 8 + y * 2 + core


def back_kernel(d_out_hbm, w_second_hbm, *refs):
    outs, (d_out_ref, w_second_ref, sems) = refs[:3], refs[3:]
    copies = [
        pltpu.make_async_copy(w_second_hbm, w_second_ref, sems.at[0]),
        pltpu.make_async_copy(d_out_hbm, d_out_ref, sems.at[1]),
    ]
    for copy in copies:
        copy.start()
    copies[0].wait()
    flat = w_second_ref[...].reshape(128, 32)
    row, col = iotas(32, 128)
    spread = dot(flat, ones_where(row == col % 32))
    row, col = iotas(128, 128)
    spread = jnp.where(row // 32 == col // 32, spread, 0.0).astype(BF16)
    block = 2 * partner(row // 8 % 4, row // 32, 1) + row // 4 % 2
    order = ones_where((block == col % 32) & (row % 4 == col // 32))
    weights = dot(order, spread).astype(BF16)
    copies[1].wait()
    result = dot(weights, d_out_ref[...], NT).astype(BF16)
    for ref, start in zip(outs, (0, 32, 64)):
        ref[...] = result[start : start + ref.shape[0], :]


def core_kernel(core_ref, far_ref, message_ref):
    message_ref[0:32, :] = core_ref[...]
    message_ref[32:64, :] = far_ref[32:64, :]


def repack_kernel(near_ref, core_ref, far_ref, *outs):
    near, core, far = (ref[...].astype(F32) for ref in (near_ref, core_ref, far_ref))
    values = (near, core[0:32, :], far[0:32, :], core[32:64, :])
    for y, ref in enumerate(outs):
        ref[...] = jnp.concatenate([v[8 * y : 8 * y + 8, :] for v in values], axis=0).astype(BF16)


def source(col):
    return partner(col // 32, col // 8 % 4, -1)


def prepare_kernel(gate_ref, w_first_ref, gate_out_ref, blocks_ref, own_ref):
    flat = w_first_ref[...].reshape(128, 64)
    row, col = iotas(64, 128)
    keep_row, keep_col = iotas(128, 128)
    keep = keep_row // 64 == keep_col // 4 % 2
    for ref, group in ((blocks_ref, col // 8), (own_ref, source(col))):
        spread = dot(flat, ones_where(row == group * 4 + col % 4))
        ref[...] = jnp.where(keep, spread, 0.0).astype(BF16)
    gate_out_ref[...] = dot(unit(), gate_ref[...], NT)


def gate_kernel(near_ref, first_ref, second_ref, third_ref, own_ref, gate_ref, conv_ref, pair_ref, returned_ref):
    pieces = [ref[...] for ref in (near_ref, first_ref, second_ref, third_ref)]
    returned = jnp.concatenate(pieces, axis=0)
    returned_ref[...] = returned
    incoming = dot(own_ref[...], returned) * gate_ref[...]
    rows = []
    for p in range(16):
        pieces = [conv_ref[128 * th + 8 * p : 128 * th + 8 * p + 8, :] for th in range(4)]
        rows.append(jnp.concatenate(pieces, axis=1))
        rows.append(incoming[8 * p : 8 * p + 8, :])
    pair_ref[...] = jnp.concatenate(rows, axis=0).astype(BF16)


def split(value):
    high = value.astype(BF16)
    return high, (value - high.astype(F32)).astype(BF16)


def by_channel(wide_ref, first, stride):
    columns = [wide_ref[pl.ds(first + c, 64, stride=stride), :] for c in range(8)]
    return jnp.concatenate(columns, axis=1).astype(BF16)


def by_slab(wide_ref, value, first, stride):
    for c in range(8):
        wide_ref[pl.ds(first + c, 64, stride=stride), :] = value[:, 128 * c : 128 * c + 128]


def unroll(wide_ref, value):
    rows = value.shape[0]
    for th in range(4):
        wide_ref[rows * th : rows * th + rows, :] = value[:, 128 * th : 128 * th + 128].astype(F32)


def enroll(wide_ref):
    rows = wide_ref.shape[0] // 4
    pieces = [wide_ref[rows * th : rows * th + rows, :].astype(BF16) for th in range(4)]
    return jnp.concatenate(pieces, axis=1)


def transform(values, outer_ref, twiddle_ref, inner_ref):
    stage = dot(outer_ref[...], jnp.concatenate([values, values], axis=0))
    cosine, sine = twiddle_ref[:, 0:128], twiddle_ref[:, 128:256]
    rows = []
    for c in range(8):
        real = stage[0:64, 128 * c : 128 * c + 128]
        imag = stage[64:128, 128 * c : 128 * c + 128]
        rows.append(
            jnp.concatenate([real * cosine - imag * sine, real * sine + imag * cosine], axis=1)
        )
    high, low = split(jnp.concatenate(rows, axis=0))
    return dot(high, inner_ref[0]) + dot(low, inner_ref[0]) + dot(high, inner_ref[1])


def restore(real, imag, back_ref, twiddle_ref, inner_ref):
    high, low = split(jnp.concatenate([real, imag], axis=1))
    stage = dot(high, inner_ref[0], NT) + dot(low, inner_ref[0], NT) + dot(high, inner_ref[1], NT)
    cosine, sine = twiddle_ref[:, 0:128], twiddle_ref[:, 128:256]
    columns = []
    for c in range(8):
        real = stage[64 * c : 64 * c + 64, 0:128]
        imag = stage[64 * c : 64 * c + 64, 128:256]
        columns.append(
            jnp.concatenate([real * cosine + imag * sine, imag * cosine - real * sine], axis=0)
        )
    high, low = split(jnp.concatenate(columns, axis=1))
    return dot(back_ref[0], high) + dot(back_ref[0], low) + dot(back_ref[1], high)


def conv_kernel(pair_ref, outer_ref, back_ref, twiddle_ref, inner_ref, conv_ref, spectra_ref, wide_ref):
    unroll(wide_ref, pair_ref[...])
    signal = transform(by_channel(wide_ref, 0, 16), outer_ref, twiddle_ref, inner_ref)
    kernel = transform(by_channel(wide_ref, 8, 16), outer_ref, twiddle_ref, inner_ref)
    spectra_ref[0] = signal
    spectra_ref[1] = kernel
    sr, si = signal[:, 0:128], signal[:, 128:256]
    kr, ki = kernel[:, 0:128], kernel[:, 128:256]
    result = restore(sr * kr - si * ki, sr * ki + si * kr, back_ref, twiddle_ref, inner_ref)
    by_slab(conv_ref, result, 0, 8)


def adjoint_kernel(
    pair_ref, spectra_ref, outer_ref, back_ref, twiddle_ref, inner_ref, grads_ref, wide_ref, out_ref
):
    unroll(wide_ref, pair_ref[...])
    spectrum = transform(by_channel(wide_ref, 8, 16), outer_ref, twiddle_ref, inner_ref)
    gr, gi = spectrum[:, 0:128], spectrum[:, 128:256]
    for field in range(2):
        real, imag = spectra_ref[1 - field, :, 0:128], spectra_ref[1 - field, :, 128:256]
        result = restore(
            gr * real + gi * imag, gi * real - gr * imag, back_ref, twiddle_ref, inner_ref
        )
        by_slab(out_ref, result, 8 * field, 16)
    grads_ref[...] = enroll(out_ref)


def conv_rows(pair_ref):
    wide = pair_ref[...].astype(F32)
    return jnp.concatenate([wide[16 * p : 16 * p + 8, :] for p in range(16)], axis=0)


def mix_kernel(pair_ref, gate_ref, blocks_ref, mix_ref):
    product = (conv_rows(pair_ref) * gate_ref[...]).astype(BF16)
    mix_ref[...] = dot(blocks_ref[...], product, TN).astype(BF16)


def first_kernel(pair_ref, gate_ref, returned_ref, own_ref, grad_gate_ref, partial_ref):
    conv = conv_rows(pair_ref)
    product = (conv * gate_ref[...]).astype(BF16)
    returned = returned_ref[...]
    grad_gate = (dot(own_ref[...], returned) * conv).astype(BF16)
    grad_gate_ref[...] = dot(grad_gate, unit(), TN).astype(BF16)
    row, col = iotas(128, 128)
    grad = jnp.where(row // 64 == col // 4 % 2, dot(product, returned, NT), 0.0)
    order = ones_where(
        (row // 8 == col % 64 // 4) & (row // 4 % 2 == col // 64) & (row % 4 == col % 4)
    )
    row, col = iotas(128, 64)
    fold = ones_where(source(row) * 4 + row % 4 == col)
    for part, piece in enumerate(split(grad)):
        partial_ref[part] = dot(order, dot(piece, fold).astype(BF16))


def second_kernel(received_ref, d_out_ref, partial_ref, grads_ref, sums_ref):
    row, col = iotas(128, 128)
    grad = jnp.where(row % 4 == col // 32, dot(received_ref[...], d_out_ref[...]), 0.0)
    row, col = iotas(128, 64)
    fold = ones_where(row % 32 == col)
    high, low = [
        jnp.concatenate([partial_ref[part], dot(piece, fold)], axis=1)
        for part, piece in enumerate(split(grad))
    ]
    rows = []
    for p in range(16):
        rows.append(high[8 * p : 8 * p + 8, :])
        rows.append(low[8 * p : 8 * p + 8, :])
    sums_ref[:, 0:512] = grads_ref[...]
    sums_ref[:, 512:640] = jnp.concatenate(rows, axis=0).astype(BF16)


def exit_kernel(sums_ref, signal_ref, filter_ref, first_ref, second_ref):
    both = dot(sums_ref[:, 0:512], pair_order(), TN).astype(BF16)
    signal_ref[...] = both[:, 0:128]
    filter_ref[...] = both[:, 128:256]
    wide = sums_ref[:, 512:640].astype(F32)
    total = wide[0:16, :]
    for p in range(1, 16):
        total = total + wide[16 * p : 16 * p + 16, :]
    total = total[0:8, :] + total[8:16, :]
    for i in range(2):
        first_ref[i] = total[4 * i : 4 * i + 4, 0:64]
        for k in range(4):
            second_ref[k, i : i + 1, :] = total[4 * i + k : 4 * i + k + 1, 64:96]


def call(body, outs, scratch=(), flops=1 << 26, moved=1 << 19, held=None, limit=32 << 20):
    extra = {}
    if held is not None:
        extra["in_specs"] = [pl.BlockSpec(memory_space=held[0])] * held[1]
    return pl.pallas_call(
        body,
        out_shape=[jax.ShapeDtypeStruct(shape, kind) for shape, kind in outs],
        scratch_shapes=list(scratch),
        compiler_params=pltpu.CompilerParams(vmem_limit_bytes=limit),
        cost_estimate=pl.CostEstimate(flops=flops, bytes_accessed=moved, transcendentals=0),
        **extra,
    )


def exchange(value, axis):
    rows, cols = value.shape
    pieces = value.reshape(16, rows // 16, cols)
    return lax.all_to_all(pieces, axis, split_axis=0, concat_axis=0, tiled=True).reshape(rows, cols)


def shift(value, y, zc):
    pairs = []
    for index in range(16):
        z, there, core = (index // 8 + zc // 2) % 2, (index // 2 + y) % 4, (index + zc) % 2
        pairs.append((index, z * 8 + there * 2 + core))
    return lax.ppermute(value, "ch", pairs)


def shards(signal, filter_raw, gate, d_out, w_first, w_second):
    rows, width = signal.shape
    outer, back, twiddle, inner = (jnp.asarray(t) for t in tables(lax.axis_size("seq"), rows))
    single, double = ((width, rows), BF16), ((2 * width, rows), BF16)
    slab = ((rows, width), BF16)
    quarter, half = ((width // 4, rows), BF16), ((width // 2, rows), BF16)
    near, core, far = call(
        back_kernel,
        [quarter, quarter, half],
        [
            pltpu.VMEM(d_out.shape, BF16),
            pltpu.VMEM(w_second.shape, BF16),
            pltpu.SemaphoreType.DMA((2,)),
        ],
        held=(pl.ANY, 2),
        limit=60 << 20,
    )(d_out, w_second)
    far = shift(far, 0, 2)
    pair = call(pair_kernel, [double])(signal, filter_raw)[0]
    pair = exchange(pair, "seq")
    core = shift(call(core_kernel, [half], flops=1 << 35)(core, far)[0], 0, 1)
    near, *others = call(repack_kernel, [quarter] * 4)(near, core, far)
    pair = lax.optimization_barrier((pair, near))[0]
    others = [shift(value, y, 0) for y, value in zip((1, 2, 3), others)]
    square = ((128, 128), BF16)
    gate, blocks, own = call(prepare_kernel, [((width, rows), F32), square, square])(gate, w_first)
    conv, spectra = call(
        conv_kernel,
        [((4 * width, 128), F32), ((2, 512, 256), F32)],
        [pltpu.VMEM((2 * width * 4, 128), F32)],
        flops=1 << 30,
    )(pair, outer, back, twiddle, inner)
    pair, returned = call(gate_kernel, [double, single])(near, *others, own, gate, conv)
    pair = exchange(pair, "seq")
    mix = call(mix_kernel, [single])(pair, gate, blocks)[0]
    received = exchange(mix, "ch")
    grads = call(
        adjoint_kernel,
        [double],
        [pltpu.VMEM((2 * width * 4, 128), F32), pltpu.VMEM((2 * width * 4, 128), F32)],
        flops=1 << 30,
    )(pair, spectra, outer, back, twiddle, inner)[0]
    grad_gate, partial = call(first_kernel, [slab, ((2, width, 64), F32)])(
        pair, gate, returned, own
    )
    sums = call(second_kernel, [((2 * width, rows + 128), BF16)])(received, d_out, partial, grads)[0]
    sums = exchange(sums, "seq")
    grad_signal, grad_filter, grad_first, grad_second = call(
        exit_kernel, [slab, slab, ((2, 4, 64), F32), ((4, 2, 32), F32)]
    )(sums)
    return (grad_signal, grad_filter, grad_gate, grad_first, grad_second)


def solution(mesh):
    in_specs = (
        P("seq", "ch"),
        P("seq", "ch"),
        P("seq", "ch"),
        P("seq", "ch"),
        P("ch", None, None),
        P("ch", None, None),
    )
    out_specs = (
        P("seq", "ch"),
        P("seq", "ch"),
        P("seq", "ch"),
        P("ch", "seq", None),
        P("ch", "seq", None),
    )
    return jax.shard_map(shards, mesh=mesh, in_specs=in_specs, out_specs=out_specs, check_vma=False)
```

```python
import math

import jax
import jax.numpy as jnp
import numpy as np
from jax import lax
from jax.experimental import pallas as pl
from jax.experimental.pallas import tpu as pltpu
from jax.sharding import PartitionSpec as P

F32 = jnp.float32
BF16 = jnp.bfloat16
NN = (((1,), (0,)), ((), ()))
NT = (((1,), (1,)), ((), ()))
TN = (((0,), (0,)), ((), ()))


def dot(a, b, form=NN):
    return lax.dot_general(a, b, form, preferred_element_type=F32)


def halves(table):
    high = table.astype(BF16)
    return high, (table - high.astype(np.float32)).astype(BF16)


def tables(devices, rows):
    lanes = 128
    length = 2 * devices * rows
    steps = devices * rows // lanes
    split = rows // lanes
    place = (np.arange(steps) % devices) * split + np.arange(steps) // devices
    turn = 2.0 * math.pi
    freq = np.arange(steps) + 0.5
    angle = turn * freq[:, None] * place[None, :] / (2 * steps)
    outer = np.concatenate([np.cos(angle), -np.sin(angle)], 0)
    scale = float(devices * rows) ** -0.5 * 2.0 / length
    back = scale * np.concatenate([np.cos(angle.T), -np.sin(angle.T)], 1)
    angle = turn * freq[:, None] * np.arange(lanes)[None, :] / length
    twiddle = np.concatenate([np.cos(angle), -np.sin(angle)], 1)
    angle = turn * (np.arange(lanes)[:, None] * np.arange(lanes)[None, :] % lanes) / lanes
    cosine, sine = np.cos(angle), np.sin(angle)
    inner = np.concatenate(
        [np.concatenate([cosine, -sine], 1), np.concatenate([sine, cosine], 1)], 0
    )
    outer_high, outer_low = halves(outer.astype(np.float32))
    back_high, back_low = halves(back.astype(np.float32))
    inner_high, inner_low = halves(inner.astype(np.float32))
    return (
        np.concatenate([outer_high, outer_low], 1),
        np.stack([back_high, back_low]),
        twiddle.astype(np.float32),
        np.stack([inner_high, inner_low]),
    )


def iotas(rows, cols):
    return (
        lax.broadcasted_iota(jnp.int32, (rows, cols), 0),
        lax.broadcasted_iota(jnp.int32, (rows, cols), 1),
    )


def ones_where(mask):
    return jnp.where(mask, 1.0, 0.0).astype(BF16)


def pair_order():
    row, col = iotas(256, 256)
    return ones_where((row // 16 == col % 128 // 8) & (row // 8 % 2 == col // 128) & (row % 8 == col % 8))


def unit():
    row, col = iotas(128, 128)
    return ones_where(row == col)


def place():
    index = lax.axis_index("ch")
    return index // 8, index // 2 % 4, index % 2


def partner(slot_y, slot_zc, step):
    z, y, core = place()
    z = (z + slot_zc // 2) % 2
    core = (core + slot_zc) % 2
    y = (y + 4 + step * slot_y) % 4
    return z * 8 + y * 2 + core


def entry_kernel(
    d_out_hbm,
    w_second_hbm,
    signal_hbm,
    filter_hbm,
    near_ref,
    core_ref,
    far_ref,
    pair_hbm,
    d_out_ref,
    w_second_ref,
    both_ref,
    pair_ref,
    sems,
):
    copies = [
        pltpu.make_async_copy(source, target, sems.at[index])
        for index, (source, target) in enumerate(
            (
                (signal_hbm, both_ref.at[0]),
                (filter_hbm, both_ref.at[1]),
                (w_second_hbm, w_second_ref),
                (d_out_hbm, d_out_ref),
            )
        )
    ]
    for copy in copies:
        copy.start()
    pairs = pair_order()
    row, col = iotas(32, 128)
    copies_of = ones_where(row == col % 32)
    row, col = iotas(128, 128)
    keep = row // 32 == col // 32
    block = 2 * partner(row // 8 % 4, row // 32, 1) + row // 4 % 2
    order = ones_where((block == col % 32) & (row % 4 == col // 32))
    copies[0].wait()
    copies[1].wait()
    both = jnp.concatenate([both_ref[0], both_ref[1]], axis=1)
    pair_ref[...] = dot(pairs, both, NT).astype(BF16)
    leave = pltpu.make_async_copy(pair_ref, pair_hbm, sems.at[4])
    leave.start()
    copies[2].wait()
    flat = w_second_ref[...].reshape(128, 32)
    spread = jnp.where(keep, dot(flat, copies_of), 0.0).astype(BF16)
    weights = dot(order, spread).astype(BF16)
    copies[3].wait()
    result = dot(weights, d_out_ref[...], NT).astype(BF16)
    for ref, start in zip((near_ref, core_ref, far_ref), (0, 32, 64)):
        ref[...] = result[start : start + ref.shape[0], :]
    leave.wait()


def core_kernel(core_ref, far_ref, message_ref):
    message_ref[0:32, :] = core_ref[...]
    message_ref[32:64, :] = far_ref[32:64, :]


def repack_kernel(near_ref, core_ref, far_ref, *outs):
    near, core, far = (ref[...].astype(F32) for ref in (near_ref, core_ref, far_ref))
    values = (near, core[0:32, :], far[0:32, :], core[32:64, :])
    for y, ref in enumerate(outs):
        ref[...] = jnp.concatenate([v[8 * y : 8 * y + 8, :] for v in values], axis=0).astype(BF16)


def source(col):
    return partner(col // 32, col // 8 % 4, -1)


def prepare_kernel(gate_ref, w_first_ref, gate_out_ref, blocks_ref, own_ref):
    flat = w_first_ref[...].reshape(128, 64)
    row, col = iotas(64, 128)
    keep_row, keep_col = iotas(128, 128)
    keep = keep_row // 64 == keep_col // 4 % 2
    for ref, group in ((blocks_ref, col // 8), (own_ref, source(col))):
        spread = dot(flat, ones_where(row == group * 4 + col % 4))
        ref[...] = jnp.where(keep, spread, 0.0).astype(BF16)
    gate_out_ref[...] = dot(unit(), gate_ref[...], NT)


def gate_kernel(near_ref, first_ref, second_ref, third_ref, own_ref, gate_ref, conv_ref, pair_ref, returned_ref):
    pieces = [ref[...] for ref in (near_ref, first_ref, second_ref, third_ref)]
    returned = jnp.concatenate(pieces, axis=0)
    returned_ref[...] = returned
    incoming = dot(own_ref[...], returned) * gate_ref[...]
    rows = []
    for p in range(16):
        pieces = [conv_ref[128 * th + 8 * p : 128 * th + 8 * p + 8, :] for th in range(4)]
        rows.append(jnp.concatenate(pieces, axis=1))
        rows.append(incoming[8 * p : 8 * p + 8, :])
    pair_ref[...] = jnp.concatenate(rows, axis=0).astype(BF16)


def split(value):
    high = value.astype(BF16)
    return high, (value - high.astype(F32)).astype(BF16)


def by_channel(wide_ref, first, stride):
    columns = [wide_ref[pl.ds(first + c, 64, stride=stride), :] for c in range(8)]
    return jnp.concatenate(columns, axis=1).astype(BF16)


def by_slab(wide_ref, value, first, stride):
    for c in range(8):
        wide_ref[pl.ds(first + c, 64, stride=stride), :] = value[:, 128 * c : 128 * c + 128]


def unroll(wide_ref, value):
    rows = value.shape[0]
    for th in range(4):
        wide_ref[rows * th : rows * th + rows, :] = value[:, 128 * th : 128 * th + 128].astype(F32)


def enroll(wide_ref):
    rows = wide_ref.shape[0] // 4
    pieces = [wide_ref[rows * th : rows * th + rows, :].astype(BF16) for th in range(4)]
    return jnp.concatenate(pieces, axis=1)


def transform(values, outer_ref, twiddle_ref, inner_ref):
    stage = dot(outer_ref[...], jnp.concatenate([values, values], axis=0))
    cosine, sine = twiddle_ref[:, 0:128], twiddle_ref[:, 128:256]
    rows = []
    for c in range(8):
        real = stage[0:64, 128 * c : 128 * c + 128]
        imag = stage[64:128, 128 * c : 128 * c + 128]
        rows.append(
            jnp.concatenate([real * cosine - imag * sine, real * sine + imag * cosine], axis=1)
        )
    high, low = split(jnp.concatenate(rows, axis=0))
    return dot(high, inner_ref[0]) + dot(low, inner_ref[0]) + dot(high, inner_ref[1])


def restore(real, imag, back_ref, twiddle_ref, inner_ref):
    high, low = split(jnp.concatenate([real, imag], axis=1))
    stage = dot(high, inner_ref[0], NT) + dot(low, inner_ref[0], NT) + dot(high, inner_ref[1], NT)
    cosine, sine = twiddle_ref[:, 0:128], twiddle_ref[:, 128:256]
    columns = []
    for c in range(8):
        real = stage[64 * c : 64 * c + 64, 0:128]
        imag = stage[64 * c : 64 * c + 64, 128:256]
        columns.append(
            jnp.concatenate([real * cosine + imag * sine, imag * cosine - real * sine], axis=0)
        )
    high, low = split(jnp.concatenate(columns, axis=1))
    return dot(back_ref[0], high) + dot(back_ref[0], low) + dot(back_ref[1], high)


def conv_kernel(pair_ref, outer_ref, back_ref, twiddle_ref, inner_ref, conv_ref, spectra_ref, wide_ref):
    unroll(wide_ref, pair_ref[...])
    signal = transform(by_channel(wide_ref, 0, 16), outer_ref, twiddle_ref, inner_ref)
    kernel = transform(by_channel(wide_ref, 8, 16), outer_ref, twiddle_ref, inner_ref)
    spectra_ref[0] = signal
    spectra_ref[1] = kernel
    sr, si = signal[:, 0:128], signal[:, 128:256]
    kr, ki = kernel[:, 0:128], kernel[:, 128:256]
    result = restore(sr * kr - si * ki, sr * ki + si * kr, back_ref, twiddle_ref, inner_ref)
    by_slab(conv_ref, result, 0, 8)


def adjoint_kernel(
    pair_ref, spectra_ref, outer_ref, back_ref, twiddle_ref, inner_ref, grads_ref, wide_ref, out_ref
):
    unroll(wide_ref, pair_ref[...])
    spectrum = transform(by_channel(wide_ref, 8, 16), outer_ref, twiddle_ref, inner_ref)
    gr, gi = spectrum[:, 0:128], spectrum[:, 128:256]
    for field in range(2):
        real, imag = spectra_ref[1 - field, :, 0:128], spectra_ref[1 - field, :, 128:256]
        result = restore(
            gr * real + gi * imag, gi * real - gr * imag, back_ref, twiddle_ref, inner_ref
        )
        by_slab(out_ref, result, 0, 8)
        grads_ref[:, 512 * field : 512 * field + 512] = enroll(out_ref)


def conv_rows(pair_ref):
    wide = pair_ref[...].astype(F32)
    return jnp.concatenate([wide[16 * p : 16 * p + 8, :] for p in range(16)], axis=0)


def mix_kernel(pair_ref, gate_ref, blocks_ref, mix_ref):
    product = (conv_rows(pair_ref) * gate_ref[...]).astype(BF16)
    mix_ref[...] = dot(blocks_ref[...], product, TN).astype(BF16)


def first_kernel(pair_ref, gate_ref, returned_ref, own_ref, grad_gate_ref, partial_ref):
    conv = conv_rows(pair_ref)
    product = (conv * gate_ref[...]).astype(BF16)
    returned = returned_ref[...]
    grad_gate = (dot(own_ref[...], returned) * conv).astype(BF16)
    grad_gate_ref[...] = dot(grad_gate, unit(), TN).astype(BF16)
    row, col = iotas(128, 128)
    grad = jnp.where(row // 64 == col // 4 % 2, dot(product, returned, NT), 0.0)
    order = ones_where(
        (row // 8 == col % 64 // 4) & (row // 4 % 2 == col // 64) & (row % 4 == col % 4)
    )
    row, col = iotas(128, 64)
    fold = ones_where(source(row) * 4 + row % 4 == col)
    partial_ref[...] = dot(order, dot(grad.astype(BF16), fold).astype(BF16))


def second_kernel(received_ref, d_out_ref, partial_ref, grads_ref, sums_ref):
    row, col = iotas(128, 128)
    grad = jnp.where(row % 4 == col // 32, dot(received_ref[...], d_out_ref[...]), 0.0)
    row, col = iotas(128, 32)
    fold = ones_where(row % 32 == col)
    pieces = [partial_ref[...]] + [dot(piece, fold) for piece in split(grad)]
    sums_ref[:, 0:1024] = grads_ref[...]
    sums_ref[:, 1024:1152] = jnp.concatenate(pieces, axis=1).astype(BF16)


def exit_kernel(sums_ref, signal_hbm, filter_hbm, first_ref, second_ref, both_ref, sems):
    square = unit()
    copies = []
    for field, target in enumerate((signal_hbm, filter_hbm)):
        values = sums_ref[:, 512 * field : 512 * field + 512]
        both_ref[field] = dot(values, square, TN).astype(BF16)
        copies.append(pltpu.make_async_copy(both_ref.at[field], target, sems.at[field]))
        copies[-1].start()
    wide = sums_ref[:, 1024:1152].astype(F32)
    total = wide[0:8, :]
    for p in range(1, 16):
        total = total + wide[8 * p : 8 * p + 8, :]
    second = total[:, 64:96] + total[:, 96:128]
    for i in range(2):
        first_ref[i] = total[4 * i : 4 * i + 4, 0:64]
        for k in range(4):
            second_ref[k, i : i + 1, :] = second[4 * i + k : 4 * i + k + 1, :]
    for copy in copies:
        copy.wait()


def call(body, outs, scratch=(), flops=1 << 26, moved=1 << 19, spaces=None):
    extra = {}
    if spaces is not None:
        extra["in_specs"], extra["out_specs"] = [
            [pl.BlockSpec(memory_space=space) for space in side] for side in spaces
        ]
    return pl.pallas_call(
        body,
        out_shape=[
            pltpu.VMEM(*out[:2]) if len(out) > 2 else jax.ShapeDtypeStruct(*out) for out in outs
        ],
        scratch_shapes=list(scratch),
        compiler_params=pltpu.CompilerParams(vmem_limit_bytes=32 << 20),
        cost_estimate=pl.CostEstimate(flops=flops, bytes_accessed=moved, transcendentals=0),
        **extra,
    )


def exchange(value, axis):
    rows, cols = value.shape
    pieces = value.reshape(16, rows // 16, cols)
    return lax.all_to_all(pieces, axis, split_axis=0, concat_axis=0, tiled=True).reshape(rows, cols)


def shift(value, y, zc):
    pairs = []
    for index in range(16):
        z, there, core = (index // 8 + zc // 2) % 2, (index // 2 + y) % 4, (index + zc) % 2
        pairs.append((index, z * 8 + there * 2 + core))
    return lax.ppermute(value, "ch", pairs)


def shards(signal, filter_raw, gate, d_out, w_first, w_second):
    rows, width = signal.shape
    outer, back, twiddle, inner = (jnp.asarray(t) for t in tables(lax.axis_size("seq"), rows))
    single, double = ((width, rows), BF16), ((2 * width, rows), BF16)
    slab = ((rows, width), BF16)
    quarter, half = ((width // 4, rows), BF16), ((width // 2, rows), BF16)
    held = [pltpu.with_memory_space_constraint(v, pltpu.HBM) for v in (d_out, w_second, signal, filter_raw)]
    near, core, far, pair = call(
        entry_kernel,
        [quarter + (True,), quarter + (True,), half + (True,), double],
        [
            pltpu.VMEM(d_out.shape, BF16),
            pltpu.VMEM(w_second.shape, BF16),
            pltpu.VMEM((2, rows, width), BF16),
            pltpu.VMEM((2 * width, rows), BF16),
            pltpu.SemaphoreType.DMA((5,)),
        ],
        spaces=([pl.ANY] * 4, [pltpu.VMEM] * 3 + [pl.ANY]),
    )(*held)
    far = shift(far, 0, 2)
    pair = exchange(pair, "seq")
    core = shift(call(core_kernel, [half], flops=1 << 35)(core, far)[0], 0, 1)
    near, *others = call(repack_kernel, [quarter] * 4)(near, core, far)
    pair = lax.optimization_barrier((pair, near))[0]
    others = [shift(value, y, 0) for y, value in zip((1, 2, 3), others)]
    square = ((128, 128), BF16)
    gate, blocks, own = call(prepare_kernel, [((width, rows), F32), square, square])(gate, w_first)
    conv, spectra = call(
        conv_kernel,
        [((4 * width, 128), F32), ((2, 512, 256), F32)],
        [pltpu.VMEM((2 * width * 4, 128), F32)],
        flops=1 << 30,
    )(pair, outer, back, twiddle, inner)
    pair, returned = call(gate_kernel, [double, single])(near, *others, own, gate, conv)
    pair = exchange(pair, "seq")
    mix = call(mix_kernel, [single])(pair, gate, blocks)[0]
    received = exchange(mix, "ch")
    grads = call(
        adjoint_kernel,
        [((width, 2 * rows), BF16)],
        [pltpu.VMEM((2 * width * 4, 128), F32), pltpu.VMEM((width * 4, 128), F32)],
        flops=1 << 30,
    )(pair, spectra, outer, back, twiddle, inner)[0]
    grad_gate, partial = call(first_kernel, [slab, ((width, 64), F32)])(
        pair, gate, returned, own
    )
    sums = call(second_kernel, [((width, 2 * rows + 128), BF16)])(received, d_out, partial, grads)[0]
    sums = exchange(sums, "seq")
    grad_signal, grad_filter, grad_first, grad_second = call(
        exit_kernel,
        [slab, slab, ((2, 4, 64), F32), ((4, 2, 32), F32)],
        [pltpu.VMEM((2, rows, width), BF16), pltpu.SemaphoreType.DMA((2,))],
        spaces=([pltpu.VMEM], [pl.ANY] * 2 + [pltpu.VMEM] * 2),
    )(sums)
    return (grad_signal, grad_filter, grad_gate, grad_first, grad_second)


def solution(mesh):
    in_specs = (
        P("seq", "ch"),
        P("seq", "ch"),
        P("seq", "ch"),
        P("seq", "ch"),
        P("ch", None, None),
        P("ch", None, None),
    )
    out_specs = (
        P("seq", "ch"),
        P("seq", "ch"),
        P("seq", "ch"),
        P("ch", "seq", None),
        P("ch", "seq", None),
    )
    return jax.shard_map(shards, mesh=mesh, in_specs=in_specs, out_specs=out_specs, check_vma=False)
```

```python
import math

import jax
import jax.numpy as jnp
import numpy as np
from jax import lax
from jax.experimental import pallas as pl
from jax.experimental.pallas import tpu as pltpu
from jax.sharding import PartitionSpec as P

F32 = jnp.float32
BF16 = jnp.bfloat16
NN = (((1,), (0,)), ((), ()))
NT = (((1,), (1,)), ((), ()))
TN = (((0,), (0,)), ((), ()))


def dot(a, b, form=NN):
    return lax.dot_general(a, b, form, preferred_element_type=F32)


def halves(table):
    high = table.astype(BF16)
    return high, (table - high.astype(np.float32)).astype(BF16)


def tables(devices, rows):
    lanes = 128
    length = 2 * devices * rows
    steps = devices * rows // lanes
    split = rows // lanes
    place = (np.arange(steps) % devices) * split + np.arange(steps) // devices
    turn = 2.0 * math.pi
    freq = np.arange(steps) + 0.5
    angle = turn * freq[:, None] * place[None, :] / (2 * steps)
    outer = np.concatenate([np.cos(angle), -np.sin(angle)], 0)
    scale = float(devices * rows) ** -0.5 * 2.0 / length
    back = scale * np.concatenate([np.cos(angle.T), -np.sin(angle.T)], 1)
    angle = turn * freq[:, None] * np.arange(lanes)[None, :] / length
    twiddle = np.concatenate([np.cos(angle), -np.sin(angle)], 1)
    angle = turn * (np.arange(lanes)[:, None] * np.arange(lanes)[None, :] % lanes) / lanes
    cosine, sine = np.cos(angle), np.sin(angle)
    inner = np.concatenate(
        [np.concatenate([cosine, -sine], 1), np.concatenate([sine, cosine], 1)], 0
    )
    outer_high, outer_low = halves(outer.astype(np.float32))
    back_high, back_low = halves(back.astype(np.float32))
    inner_high, inner_low = halves(inner.astype(np.float32))
    return (
        np.concatenate([outer_high, outer_low], 1),
        np.stack([back_high, back_low]),
        twiddle.astype(np.float32),
        np.stack([inner_high, inner_low]),
    )


def iotas(rows, cols):
    return (
        lax.broadcasted_iota(jnp.int32, (rows, cols), 0),
        lax.broadcasted_iota(jnp.int32, (rows, cols), 1),
    )


def ones_where(mask):
    return jnp.where(mask, 1.0, 0.0).astype(BF16)


def pair_order():
    row, col = iotas(256, 256)
    return ones_where((row // 16 == col % 128 // 8) & (row // 8 % 2 == col // 128) & (row % 8 == col % 8))


def unit():
    row, col = iotas(128, 128)
    return ones_where(row == col)


def place():
    index = lax.axis_index("ch")
    return index // 8, index // 2 % 4, index % 2


def partner(slot_y, slot_zc, step):
    z, y, core = place()
    z = (z + slot_zc // 2) % 2
    core = (core + slot_zc) % 2
    y = (y + 4 + step * slot_y) % 4
    return z * 8 + y * 2 + core


def entry_kernel(
    d_out_hbm,
    w_second_hbm,
    signal_hbm,
    filter_hbm,
    near_ref,
    core_ref,
    far_ref,
    pair_hbm,
    d_out_ref,
    w_second_ref,
    both_ref,
    pair_ref,
    sems,
):
    copies = [
        pltpu.make_async_copy(source, target, sems.at[index])
        for index, (source, target) in enumerate(
            (
                (signal_hbm, both_ref.at[0]),
                (filter_hbm, both_ref.at[1]),
                (w_second_hbm, w_second_ref),
                (d_out_hbm, d_out_ref),
            )
        )
    ]
    for copy in copies:
        copy.start()
    pairs = pair_order()
    row, col = iotas(32, 128)
    copies_of = ones_where(row == col % 32)
    row, col = iotas(128, 128)
    keep = row // 32 == col // 32
    block = 2 * partner(row // 8 % 4, row // 32, 1) + row // 4 % 2
    order = ones_where((block == col % 32) & (row % 4 == col // 32))
    copies[0].wait()
    copies[1].wait()
    both = jnp.concatenate([both_ref[0], both_ref[1]], axis=1)
    pair_ref[...] = dot(pairs, both, NT).astype(BF16)
    leave = pltpu.make_async_copy(pair_ref, pair_hbm, sems.at[4])
    leave.start()
    copies[2].wait()
    flat = w_second_ref[...].reshape(128, 32)
    spread = jnp.where(keep, dot(flat, copies_of), 0.0).astype(BF16)
    weights = dot(order, spread).astype(BF16)
    copies[3].wait()
    result = dot(weights, d_out_ref[...], NT).astype(BF16)
    for ref, start in zip((near_ref, core_ref, far_ref), (0, 32, 64)):
        ref[...] = result[start : start + ref.shape[0], :]
    leave.wait()


def core_kernel(core_ref, far_ref, message_ref):
    message_ref[0:32, :] = core_ref[...]
    message_ref[32:64, :] = far_ref[32:64, :]


def repack_kernel(near_ref, core_ref, far_ref, *outs):
    near, core, far = (ref[...].astype(F32) for ref in (near_ref, core_ref, far_ref))
    values = (near, core[0:32, :], far[0:32, :], core[32:64, :])
    for y, ref in enumerate(outs):
        ref[...] = jnp.concatenate([v[8 * y : 8 * y + 8, :] for v in values], axis=0).astype(BF16)


def source(col):
    return partner(col // 32, col // 8 % 4, -1)


def prepare_kernel(gate_ref, w_first_ref, gate_out_ref, blocks_ref, own_ref):
    flat = w_first_ref[...].reshape(128, 64)
    row, col = iotas(64, 128)
    keep_row, keep_col = iotas(128, 128)
    keep = keep_row // 64 == keep_col // 4 % 2
    for ref, group in ((blocks_ref, col // 8), (own_ref, source(col))):
        spread = dot(flat, ones_where(row == group * 4 + col % 4))
        ref[...] = jnp.where(keep, spread, 0.0).astype(BF16)
    gate_out_ref[...] = dot(unit(), gate_ref[...], NT)


def gate_kernel(near_ref, first_ref, second_ref, third_ref, own_ref, gate_ref, conv_ref, pair_ref, returned_ref):
    pieces = [ref[...] for ref in (near_ref, first_ref, second_ref, third_ref)]
    returned = jnp.concatenate(pieces, axis=0)
    returned_ref[...] = returned
    incoming = dot(own_ref[...], returned) * gate_ref[...]
    rows = []
    for p in range(16):
        pieces = [conv_ref[128 * th + 8 * p : 128 * th + 8 * p + 8, :] for th in range(4)]
        rows.append(jnp.concatenate(pieces, axis=1))
        rows.append(incoming[8 * p : 8 * p + 8, :])
    pair_ref[...] = jnp.concatenate(rows, axis=0).astype(BF16)


def split(value):
    high = value.astype(BF16)
    return high, (value - high.astype(F32)).astype(BF16)


def by_channel(wide_ref, first, stride):
    columns = [wide_ref[pl.ds(first + c, 64, stride=stride), :] for c in range(8)]
    return jnp.concatenate(columns, axis=1).astype(BF16)


def by_slab(wide_ref, value, first, stride):
    for c in range(8):
        wide_ref[pl.ds(first + c, 64, stride=stride), :] = value[:, 128 * c : 128 * c + 128]


def unroll(wide_ref, value):
    rows = value.shape[0]
    for th in range(4):
        wide_ref[rows * th : rows * th + rows, :] = value[:, 128 * th : 128 * th + 128].astype(F32)


def enroll(wide_ref):
    rows = wide_ref.shape[0] // 4
    pieces = [wide_ref[rows * th : rows * th + rows, :].astype(BF16) for th in range(4)]
    return jnp.concatenate(pieces, axis=1)


def transform(values, outer_ref, twiddle_ref, inner_ref):
    stage = dot(outer_ref[...], jnp.concatenate([values, values], axis=0))
    cosine, sine = twiddle_ref[:, 0:128], twiddle_ref[:, 128:256]
    rows = []
    for c in range(8):
        real = stage[0:64, 128 * c : 128 * c + 128]
        imag = stage[64:128, 128 * c : 128 * c + 128]
        rows.append(
            jnp.concatenate([real * cosine - imag * sine, real * sine + imag * cosine], axis=1)
        )
    high, low = split(jnp.concatenate(rows, axis=0))
    return dot(high, inner_ref[0]) + dot(low, inner_ref[0]) + dot(high, inner_ref[1])


def restore(real, imag, back_ref, twiddle_ref, inner_ref):
    high, low = split(jnp.concatenate([real, imag], axis=1))
    stage = dot(high, inner_ref[0], NT) + dot(low, inner_ref[0], NT) + dot(high, inner_ref[1], NT)
    cosine, sine = twiddle_ref[:, 0:128], twiddle_ref[:, 128:256]
    columns = []
    for c in range(8):
        real = stage[64 * c : 64 * c + 64, 0:128]
        imag = stage[64 * c : 64 * c + 64, 128:256]
        columns.append(
            jnp.concatenate([real * cosine + imag * sine, imag * cosine - real * sine], axis=0)
        )
    high, low = split(jnp.concatenate(columns, axis=1))
    return dot(back_ref[0], high) + dot(back_ref[0], low) + dot(back_ref[1], high)


def conv_kernel(pair_ref, outer_ref, back_ref, twiddle_ref, inner_ref, conv_ref, spectra_ref, wide_ref):
    unroll(wide_ref, pair_ref[...])
    signal = transform(by_channel(wide_ref, 0, 16), outer_ref, twiddle_ref, inner_ref)
    kernel = transform(by_channel(wide_ref, 8, 16), outer_ref, twiddle_ref, inner_ref)
    spectra_ref[0] = signal
    spectra_ref[1] = kernel
    sr, si = signal[:, 0:128], signal[:, 128:256]
    kr, ki = kernel[:, 0:128], kernel[:, 128:256]
    result = restore(sr * kr - si * ki, sr * ki + si * kr, back_ref, twiddle_ref, inner_ref)
    by_slab(conv_ref, result, 0, 8)


def adjoint_kernel(
    pair_ref, spectra_ref, outer_ref, back_ref, twiddle_ref, inner_ref, grads_ref, wide_ref, out_ref
):
    unroll(wide_ref, pair_ref[...])
    spectrum = transform(by_channel(wide_ref, 8, 16), outer_ref, twiddle_ref, inner_ref)
    gr, gi = spectrum[:, 0:128], spectrum[:, 128:256]
    for field in range(2):
        real, imag = spectra_ref[1 - field, :, 0:128], spectra_ref[1 - field, :, 128:256]
        result = restore(
            gr * real + gi * imag, gi * real - gr * imag, back_ref, twiddle_ref, inner_ref
        )
        by_slab(out_ref, result, 0, 8)
        grads_ref[:, 512 * field : 512 * field + 512] = enroll(out_ref)


def conv_rows(pair_ref):
    wide = pair_ref[...].astype(F32)
    return jnp.concatenate([wide[16 * p : 16 * p + 8, :] for p in range(16)], axis=0)


def mix_kernel(pair_ref, gate_ref, blocks_ref, mix_ref):
    product = (conv_rows(pair_ref) * gate_ref[...]).astype(BF16)
    mix_ref[...] = dot(blocks_ref[...], product, TN).astype(BF16)


def first_kernel(pair_ref, gate_ref, returned_ref, own_ref, grad_gate_ref, partial_ref):
    conv = conv_rows(pair_ref)
    product = (conv * gate_ref[...]).astype(BF16)
    returned = returned_ref[...]
    grad_gate = (dot(own_ref[...], returned) * conv).astype(BF16)
    grad_gate_ref[...] = dot(grad_gate, unit(), TN).astype(BF16)
    row, col = iotas(128, 128)
    grad = jnp.where(row // 64 == col // 4 % 2, dot(product, returned, NT), 0.0)
    order = ones_where(
        (row // 8 == col % 64 // 4) & (row // 4 % 2 == col // 64) & (row % 4 == col % 4)
    )
    row, col = iotas(128, 64)
    fold = ones_where(source(row) * 4 + row % 4 == col)
    partial_ref[...] = dot(order, dot(grad.astype(BF16), fold).astype(BF16))


def second_kernel(received_ref, d_out_ref, partial_ref, grads_ref, sums_ref):
    row, col = iotas(128, 128)
    grad = jnp.where(row % 4 == col // 32, dot(received_ref[...], d_out_ref[...]), 0.0)
    row, col = iotas(128, 32)
    fold = ones_where(row % 32 == col)
    pieces = [partial_ref[...]] + [dot(piece, fold) for piece in split(grad)]
    sums_ref[:, 0:1024] = grads_ref[...]
    sums_ref[:, 1024:1152] = jnp.concatenate(pieces, axis=1).astype(BF16)


def exit_kernel(
    sums_ref, signal_hbm, filter_hbm, first_hbm, second_hbm, both_ref, first_ref, second_ref, sems
):
    copies = []

    def leave(source, target):
        copies.append(pltpu.make_async_copy(source, target, sems.at[len(copies)]))
        copies[-1].start()

    square = unit()
    for field, target in enumerate((signal_hbm, filter_hbm)):
        values = sums_ref[:, 512 * field : 512 * field + 512]
        both_ref[field] = dot(values, square, TN).astype(BF16)
        leave(both_ref.at[field], target)
    wide = sums_ref[:, 1024:1152].astype(F32)
    total = wide[0:8, :]
    for p in range(1, 16):
        total = total + wide[8 * p : 8 * p + 8, :]
    second = total[:, 64:96] + total[:, 96:128]
    for i in range(2):
        first_ref[i] = total[4 * i : 4 * i + 4, 0:64]
        for k in range(4):
            second_ref[k, i : i + 1, :] = second[4 * i + k : 4 * i + k + 1, :]
    leave(first_ref, first_hbm)
    leave(second_ref, second_hbm)
    for copy in copies:
        copy.wait()


def call(body, outs, scratch=(), flops=1 << 26, moved=1 << 19, spaces=None):
    extra = {}
    if spaces is not None:
        extra["in_specs"], extra["out_specs"] = [
            [pl.BlockSpec(memory_space=space) for space in side] for side in spaces
        ]
    return pl.pallas_call(
        body,
        out_shape=[
            pltpu.VMEM(*out[:2]) if len(out) > 2 else jax.ShapeDtypeStruct(*out) for out in outs
        ],
        scratch_shapes=list(scratch),
        compiler_params=pltpu.CompilerParams(vmem_limit_bytes=32 << 20),
        cost_estimate=pl.CostEstimate(flops=flops, bytes_accessed=moved, transcendentals=0),
        **extra,
    )


def exchange(value, axis):
    rows, cols = value.shape
    pieces = value.reshape(16, rows // 16, cols)
    return lax.all_to_all(pieces, axis, split_axis=0, concat_axis=0, tiled=True).reshape(rows, cols)


def shift(value, y, zc):
    pairs = []
    for index in range(16):
        z, there, core = (index // 8 + zc // 2) % 2, (index // 2 + y) % 4, (index + zc) % 2
        pairs.append((index, z * 8 + there * 2 + core))
    return lax.ppermute(value, "ch", pairs)


def shards(signal, filter_raw, gate, d_out, w_first, w_second):
    rows, width = signal.shape
    outer, back, twiddle, inner = (jnp.asarray(t) for t in tables(lax.axis_size("seq"), rows))
    single, double = ((width, rows), BF16), ((2 * width, rows), BF16)
    slab = ((rows, width), BF16)
    quarter, half = ((width // 4, rows), BF16), ((width // 2, rows), BF16)
    held = [pltpu.with_memory_space_constraint(v, pltpu.HBM) for v in (d_out, w_second, signal, filter_raw)]
    near, core, far, pair = call(
        entry_kernel,
        [quarter + (True,), quarter + (True,), half + (True,), double],
        [
            pltpu.VMEM(d_out.shape, BF16),
            pltpu.VMEM(w_second.shape, BF16),
            pltpu.VMEM((2, rows, width), BF16),
            pltpu.VMEM((2 * width, rows), BF16),
            pltpu.SemaphoreType.DMA((5,)),
        ],
        spaces=([pl.ANY] * 4, [pltpu.VMEM] * 3 + [pl.ANY]),
    )(*held)
    far = shift(far, 0, 2)
    pair = exchange(pair, "seq")
    core = shift(call(core_kernel, [half], flops=1 << 35)(core, far)[0], 0, 1)
    near, *others = call(repack_kernel, [quarter] * 4)(near, core, far)
    pair = lax.optimization_barrier((pair, near))[0]
    others = [shift(value, y, 0) for y, value in zip((1, 2, 3), others)]
    square = ((128, 128), BF16)
    gate, blocks, own = call(prepare_kernel, [((width, rows), F32), square, square])(gate, w_first)
    conv, spectra = call(
        conv_kernel,
        [((4 * width, 128), F32), ((2, 512, 256), F32)],
        [pltpu.VMEM((2 * width * 4, 128), F32)],
        flops=1 << 30,
    )(pair, outer, back, twiddle, inner)
    pair, returned = call(gate_kernel, [double, single])(near, *others, own, gate, conv)
    pair = exchange(pair, "seq")
    mix = call(mix_kernel, [single])(pair, gate, blocks)[0]
    received = exchange(mix, "ch")
    grads = call(
        adjoint_kernel,
        [((width, 2 * rows), BF16)],
        [pltpu.VMEM((2 * width * 4, 128), F32), pltpu.VMEM((width * 4, 128), F32)],
        flops=1 << 30,
    )(pair, spectra, outer, back, twiddle, inner)[0]
    grad_gate, partial = call(first_kernel, [slab, ((width, 64), F32)])(
        pair, gate, returned, own
    )
    sums = call(second_kernel, [((width, 2 * rows + 128), BF16)])(received, d_out, partial, grads)[0]
    sums = exchange(sums, "seq")
    grad_signal, grad_filter, grad_first, grad_second = call(
        exit_kernel,
        [slab, slab, ((2, 4, 64), F32), ((4, 2, 32), F32)],
        [
            pltpu.VMEM((2, rows, width), BF16),
            pltpu.VMEM((2, 4, 64), F32),
            pltpu.VMEM((4, 2, 32), F32),
            pltpu.SemaphoreType.DMA((4,)),
        ],
        spaces=([pltpu.VMEM], [pl.ANY] * 4),
    )(sums)
    return (grad_signal, grad_filter, grad_gate, grad_first, grad_second)


def solution(mesh):
    in_specs = (
        P("seq", "ch"),
        P("seq", "ch"),
        P("seq", "ch"),
        P("seq", "ch"),
        P("ch", None, None),
        P("ch", None, None),
    )
    out_specs = (
        P("seq", "ch"),
        P("seq", "ch"),
        P("seq", "ch"),
        P("ch", "seq", None),
        P("ch", "seq", None),
    )
    return jax.shard_map(shards, mesh=mesh, in_specs=in_specs, out_specs=out_specs, check_vma=False)
```

```python
import math

import jax
import jax.numpy as jnp
import numpy as np
from jax import lax
from jax.experimental import pallas as pl
from jax.experimental.pallas import tpu as pltpu
from jax.sharding import PartitionSpec as P

F32 = jnp.float32
BF16 = jnp.bfloat16
NN = (((1,), (0,)), ((), ()))
NT = (((1,), (1,)), ((), ()))
TN = (((0,), (0,)), ((), ()))


def dot(a, b, form=NN):
    return lax.dot_general(a, b, form, preferred_element_type=F32)


def halves(table):
    high = table.astype(BF16)
    return high, (table - high.astype(np.float32)).astype(BF16)


def tables(devices, rows):
    lanes = 128
    length = 2 * devices * rows
    steps = devices * rows // lanes
    split = rows // lanes
    place = (np.arange(steps) % devices) * split + np.arange(steps) // devices
    turn = 2.0 * math.pi
    freq = np.arange(steps) + 0.5
    angle = turn * freq[:, None] * place[None, :] / (2 * steps)
    outer = np.concatenate([np.cos(angle), -np.sin(angle)], 0)
    scale = float(devices * rows) ** -0.5 * 2.0 / length
    back = scale * np.concatenate([np.cos(angle.T), -np.sin(angle.T)], 1)
    angle = turn * freq[:, None] * np.arange(lanes)[None, :] / length
    twiddle = np.concatenate([np.cos(angle), -np.sin(angle)], 1)
    angle = turn * (np.arange(lanes)[:, None] * np.arange(lanes)[None, :] % lanes) / lanes
    cosine, sine = np.cos(angle), np.sin(angle)
    inner = np.concatenate(
        [np.concatenate([cosine, -sine], 1), np.concatenate([sine, cosine], 1)], 0
    )
    outer_high, outer_low = halves(outer.astype(np.float32))
    back_high, back_low = halves(back.astype(np.float32))
    inner_high, inner_low = halves(inner.astype(np.float32))
    return (
        np.concatenate([outer_high, outer_low], 1),
        np.stack([back_high, back_low]),
        twiddle.astype(np.float32),
        np.stack([inner_high, inner_low]),
    )


def iotas(rows, cols):
    return (
        lax.broadcasted_iota(jnp.int32, (rows, cols), 0),
        lax.broadcasted_iota(jnp.int32, (rows, cols), 1),
    )


def ones_where(mask):
    return jnp.where(mask, 1.0, 0.0).astype(BF16)


def pair_order():
    row, col = iotas(256, 256)
    return ones_where((row // 16 == col % 128 // 8) & (row // 8 % 2 == col // 128) & (row % 8 == col % 8))


def unit():
    row, col = iotas(128, 128)
    return ones_where(row == col)


def place():
    index = lax.axis_index("ch")
    return index // 8, index // 2 % 4, index % 2


def partner(slot_y, slot_zc, step):
    z, y, core = place()
    z = (z + slot_zc // 2) % 2
    core = (core + slot_zc) % 2
    y = (y + 4 + step * slot_y) % 4
    return z * 8 + y * 2 + core


def entry_kernel(
    d_out_hbm,
    w_second_hbm,
    signal_hbm,
    filter_hbm,
    near_ref,
    core_ref,
    far_ref,
    pair_hbm,
    d_out_ref,
    w_second_ref,
    both_ref,
    pair_ref,
    sems,
):
    copies = [
        pltpu.make_async_copy(source, target, sems.at[index])
        for index, (source, target) in enumerate(
            (
                (signal_hbm, both_ref.at[0]),
                (filter_hbm, both_ref.at[1]),
                (w_second_hbm, w_second_ref),
                (d_out_hbm, d_out_ref),
            )
        )
    ]
    for copy in copies:
        copy.start()
    pairs = pair_order()
    row, col = iotas(32, 128)
    copies_of = ones_where(row == col % 32)
    row, col = iotas(128, 128)
    keep = row // 32 == col // 32
    block = 2 * target(row) + row // 4 % 2
    order = ones_where((block == col % 32) & (row % 4 == col // 32))
    copies[0].wait()
    copies[1].wait()
    both = jnp.concatenate([both_ref[0], both_ref[1]], axis=1)
    pair_ref[...] = dot(pairs, both, NT).astype(BF16)
    leave = pltpu.make_async_copy(pair_ref, pair_hbm, sems.at[4])
    leave.start()
    copies[2].wait()
    flat = w_second_ref[...].reshape(128, 32)
    spread = jnp.where(keep, dot(flat, copies_of), 0.0).astype(BF16)
    weights = dot(order, spread).astype(BF16)
    copies[3].wait()
    result = dot(weights, d_out_ref[...], NT).astype(BF16)
    for ref, start in zip((near_ref, core_ref, far_ref), (0, 32, 64)):
        ref[...] = result[start : start + ref.shape[0], :]
    leave.wait()


def core_kernel(core_ref, far_ref, message_ref):
    message_ref[0:32, :] = core_ref[...]
    message_ref[32:64, :] = far_ref[32:64, :]


def repack_kernel(near_ref, core_ref, far_ref, *outs):
    near, core, far = (ref[...].astype(F32) for ref in (near_ref, core_ref, far_ref))
    values = (near, core[0:32, :], far[0:32, :], core[32:64, :])
    for y, ref in enumerate(outs):
        ref[...] = jnp.concatenate([v[8 * y : 8 * y + 8, :] for v in values], axis=0).astype(BF16)


def target(col):
    return partner(col // 8 % 4, col // 32, 1)


def source(col):
    return partner(col // 32, col // 8 % 4, -1)


def prepare_kernel(gate_ref, w_first_ref, gate_out_ref, blocks_ref, own_ref):
    flat = w_first_ref[...].reshape(128, 64)
    row, col = iotas(64, 128)
    keep_row, keep_col = iotas(128, 128)
    keep = keep_row // 64 == keep_col // 4 % 2
    for ref, group in ((blocks_ref, target(col)), (own_ref, source(col))):
        spread = dot(flat, ones_where(row == group * 4 + col % 4))
        ref[...] = jnp.where(keep, spread, 0.0).astype(BF16)
    gate_out_ref[...] = dot(unit(), gate_ref[...], NT)


def gate_kernel(near_ref, first_ref, second_ref, third_ref, own_ref, gate_ref, conv_ref, pair_ref, returned_ref):
    pieces = [ref[...] for ref in (near_ref, first_ref, second_ref, third_ref)]
    returned = jnp.concatenate(pieces, axis=0)
    returned_ref[...] = returned
    incoming = dot(own_ref[...], returned) * gate_ref[...]
    rows = []
    for p in range(16):
        pieces = [conv_ref[128 * th + 8 * p : 128 * th + 8 * p + 8, :] for th in range(4)]
        rows.append(jnp.concatenate(pieces, axis=1))
        rows.append(incoming[8 * p : 8 * p + 8, :])
    pair_ref[...] = jnp.concatenate(rows, axis=0).astype(BF16)


def split(value):
    high = value.astype(BF16)
    return high, (value - high.astype(F32)).astype(BF16)


def by_channel(wide_ref, first, stride):
    columns = [wide_ref[pl.ds(first + c, 64, stride=stride), :] for c in range(8)]
    return jnp.concatenate(columns, axis=1).astype(BF16)


def by_slab(wide_ref, value, first, stride):
    for c in range(8):
        wide_ref[pl.ds(first + c, 64, stride=stride), :] = value[:, 128 * c : 128 * c + 128]


def unroll(wide_ref, value):
    rows = value.shape[0]
    for th in range(4):
        wide_ref[rows * th : rows * th + rows, :] = value[:, 128 * th : 128 * th + 128].astype(F32)


def enroll(wide_ref):
    rows = wide_ref.shape[0] // 4
    pieces = [wide_ref[rows * th : rows * th + rows, :].astype(BF16) for th in range(4)]
    return jnp.concatenate(pieces, axis=1)


def transform(values, outer_ref, twiddle_ref, inner_ref):
    stage = dot(outer_ref[...], jnp.concatenate([values, values], axis=0))
    cosine, sine = twiddle_ref[:, 0:128], twiddle_ref[:, 128:256]
    rows = []
    for c in range(8):
        real = stage[0:64, 128 * c : 128 * c + 128]
        imag = stage[64:128, 128 * c : 128 * c + 128]
        rows.append(
            jnp.concatenate([real * cosine - imag * sine, real * sine + imag * cosine], axis=1)
        )
    high, low = split(jnp.concatenate(rows, axis=0))
    return dot(high, inner_ref[0]) + dot(low, inner_ref[0]) + dot(high, inner_ref[1])


def restore(real, imag, back_ref, twiddle_ref, inner_ref):
    high, low = split(jnp.concatenate([real, imag], axis=1))
    stage = dot(high, inner_ref[0], NT) + dot(low, inner_ref[0], NT) + dot(high, inner_ref[1], NT)
    cosine, sine = twiddle_ref[:, 0:128], twiddle_ref[:, 128:256]
    columns = []
    for c in range(8):
        real = stage[64 * c : 64 * c + 64, 0:128]
        imag = stage[64 * c : 64 * c + 64, 128:256]
        columns.append(
            jnp.concatenate([real * cosine + imag * sine, imag * cosine - real * sine], axis=0)
        )
    high, low = split(jnp.concatenate(columns, axis=1))
    return dot(back_ref[0], high) + dot(back_ref[0], low) + dot(back_ref[1], high)


def conv_kernel(pair_ref, outer_ref, back_ref, twiddle_ref, inner_ref, conv_ref, spectra_ref, wide_ref):
    unroll(wide_ref, pair_ref[...])
    signal = transform(by_channel(wide_ref, 0, 16), outer_ref, twiddle_ref, inner_ref)
    kernel = transform(by_channel(wide_ref, 8, 16), outer_ref, twiddle_ref, inner_ref)
    spectra_ref[0] = signal
    spectra_ref[1] = kernel
    sr, si = signal[:, 0:128], signal[:, 128:256]
    kr, ki = kernel[:, 0:128], kernel[:, 128:256]
    result = restore(sr * kr - si * ki, sr * ki + si * kr, back_ref, twiddle_ref, inner_ref)
    by_slab(conv_ref, result, 0, 8)


def adjoint_kernel(
    pair_ref, spectra_ref, outer_ref, back_ref, twiddle_ref, inner_ref, grads_ref, wide_ref, out_ref
):
    unroll(wide_ref, pair_ref[...])
    spectrum = transform(by_channel(wide_ref, 8, 16), outer_ref, twiddle_ref, inner_ref)
    gr, gi = spectrum[:, 0:128], spectrum[:, 128:256]
    for field in range(2):
        real, imag = spectra_ref[1 - field, :, 0:128], spectra_ref[1 - field, :, 128:256]
        result = restore(
            gr * real + gi * imag, gi * real - gr * imag, back_ref, twiddle_ref, inner_ref
        )
        by_slab(out_ref, result, 0, 8)
        grads_ref[:, 512 * field : 512 * field + 512] = enroll(out_ref)


def conv_rows(pair_ref):
    wide = pair_ref[...].astype(F32)
    return jnp.concatenate([wide[16 * p : 16 * p + 8, :] for p in range(16)], axis=0)


def mix_kernel(pair_ref, gate_ref, blocks_ref, near_ref, core_ref, far_ref):
    product = (conv_rows(pair_ref) * gate_ref[...]).astype(BF16)
    result = dot(blocks_ref[...], product, TN).astype(BF16)
    for ref, start in zip((near_ref, core_ref, far_ref), (0, 32, 64)):
        ref[...] = result[start : start + ref.shape[0], :]


def first_kernel(pair_ref, gate_ref, returned_ref, own_ref, grad_gate_ref, partial_ref):
    conv = conv_rows(pair_ref)
    product = (conv * gate_ref[...]).astype(BF16)
    returned = returned_ref[...]
    grad_gate = (dot(own_ref[...], returned) * conv).astype(BF16)
    grad_gate_ref[...] = dot(grad_gate, unit(), TN).astype(BF16)
    row, col = iotas(128, 128)
    grad = jnp.where(row // 64 == col // 4 % 2, dot(product, returned, NT), 0.0)
    order = ones_where(
        (row // 8 == col % 64 // 4) & (row // 4 % 2 == col // 64) & (row % 4 == col % 4)
    )
    row, col = iotas(128, 64)
    fold = ones_where(source(row) * 4 + row % 4 == col)
    partial_ref[...] = dot(order, dot(grad.astype(BF16), fold).astype(BF16))


def second_kernel(*refs):
    pieces, (d_out_ref, partial_ref, sums_ref) = refs[:4], refs[4:]
    received = jnp.concatenate([ref[...] for ref in pieces], axis=0)
    row, col = iotas(128, 128)
    grad = jnp.where(row % 4 == col // 32, dot(received, d_out_ref[...]), 0.0)
    order = ones_where((source(col) == row // 8) & (row % 8 == col % 8))
    row, col = iotas(128, 32)
    fold = ones_where(row % 32 == col)
    parts = [dot(order, dot(piece, fold).astype(BF16)) for piece in split(grad)]
    sums_ref[...] = jnp.concatenate([partial_ref[...]] + parts, axis=1).astype(BF16)


def leave_all(pairs, sems):
    copies = []
    for index, (source, target) in enumerate(pairs):
        copies.append(pltpu.make_async_copy(source, target, sems.at[index]))
        copies[-1].start()
    for copy in copies:
        copy.wait()


def exit_kernel(grads_ref, signal_hbm, filter_hbm, both_ref, sems):
    square = unit()
    for field in range(2):
        values = grads_ref[:, 512 * field : 512 * field + 512]
        both_ref[field] = dot(values, square, TN).astype(BF16)
    leave_all(((both_ref.at[0], signal_hbm), (both_ref.at[1], filter_hbm)), sems)


def sum_kernel(sums_ref, first_ref, second_ref):
    wide = sums_ref[...].astype(F32)
    total = wide[0:8, :]
    for p in range(1, 16):
        total = total + wide[8 * p : 8 * p + 8, :]
    second = total[:, 64:96] + total[:, 96:128]
    for i in range(2):
        first_ref[i] = total[4 * i : 4 * i + 4, 0:64]
        for k in range(4):
            second_ref[k, i : i + 1, :] = second[4 * i + k : 4 * i + k + 1, :]


def call(body, outs, scratch=(), flops=1 << 26, moved=1 << 19, spaces=None):
    extra = {}
    if spaces is not None:
        extra["in_specs"], extra["out_specs"] = [
            [pl.BlockSpec(memory_space=space) for space in side] for side in spaces
        ]
    return pl.pallas_call(
        body,
        out_shape=[
            pltpu.VMEM(*out[:2]) if len(out) > 2 else jax.ShapeDtypeStruct(*out) for out in outs
        ],
        scratch_shapes=list(scratch),
        compiler_params=pltpu.CompilerParams(vmem_limit_bytes=32 << 20),
        cost_estimate=pl.CostEstimate(flops=flops, bytes_accessed=moved, transcendentals=0),
        **extra,
    )


def exchange(value, axis):
    rows, cols = value.shape
    pieces = value.reshape(16, rows // 16, cols)
    return lax.all_to_all(pieces, axis, split_axis=0, concat_axis=0, tiled=True).reshape(rows, cols)


def shift(value, y, zc):
    pairs = []
    for index in range(16):
        z, there, core = (index // 8 + zc // 2) % 2, (index // 2 + y) % 4, (index + zc) % 2
        pairs.append((index, z * 8 + there * 2 + core))
    return lax.ppermute(value, "ch", pairs)


def cross(near, core, far):
    rows, width = near.shape
    half, quarter = ((2 * rows, width), BF16), ((rows, width), BF16)
    core = shift(call(core_kernel, [half], flops=1 << 35)(core, far)[0], 0, 1)
    near, *others = call(repack_kernel, [quarter] * 4)(near, core, far)
    return near, lambda: [shift(value, y, 0) for y, value in zip((1, 2, 3), others)]


def shards(signal, filter_raw, gate, d_out, w_first, w_second):
    rows, width = signal.shape
    outer, back, twiddle, inner = (jnp.asarray(t) for t in tables(lax.axis_size("seq"), rows))
    single, double = ((width, rows), BF16), ((2 * width, rows), BF16)
    slab = ((rows, width), BF16)
    quarter, half = ((width // 4, rows), BF16), ((width // 2, rows), BF16)
    held = [pltpu.with_memory_space_constraint(v, pltpu.HBM) for v in (d_out, w_second, signal, filter_raw)]
    near, core, far, pair = call(
        entry_kernel,
        [quarter + (True,), quarter + (True,), half + (True,), double],
        [
            pltpu.VMEM(d_out.shape, BF16),
            pltpu.VMEM(w_second.shape, BF16),
            pltpu.VMEM((2, rows, width), BF16),
            pltpu.VMEM((2 * width, rows), BF16),
            pltpu.SemaphoreType.DMA((5,)),
        ],
        spaces=([pl.ANY] * 4, [pltpu.VMEM] * 3 + [pl.ANY]),
    )(*held)
    far = shift(far, 0, 2)
    pair = exchange(pair, "seq")
    near, turns = cross(near, core, far)
    pair = lax.optimization_barrier((pair, near))[0]
    others = turns()
    square = ((128, 128), BF16)
    gate, blocks, own = call(prepare_kernel, [((width, rows), F32), square, square])(gate, w_first)
    conv, spectra = call(
        conv_kernel,
        [((4 * width, 128), F32), ((2, 512, 256), F32)],
        [pltpu.VMEM((2 * width * 4, 128), F32)],
        flops=1 << 30,
    )(pair, outer, back, twiddle, inner)
    pair, returned = call(gate_kernel, [double, single])(near, *others, own, gate, conv)
    pair = exchange(pair, "seq")
    near, core, far = call(mix_kernel, [quarter + (True,), quarter + (True,), half + (True,)])(
        pair, gate, blocks
    )
    far = shift(far, 0, 2)
    grads = call(
        adjoint_kernel,
        [((width, 2 * rows), BF16)],
        [pltpu.VMEM((2 * width * 4, 128), F32), pltpu.VMEM((width * 4, 128), F32)],
        flops=1 << 30,
    )(pair, spectra, outer, back, twiddle, inner)[0]
    grads = exchange(grads, "seq")
    grad_gate, partial = call(first_kernel, [slab, ((width, 64), F32)])(
        pair, gate, returned, own
    )
    near, turns = cross(near, core, far)
    sums = call(second_kernel, [((width, 128), BF16)])(near, *turns(), d_out, partial)[0]
    sums, grads = lax.optimization_barrier((sums, grads))
    sums = exchange(sums, "seq")
    grad_signal, grad_filter = call(
        exit_kernel,
        [slab, slab],
        [pltpu.VMEM((2, rows, width), BF16), pltpu.SemaphoreType.DMA((2,))],
        spaces=([pltpu.VMEM], [pl.ANY] * 2),
    )(grads)
    grad_first, grad_second = call(sum_kernel, [((2, 4, 64), F32), ((4, 2, 32), F32)])(sums)
    return (grad_signal, grad_filter, grad_gate, grad_first, grad_second)


def solution(mesh):
    in_specs = (
        P("seq", "ch"),
        P("seq", "ch"),
        P("seq", "ch"),
        P("seq", "ch"),
        P("ch", None, None),
        P("ch", None, None),
    )
    out_specs = (
        P("seq", "ch"),
        P("seq", "ch"),
        P("seq", "ch"),
        P("ch", "seq", None),
        P("ch", "seq", None),
    )
    return jax.shard_map(shards, mesh=mesh, in_specs=in_specs, out_specs=out_specs, check_vma=False)
```

```python
import math

import jax
import jax.numpy as jnp
import numpy as np
from jax import lax
from jax.experimental import pallas as pl
from jax.experimental.pallas import tpu as pltpu
from jax.sharding import PartitionSpec as P

F32 = jnp.float32
BF16 = jnp.bfloat16
NN = (((1,), (0,)), ((), ()))
NT = (((1,), (1,)), ((), ()))
TN = (((0,), (0,)), ((), ()))


def dot(a, b, form=NN):
    return lax.dot_general(a, b, form, preferred_element_type=F32)


def halves(table):
    high = table.astype(BF16)
    return high, (table - high.astype(np.float32)).astype(BF16)


def tables(devices, rows):
    lanes = 128
    length = 2 * devices * rows
    steps = devices * rows // lanes
    split = rows // lanes
    place = (np.arange(steps) % devices) * split + np.arange(steps) // devices
    turn = 2.0 * math.pi
    freq = np.arange(steps) + 0.5
    angle = turn * freq[:, None] * place[None, :] / (2 * steps)
    outer = np.concatenate([np.cos(angle), -np.sin(angle)], 0)
    scale = float(devices * rows) ** -0.5 * 2.0 / length
    back = scale * np.concatenate([np.cos(angle.T), -np.sin(angle.T)], 1)
    angle = turn * freq[:, None] * np.arange(lanes)[None, :] / length
    twiddle = np.concatenate([np.cos(angle), -np.sin(angle)], 1)
    angle = turn * (np.arange(lanes)[:, None] * np.arange(lanes)[None, :] % lanes) / lanes
    cosine, sine = np.cos(angle), np.sin(angle)
    inner = np.concatenate(
        [np.concatenate([cosine, -sine], 1), np.concatenate([sine, cosine], 1)], 0
    )
    outer_high, outer_low = halves(outer.astype(np.float32))
    back_high, back_low = halves(back.astype(np.float32))
    inner_high, inner_low = halves(inner.astype(np.float32))
    return (
        np.concatenate([outer_high, outer_low], 1),
        np.stack([back_high, back_low]),
        twiddle.astype(np.float32),
        np.stack([inner_high, inner_low]),
    )


def iotas(rows, cols):
    return (
        lax.broadcasted_iota(jnp.int32, (rows, cols), 0),
        lax.broadcasted_iota(jnp.int32, (rows, cols), 1),
    )


def ones_where(mask):
    return jnp.where(mask, 1.0, 0.0).astype(BF16)


def pair_order():
    row, col = iotas(256, 256)
    return ones_where((row // 16 == col % 128 // 8) & (row // 8 % 2 == col // 128) & (row % 8 == col % 8))


def unit():
    row, col = iotas(128, 128)
    return ones_where(row == col)


def place():
    index = lax.axis_index("ch")
    return index // 8, index // 2 % 4, index % 2


def partner(slot_y, slot_zc, step):
    z, y, core = place()
    z = (z + slot_zc // 2) % 2
    core = (core + slot_zc) % 2
    y = (y + 4 + step * slot_y) % 4
    return z * 8 + y * 2 + core


def entry_kernel(
    d_out_hbm,
    w_second_hbm,
    signal_hbm,
    filter_hbm,
    near_ref,
    core_ref,
    far_ref,
    pair_hbm,
    d_out_ref,
    w_second_ref,
    both_ref,
    pair_ref,
    sems,
):
    copies = [
        pltpu.make_async_copy(source, target, sems.at[index])
        for index, (source, target) in enumerate(
            (
                (signal_hbm, both_ref.at[0]),
                (filter_hbm, both_ref.at[1]),
                (w_second_hbm, w_second_ref),
                (d_out_hbm, d_out_ref),
            )
        )
    ]
    for copy in copies:
        copy.start()
    pairs = pair_order()
    row, col = iotas(32, 128)
    copies_of = ones_where(row == col % 32)
    row, col = iotas(128, 128)
    keep = row // 32 == col // 32
    block = 2 * partner(row // 8 % 4, row // 32, 1) + row // 4 % 2
    order = ones_where((block == col % 32) & (row % 4 == col // 32))
    copies[0].wait()
    copies[1].wait()
    both = jnp.concatenate([both_ref[0], both_ref[1]], axis=1)
    pair_ref[...] = dot(pairs, both, NT).astype(BF16)
    leave = pltpu.make_async_copy(pair_ref, pair_hbm, sems.at[4])
    leave.start()
    copies[2].wait()
    flat = w_second_ref[...].reshape(128, 32)
    spread = jnp.where(keep, dot(flat, copies_of), 0.0).astype(BF16)
    weights = dot(order, spread).astype(BF16)
    copies[3].wait()
    result = dot(weights, d_out_ref[...], NT).astype(BF16)
    for ref, start in zip((near_ref, core_ref, far_ref), (0, 32, 64)):
        ref[...] = result[start : start + ref.shape[0], :]
    leave.wait()


def core_kernel(core_ref, far_ref, message_ref):
    message_ref[0:32, :] = core_ref[...]
    message_ref[32:64, :] = far_ref[32:64, :]


def repack_kernel(near_ref, core_ref, far_ref, *outs):
    near, core, far = (ref[...].astype(F32) for ref in (near_ref, core_ref, far_ref))
    values = (near, core[0:32, :], far[0:32, :], core[32:64, :])
    for y, ref in enumerate(outs):
        ref[...] = jnp.concatenate([v[8 * y : 8 * y + 8, :] for v in values], axis=0).astype(BF16)


def source(col):
    return partner(col // 32, col // 8 % 4, -1)


def prepare_kernel(gate_ref, w_first_ref, gate_out_ref, blocks_ref, own_ref):
    flat = w_first_ref[...].reshape(128, 64)
    row, col = iotas(64, 128)
    keep_row, keep_col = iotas(128, 128)
    keep = keep_row // 64 == keep_col // 4 % 2
    for ref, group in ((blocks_ref, col // 8), (own_ref, source(col))):
        spread = dot(flat, ones_where(row == group * 4 + col % 4))
        ref[...] = jnp.where(keep, spread, 0.0).astype(BF16)
    gate_out_ref[...] = dot(unit(), gate_ref[...], NT)


def gate_kernel(near_ref, first_ref, second_ref, third_ref, own_ref, gate_ref, conv_ref, pair_ref, returned_ref):
    pieces = [ref[...] for ref in (near_ref, first_ref, second_ref, third_ref)]
    returned = jnp.concatenate(pieces, axis=0)
    returned_ref[...] = returned
    incoming = dot(own_ref[...], returned) * gate_ref[...]
    rows = []
    for p in range(16):
        pieces = [conv_ref[128 * th + 8 * p : 128 * th + 8 * p + 8, :] for th in range(4)]
        rows.append(jnp.concatenate(pieces, axis=1))
        rows.append(incoming[8 * p : 8 * p + 8, :])
    pair_ref[...] = jnp.concatenate(rows, axis=0).astype(BF16)


def split(value):
    high = value.astype(BF16)
    return high, (value - high.astype(F32)).astype(BF16)


def by_channel(wide_ref, first, stride):
    columns = [wide_ref[pl.ds(first + c, 64, stride=stride), :] for c in range(8)]
    return jnp.concatenate(columns, axis=1).astype(BF16)


def by_slab(wide_ref, value, first, stride):
    for c in range(8):
        wide_ref[pl.ds(first + c, 64, stride=stride), :] = value[:, 128 * c : 128 * c + 128]


def unroll(wide_ref, value):
    rows = value.shape[0]
    for th in range(4):
        wide_ref[rows * th : rows * th + rows, :] = value[:, 128 * th : 128 * th + 128].astype(F32)


def enroll(wide_ref):
    rows = wide_ref.shape[0] // 4
    pieces = [wide_ref[rows * th : rows * th + rows, :].astype(BF16) for th in range(4)]
    return jnp.concatenate(pieces, axis=1)


def transform(values, outer_ref, twiddle_ref, inner_ref):
    stage = dot(outer_ref[...], jnp.concatenate([values, values], axis=0))
    cosine, sine = twiddle_ref[:, 0:128], twiddle_ref[:, 128:256]
    rows = []
    for c in range(8):
        real = stage[0:64, 128 * c : 128 * c + 128]
        imag = stage[64:128, 128 * c : 128 * c + 128]
        rows.append(
            jnp.concatenate([real * cosine - imag * sine, real * sine + imag * cosine], axis=1)
        )
    high, low = split(jnp.concatenate(rows, axis=0))
    return dot(high, inner_ref[0]) + dot(low, inner_ref[0]) + dot(high, inner_ref[1])


def restore(real, imag, back_ref, twiddle_ref, inner_ref):
    high, low = split(jnp.concatenate([real, imag], axis=1))
    stage = dot(high, inner_ref[0], NT) + dot(low, inner_ref[0], NT) + dot(high, inner_ref[1], NT)
    cosine, sine = twiddle_ref[:, 0:128], twiddle_ref[:, 128:256]
    columns = []
    for c in range(8):
        real = stage[64 * c : 64 * c + 64, 0:128]
        imag = stage[64 * c : 64 * c + 64, 128:256]
        columns.append(
            jnp.concatenate([real * cosine + imag * sine, imag * cosine - real * sine], axis=0)
        )
    high, low = split(jnp.concatenate(columns, axis=1))
    return dot(back_ref[0], high) + dot(back_ref[0], low) + dot(back_ref[1], high)


def conv_kernel(pair_ref, outer_ref, back_ref, twiddle_ref, inner_ref, conv_ref, spectra_ref, wide_ref):
    unroll(wide_ref, pair_ref[...])
    signal = transform(by_channel(wide_ref, 0, 16), outer_ref, twiddle_ref, inner_ref)
    kernel = transform(by_channel(wide_ref, 8, 16), outer_ref, twiddle_ref, inner_ref)
    spectra_ref[0] = signal
    spectra_ref[1] = kernel
    sr, si = signal[:, 0:128], signal[:, 128:256]
    kr, ki = kernel[:, 0:128], kernel[:, 128:256]
    result = restore(sr * kr - si * ki, sr * ki + si * kr, back_ref, twiddle_ref, inner_ref)
    by_slab(conv_ref, result, 0, 8)


def adjoint_kernel(
    pair_ref, spectra_ref, outer_ref, back_ref, twiddle_ref, inner_ref, grads_ref, wide_ref, out_ref
):
    unroll(wide_ref, pair_ref[...])
    spectrum = transform(by_channel(wide_ref, 8, 16), outer_ref, twiddle_ref, inner_ref)
    gr, gi = spectrum[:, 0:128], spectrum[:, 128:256]
    for field in range(2):
        real, imag = spectra_ref[1 - field, :, 0:128], spectra_ref[1 - field, :, 128:256]
        result = restore(
            gr * real + gi * imag, gi * real - gr * imag, back_ref, twiddle_ref, inner_ref
        )
        by_slab(out_ref, result, 0, 8)
        grads_ref[:, 512 * field : 512 * field + 512] = enroll(out_ref)


def conv_rows(pair_ref):
    wide = pair_ref[...].astype(F32)
    return jnp.concatenate([wide[16 * p : 16 * p + 8, :] for p in range(16)], axis=0)


def mix_kernel(pair_ref, gate_ref, blocks_ref, mix_ref):
    product = (conv_rows(pair_ref) * gate_ref[...]).astype(BF16)
    mix_ref[...] = dot(blocks_ref[...], product, TN).astype(BF16)


def first_kernel(pair_ref, gate_ref, returned_ref, own_ref, grad_gate_ref, partial_ref):
    conv = conv_rows(pair_ref)
    product = (conv * gate_ref[...]).astype(BF16)
    returned = returned_ref[...]
    grad_gate = (dot(own_ref[...], returned) * conv).astype(BF16)
    grad_gate_ref[...] = dot(grad_gate, unit(), TN).astype(BF16)
    row, col = iotas(128, 128)
    grad = jnp.where(row // 64 == col // 4 % 2, dot(product, returned, NT), 0.0)
    order = ones_where(
        (row // 8 == col % 64 // 4) & (row // 4 % 2 == col // 64) & (row % 4 == col % 4)
    )
    row, col = iotas(128, 64)
    fold = ones_where(source(row) * 4 + row % 4 == col)
    partial_ref[...] = dot(order, dot(grad.astype(BF16), fold).astype(BF16))


def second_kernel(received_ref, d_out_ref, partial_ref, grads_ref, sums_ref):
    row, col = iotas(128, 128)
    grad = jnp.where(row % 4 == col // 32, dot(received_ref[...], d_out_ref[...]), 0.0)
    row, col = iotas(128, 32)
    fold = ones_where(row % 32 == col)
    pieces = [partial_ref[...]] + [dot(piece, fold) for piece in split(grad)]
    sums_ref[:, 0:1024] = grads_ref[...]
    sums_ref[:, 1024:1152] = jnp.concatenate(pieces, axis=1).astype(BF16)


def exit_kernel(
    sums_ref, signal_hbm, filter_hbm, first_hbm, second_hbm, both_ref, first_ref, second_ref, sems
):
    copies = []

    def leave(source, target):
        copies.append(pltpu.make_async_copy(source, target, sems.at[len(copies)]))
        copies[-1].start()

    square = unit()
    for field, target in enumerate((signal_hbm, filter_hbm)):
        values = sums_ref[:, 512 * field : 512 * field + 512]
        both_ref[field] = dot(values, square, TN).astype(BF16)
        leave(both_ref.at[field], target)
    wide = sums_ref[:, 1024:1152].astype(F32)
    total = wide[0:8, :]
    for p in range(1, 16):
        total = total + wide[8 * p : 8 * p + 8, :]
    second = total[:, 64:96] + total[:, 96:128]
    for i in range(2):
        first_ref[i] = total[4 * i : 4 * i + 4, 0:64]
        for k in range(4):
            second_ref[k, i : i + 1, :] = second[4 * i + k : 4 * i + k + 1, :]
    leave(first_ref, first_hbm)
    leave(second_ref, second_hbm)
    for copy in copies:
        copy.wait()


def call(body, outs, scratch=(), flops=1 << 26, moved=1 << 19, spaces=None):
    extra = {}
    if spaces is not None:
        extra["in_specs"], extra["out_specs"] = [
            [pl.BlockSpec(memory_space=space) for space in side] for side in spaces
        ]
    return pl.pallas_call(
        body,
        out_shape=[
            pltpu.VMEM(*out[:2]) if len(out) > 2 else jax.ShapeDtypeStruct(*out) for out in outs
        ],
        scratch_shapes=list(scratch),
        compiler_params=pltpu.CompilerParams(vmem_limit_bytes=32 << 20),
        cost_estimate=pl.CostEstimate(flops=flops, bytes_accessed=moved, transcendentals=0),
        **extra,
    )


def exchange(value, axis):
    rows, cols = value.shape
    pieces = value.reshape(16, rows // 16, cols)
    return lax.all_to_all(pieces, axis, split_axis=0, concat_axis=0, tiled=True).reshape(rows, cols)


def shift(value, y, zc):
    pairs = []
    for index in range(16):
        z, there, core = (index // 8 + zc // 2) % 2, (index // 2 + y) % 4, (index + zc) % 2
        pairs.append((index, z * 8 + there * 2 + core))
    return lax.ppermute(value, "ch", pairs)


def shards(signal, filter_raw, gate, d_out, w_first, w_second):
    rows, width = signal.shape
    outer, back, twiddle, inner = (jnp.asarray(t) for t in tables(lax.axis_size("seq"), rows))
    single, double = ((width, rows), BF16), ((2 * width, rows), BF16)
    slab = ((rows, width), BF16)
    quarter, half = ((width // 4, rows), BF16), ((width // 2, rows), BF16)
    held = [pltpu.with_memory_space_constraint(v, pltpu.HBM) for v in (d_out, w_second, signal, filter_raw)]
    near, core, far, pair = call(
        entry_kernel,
        [quarter + (True,), quarter + (True,), half + (True,), double],
        [
            pltpu.VMEM(d_out.shape, BF16),
            pltpu.VMEM(w_second.shape, BF16),
            pltpu.VMEM((2, rows, width), BF16),
            pltpu.VMEM((2 * width, rows), BF16),
            pltpu.SemaphoreType.DMA((5,)),
        ],
        spaces=([pl.ANY] * 4, [pltpu.VMEM] * 3 + [pl.ANY]),
    )(*held)
    far = shift(far, 0, 2)
    pair = exchange(pair, "seq")
    core = shift(call(core_kernel, [half], flops=1 << 35)(core, far)[0], 0, 1)
    near, *others = call(repack_kernel, [quarter] * 4)(near, core, far)
    pair = lax.optimization_barrier((pair, near))[0]
    others = [shift(value, y, 0) for y, value in zip((1, 2, 3), others)]
    square = ((128, 128), BF16)
    gate, blocks, own = call(prepare_kernel, [((width, rows), F32), square, square])(gate, w_first)
    conv, spectra = call(
        conv_kernel,
        [((4 * width, 128), F32), ((2, 512, 256), F32)],
        [pltpu.VMEM((2 * width * 4, 128), F32)],
        flops=1 << 30,
    )(pair, outer, back, twiddle, inner)
    pair, returned = call(gate_kernel, [double, single])(near, *others, own, gate, conv)
    pair = exchange(pair, "seq")
    grads = call(
        adjoint_kernel,
        [((width, 2 * rows), BF16)],
        [pltpu.VMEM((2 * width * 4, 128), F32), pltpu.VMEM((width * 4, 128), F32)],
        flops=1 << 30,
    )(pair, spectra, outer, back, twiddle, inner)[0]
    grad_gate, partial = call(first_kernel, [slab, ((width, 64), F32)])(
        pair, gate, returned, own
    )
    pair, grads, partial = lax.optimization_barrier((pair, grads, partial))
    mix = call(mix_kernel, [single])(pair, gate, blocks)[0]
    received = exchange(mix, "ch")
    sums = call(second_kernel, [((width, 2 * rows + 128), BF16)])(received, d_out, partial, grads)[0]
    sums = exchange(sums, "seq")
    grad_signal, grad_filter, grad_first, grad_second = call(
        exit_kernel,
        [slab, slab, ((2, 4, 64), F32), ((4, 2, 32), F32)],
        [
            pltpu.VMEM((2, rows, width), BF16),
            pltpu.VMEM((2, 4, 64), F32),
            pltpu.VMEM((4, 2, 32), F32),
            pltpu.SemaphoreType.DMA((4,)),
        ],
        spaces=([pltpu.VMEM], [pl.ANY] * 4),
    )(sums)
    return (grad_signal, grad_filter, grad_gate, grad_first, grad_second)


def solution(mesh):
    in_specs = (
        P("seq", "ch"),
        P("seq", "ch"),
        P("seq", "ch"),
        P("seq", "ch"),
        P("ch", None, None),
        P("ch", None, None),
    )
    out_specs = (
        P("seq", "ch"),
        P("seq", "ch"),
        P("seq", "ch"),
        P("ch", "seq", None),
        P("ch", "seq", None),
    )
    return jax.shard_map(shards, mesh=mesh, in_specs=in_specs, out_specs=out_specs, check_vma=False)
```

```python
import math

import jax
import jax.numpy as jnp
import numpy as np
from jax import lax
from jax.experimental import pallas as pl
from jax.experimental.pallas import tpu as pltpu
from jax.sharding import PartitionSpec as P

F32 = jnp.float32
BF16 = jnp.bfloat16
NN = (((1,), (0,)), ((), ()))
NT = (((1,), (1,)), ((), ()))
TN = (((0,), (0,)), ((), ()))


def dot(a, b, form=NN):
    return lax.dot_general(a, b, form, preferred_element_type=F32)


def halves(table):
    high = table.astype(BF16)
    return high, (table - high.astype(np.float32)).astype(BF16)


def tables(devices, rows):
    lanes = 128
    length = 2 * devices * rows
    steps = devices * rows // lanes
    split = rows // lanes
    place = (np.arange(steps) % devices) * split + np.arange(steps) // devices
    turn = 2.0 * math.pi
    freq = np.arange(steps) + 0.5
    angle = turn * freq[:, None] * place[None, :] / (2 * steps)
    outer = np.concatenate([np.cos(angle), -np.sin(angle)], 0)
    scale = float(devices * rows) ** -0.5 * 2.0 / length
    back = scale * np.concatenate([np.cos(angle.T), -np.sin(angle.T)], 1)
    angle = turn * freq[:, None] * np.arange(lanes)[None, :] / length
    twiddle = np.concatenate([np.cos(angle), -np.sin(angle)], 1)
    angle = turn * (np.arange(lanes)[:, None] * np.arange(lanes)[None, :] % lanes) / lanes
    cosine, sine = np.cos(angle), np.sin(angle)
    inner = np.concatenate(
        [np.concatenate([cosine, -sine], 1), np.concatenate([sine, cosine], 1)], 0
    )
    outer_high, outer_low = halves(outer.astype(np.float32))
    back_high, back_low = halves(back.astype(np.float32))
    inner_high, inner_low = halves(inner.astype(np.float32))
    return (
        np.concatenate([outer_high, outer_low], 1),
        np.concatenate([back_high, back_low], 0),
        twiddle.astype(np.float32),
        np.stack([inner_high, inner_low]),
    )


def iotas(rows, cols):
    return (
        lax.broadcasted_iota(jnp.int32, (rows, cols), 0),
        lax.broadcasted_iota(jnp.int32, (rows, cols), 1),
    )


def ones_where(mask):
    return jnp.where(mask, 1.0, 0.0).astype(BF16)


def pair_order():
    row, col = iotas(256, 256)
    return ones_where((row // 16 == col % 128 // 8) & (row // 8 % 2 == col // 128) & (row % 8 == col % 8))


def unit():
    row, col = iotas(128, 128)
    return ones_where(row == col)


def place():
    index = lax.axis_index("ch")
    return index // 8, index // 2 % 4, index % 2


def partner(slot_y, slot_zc, step):
    z, y, core = place()
    z = (z + slot_zc // 2) % 2
    core = (core + slot_zc) % 2
    y = (y + 4 + step * slot_y) % 4
    return z * 8 + y * 2 + core


def entry_kernel(
    d_out_hbm,
    w_second_hbm,
    signal_hbm,
    filter_hbm,
    near_ref,
    core_ref,
    far_ref,
    cross_ref,
    pair_hbm,
    d_out_ref,
    w_second_ref,
    both_ref,
    pair_ref,
    sems,
):
    copies = [
        pltpu.make_async_copy(source, target, sems.at[index])
        for index, (source, target) in enumerate(
            (
                (signal_hbm, both_ref.at[0]),
                (filter_hbm, both_ref.at[1]),
                (w_second_hbm, w_second_ref),
                (d_out_hbm, d_out_ref),
            )
        )
    ]
    for copy in copies:
        copy.start()
    pairs = pair_order()
    row, col = iotas(32, 128)
    copies_of = ones_where(row == col % 32)
    row, col = iotas(128, 128)
    keep = row // 32 == col // 32
    block = 2 * partner(row // 8 % 4, row // 32, 1) + row // 4 % 2
    order = ones_where((block == col % 32) & (row % 4 == col // 32))
    copies[0].wait()
    copies[1].wait()
    both = jnp.concatenate([both_ref[0], both_ref[1]], axis=1)
    pair_ref[...] = dot(pairs, both, NT).astype(BF16)
    leave = pltpu.make_async_copy(pair_ref, pair_hbm, sems.at[4])
    leave.start()
    copies[2].wait()
    flat = w_second_ref[...].reshape(128, 32)
    spread = jnp.where(keep, dot(flat, copies_of), 0.0).astype(BF16)
    weights = dot(order, spread).astype(BF16)
    copies[3].wait()
    result = dot(weights, d_out_ref[...], NT).astype(BF16)
    for zc, ref in enumerate((near_ref, core_ref, far_ref, cross_ref)):
        ref[...] = result[32 * zc : 32 * zc + 32, :]
    leave.wait()


def repack_kernel(*refs):
    values = [ref[...].astype(F32) for ref in refs[:4]]
    for y, ref in enumerate(refs[4:]):
        ref[...] = jnp.concatenate([v[8 * y : 8 * y + 8, :] for v in values], axis=0).astype(BF16)


def source(col):
    return partner(col // 32, col // 8 % 4, -1)


def prepare_kernel(gate_ref, w_first_ref, gate_out_ref, blocks_ref, own_ref):
    flat = w_first_ref[...].reshape(128, 64)
    row, col = iotas(64, 128)
    keep_row, keep_col = iotas(128, 128)
    keep = keep_row // 64 == keep_col // 4 % 2
    for ref, group in ((blocks_ref, col // 8), (own_ref, source(col))):
        spread = dot(flat, ones_where(row == group * 4 + col % 4))
        ref[...] = jnp.where(keep, spread, 0.0).astype(BF16)
    gate_out_ref[...] = dot(unit(), gate_ref[...], NT)


def gate_kernel(near_ref, first_ref, second_ref, third_ref, own_ref, gate_ref, conv_ref, pair_ref, returned_ref):
    pieces = [ref[...] for ref in (near_ref, first_ref, second_ref, third_ref)]
    returned = jnp.concatenate(pieces, axis=0)
    returned_ref[...] = returned
    incoming = dot(own_ref[...], returned) * gate_ref[...]
    rows = []
    for p in range(16):
        pieces = [conv_ref[128 * th + 8 * p : 128 * th + 8 * p + 8, :] for th in range(4)]
        rows.append(jnp.concatenate(pieces, axis=1))
        rows.append(incoming[8 * p : 8 * p + 8, :])
    pair_ref[...] = jnp.concatenate(rows, axis=0).astype(BF16)


def split(value):
    high = value.astype(BF16)
    return high, (value - high.astype(F32)).astype(BF16)


def by_channel(wide_ref, first, stride):
    columns = [wide_ref[pl.ds(first + c, 64, stride=stride), :] for c in range(8)]
    return jnp.concatenate(columns, axis=1).astype(BF16)


def by_slab(wide_ref, value, first, stride):
    for c in range(8):
        wide_ref[pl.ds(first + c, 64, stride=stride), :] = value[:, 128 * c : 128 * c + 128]


def unroll(wide_ref, value):
    rows = value.shape[0]
    for th in range(4):
        wide_ref[rows * th : rows * th + rows, :] = value[:, 128 * th : 128 * th + 128].astype(F32)


def enroll(wide_ref):
    rows = wide_ref.shape[0] // 4
    pieces = [wide_ref[rows * th : rows * th + rows, :].astype(BF16) for th in range(4)]
    return jnp.concatenate(pieces, axis=1)


def transform(values, outer_ref, twiddle_ref, inner_ref):
    stage = dot(outer_ref[...], jnp.concatenate([values, values], axis=0))
    cosine, sine = twiddle_ref[:, 0:128], twiddle_ref[:, 128:256]
    rows = []
    for c in range(8):
        real = stage[0:64, 128 * c : 128 * c + 128]
        imag = stage[64:128, 128 * c : 128 * c + 128]
        rows.append(
            jnp.concatenate([real * cosine - imag * sine, real * sine + imag * cosine], axis=1)
        )
    high, low = split(jnp.concatenate(rows, axis=0))
    return dot(high, inner_ref[0]) + dot(low, inner_ref[0]) + dot(high, inner_ref[1])


def restore(real, imag, back_ref, twiddle_ref, inner_ref):
    high, low = split(jnp.concatenate([real, imag], axis=1))
    stage = dot(high, inner_ref[0], NT) + dot(low, inner_ref[0], NT) + dot(high, inner_ref[1], NT)
    cosine, sine = twiddle_ref[:, 0:128], twiddle_ref[:, 128:256]
    columns = []
    for c in range(8):
        real = stage[64 * c : 64 * c + 64, 0:128]
        imag = stage[64 * c : 64 * c + 64, 128:256]
        columns.append(
            jnp.concatenate([real * cosine + imag * sine, imag * cosine - real * sine], axis=0)
        )
    high, low = split(jnp.concatenate(columns, axis=1))
    both = dot(back_ref[...], high)
    return both[0:64, :] + both[64:128, :] + dot(back_ref[0:64, :], low)


def conv_kernel(pair_ref, outer_ref, back_ref, twiddle_ref, inner_ref, conv_ref, spectra_ref, wide_ref):
    unroll(wide_ref, pair_ref[...])
    signal = transform(by_channel(wide_ref, 0, 16), outer_ref, twiddle_ref, inner_ref)
    kernel = transform(by_channel(wide_ref, 8, 16), outer_ref, twiddle_ref, inner_ref)
    spectra_ref[0] = signal
    spectra_ref[1] = kernel
    sr, si = signal[:, 0:128], signal[:, 128:256]
    kr, ki = kernel[:, 0:128], kernel[:, 128:256]
    result = restore(sr * kr - si * ki, sr * ki + si * kr, back_ref, twiddle_ref, inner_ref)
    by_slab(conv_ref, result, 0, 8)


def adjoint_kernel(
    pair_ref, spectra_ref, outer_ref, back_ref, twiddle_ref, inner_ref, grads_ref, wide_ref, out_ref
):
    unroll(wide_ref, pair_ref[...])
    spectrum = transform(by_channel(wide_ref, 8, 16), outer_ref, twiddle_ref, inner_ref)
    gr, gi = spectrum[:, 0:128], spectrum[:, 128:256]
    for field in range(2):
        real, imag = spectra_ref[1 - field, :, 0:128], spectra_ref[1 - field, :, 128:256]
        result = restore(
            gr * real + gi * imag, gi * real - gr * imag, back_ref, twiddle_ref, inner_ref
        )
        by_slab(out_ref, result, 0, 8)
        grads_ref[:, 512 * field : 512 * field + 512] = enroll(out_ref)


def conv_rows(pair_ref):
    wide = pair_ref[...].astype(F32)
    return jnp.concatenate([wide[16 * p : 16 * p + 8, :] for p in range(16)], axis=0)


def mix_kernel(pair_ref, gate_ref, blocks_ref, mix_ref):
    product = (conv_rows(pair_ref) * gate_ref[...]).astype(BF16)
    mix_ref[...] = dot(blocks_ref[...], product, TN).astype(BF16)


def first_kernel(pair_ref, gate_ref, returned_ref, own_ref, grad_gate_ref, partial_ref):
    conv = conv_rows(pair_ref)
    product = (conv * gate_ref[...]).astype(BF16)
    returned = returned_ref[...]
    grad_gate = (dot(own_ref[...], returned) * conv).astype(BF16)
    grad_gate_ref[...] = dot(grad_gate, unit(), TN).astype(BF16)
    row, col = iotas(128, 128)
    grad = jnp.where(row // 64 == col // 4 % 2, dot(product, returned, NT), 0.0)
    order = ones_where(
        (row // 8 == col % 64 // 4) & (row // 4 % 2 == col // 64) & (row % 4 == col % 4)
    )
    row, col = iotas(128, 64)
    fold = ones_where(source(row) * 4 + row % 4 == col)
    partial_ref[...] = dot(order, dot(grad.astype(BF16), fold).astype(BF16))


def second_kernel(received_ref, d_out_ref, partial_ref, grads_ref, sums_ref):
    row, col = iotas(128, 128)
    grad = jnp.where(row % 4 == col // 32, dot(received_ref[...], d_out_ref[...]), 0.0)
    row, col = iotas(128, 32)
    fold = ones_where(row % 32 == col)
    pieces = [partial_ref[...]] + [dot(piece, fold) for piece in split(grad)]
    sums_ref[:, 0:1024] = grads_ref[...]
    sums_ref[:, 1024:1152] = jnp.concatenate(pieces, axis=1).astype(BF16)


def exit_kernel(
    sums_ref, signal_hbm, filter_hbm, first_hbm, second_hbm, both_ref, first_ref, second_ref, sems
):
    copies = []

    def leave(source, target):
        copies.append(pltpu.make_async_copy(source, target, sems.at[len(copies)]))
        copies[-1].start()

    square = unit()
    for field, target in enumerate((signal_hbm, filter_hbm)):
        values = sums_ref[:, 512 * field : 512 * field + 512]
        both_ref[field] = dot(values, square, TN).astype(BF16)
        leave(both_ref.at[field], target)
    wide = sums_ref[:, 1024:1152].astype(F32)
    total = wide[0:8, :]
    for p in range(1, 16):
        total = total + wide[8 * p : 8 * p + 8, :]
    second = total[:, 64:96] + total[:, 96:128]
    for i in range(2):
        first_ref[i] = total[4 * i : 4 * i + 4, 0:64]
        for k in range(4):
            second_ref[k, i : i + 1, :] = second[4 * i + k : 4 * i + k + 1, :]
    leave(first_ref, first_hbm)
    leave(second_ref, second_hbm)
    for copy in copies:
        copy.wait()


def call(body, outs, scratch=(), flops=1 << 26, moved=1 << 19, spaces=None):
    extra = {}
    if spaces is not None:
        extra["in_specs"], extra["out_specs"] = [
            [pl.BlockSpec(memory_space=space) for space in side] for side in spaces
        ]
    return pl.pallas_call(
        body,
        out_shape=[
            pltpu.VMEM(*out[:2]) if len(out) > 2 else jax.ShapeDtypeStruct(*out) for out in outs
        ],
        scratch_shapes=list(scratch),
        compiler_params=pltpu.CompilerParams(vmem_limit_bytes=32 << 20),
        cost_estimate=pl.CostEstimate(flops=flops, bytes_accessed=moved, transcendentals=0),
        **extra,
    )


def exchange(value, axis):
    rows, cols = value.shape
    pieces = value.reshape(16, rows // 16, cols)
    return lax.all_to_all(pieces, axis, split_axis=0, concat_axis=0, tiled=True).reshape(rows, cols)


def shift(value, y, zc):
    pairs = []
    for index in range(16):
        z, there, core = (index // 8 + zc // 2) % 2, (index // 2 + y) % 4, (index + zc) % 2
        pairs.append((index, z * 8 + there * 2 + core))
    return lax.ppermute(value, "ch", pairs)


def shards(signal, filter_raw, gate, d_out, w_first, w_second):
    rows, width = signal.shape
    outer, back, twiddle, inner = (jnp.asarray(t) for t in tables(lax.axis_size("seq"), rows))
    single, double = ((width, rows), BF16), ((2 * width, rows), BF16)
    slab = ((rows, width), BF16)
    quarter = ((width // 4, rows), BF16)
    held = [pltpu.with_memory_space_constraint(v, pltpu.HBM) for v in (d_out, w_second, signal, filter_raw)]
    near, *others, pair = call(
        entry_kernel,
        [quarter + (True,)] * 4 + [double],
        [
            pltpu.VMEM(d_out.shape, BF16),
            pltpu.VMEM(w_second.shape, BF16),
            pltpu.VMEM((2, rows, width), BF16),
            pltpu.VMEM((2 * width, rows), BF16),
            pltpu.SemaphoreType.DMA((5,)),
        ],
        spaces=([pl.ANY] * 4, [pltpu.VMEM] * 4 + [pl.ANY]),
    )(*held)
    others = [shift(value, 0, zc) for zc, value in zip((1, 2, 3), others)]
    pair = exchange(pair, "seq")
    near, *others = call(repack_kernel, [quarter] * 4, flops=1 << 35)(near, *others)
    pair = lax.optimization_barrier((pair, near))[0]
    others = [shift(value, y, 0) for y, value in zip((1, 2, 3), others)]
    square = ((128, 128), BF16)
    gate, blocks, own = call(prepare_kernel, [((width, rows), F32), square, square])(gate, w_first)
    conv, spectra = call(
        conv_kernel,
        [((4 * width, 128), F32), ((2, 512, 256), F32)],
        [pltpu.VMEM((2 * width * 4, 128), F32)],
        flops=1 << 30,
    )(pair, outer, back, twiddle, inner)
    pair, returned = call(gate_kernel, [double, single])(near, *others, own, gate, conv)
    pair = exchange(pair, "seq")
    mix = call(mix_kernel, [single])(pair, gate, blocks)[0]
    received = exchange(mix, "ch")
    grads = call(
        adjoint_kernel,
        [((width, 2 * rows), BF16)],
        [pltpu.VMEM((2 * width * 4, 128), F32), pltpu.VMEM((width * 4, 128), F32)],
        flops=1 << 30,
    )(pair, spectra, outer, back, twiddle, inner)[0]
    grad_gate, partial = call(first_kernel, [slab, ((width, 64), F32)])(
        pair, gate, returned, own
    )
    sums = call(second_kernel, [((width, 2 * rows + 128), BF16)])(received, d_out, partial, grads)[0]
    sums = exchange(sums, "seq")
    grad_signal, grad_filter, grad_first, grad_second = call(
        exit_kernel,
        [slab, slab, ((2, 4, 64), F32), ((4, 2, 32), F32)],
        [
            pltpu.VMEM((2, rows, width), BF16),
            pltpu.VMEM((2, 4, 64), F32),
            pltpu.VMEM((4, 2, 32), F32),
            pltpu.SemaphoreType.DMA((4,)),
        ],
        spaces=([pltpu.VMEM], [pl.ANY] * 4),
    )(sums)
    return (grad_signal, grad_filter, grad_gate, grad_first, grad_second)


def solution(mesh):
    in_specs = (
        P("seq", "ch"),
        P("seq", "ch"),
        P("seq", "ch"),
        P("seq", "ch"),
        P("ch", None, None),
        P("ch", None, None),
    )
    out_specs = (
        P("seq", "ch"),
        P("seq", "ch"),
        P("seq", "ch"),
        P("ch", "seq", None),
        P("ch", "seq", None),
    )
    return jax.shard_map(shards, mesh=mesh, in_specs=in_specs, out_specs=out_specs, check_vma=False)
```

```python
import math

import jax
import jax.numpy as jnp
import numpy as np
from jax import lax
from jax.experimental import pallas as pl
from jax.experimental.pallas import tpu as pltpu
from jax.sharding import PartitionSpec as P

F32 = jnp.float32
BF16 = jnp.bfloat16
NN = (((1,), (0,)), ((), ()))
NT = (((1,), (1,)), ((), ()))
TN = (((0,), (0,)), ((), ()))


def dot(a, b, form=NN):
    return lax.dot_general(a, b, form, preferred_element_type=F32)


def halves(table):
    high = table.astype(BF16)
    return high, (table - high.astype(np.float32)).astype(BF16)


def tables(devices, rows):
    lanes = 128
    length = 2 * devices * rows
    steps = devices * rows // lanes
    split = rows // lanes
    place = (np.arange(steps) % devices) * split + np.arange(steps) // devices
    turn = 2.0 * math.pi
    freq = np.arange(steps) + 0.5
    angle = turn * freq[:, None] * place[None, :] / (2 * steps)
    outer = np.concatenate([np.cos(angle), -np.sin(angle)], 0)
    scale = float(devices * rows) ** -0.5 * 2.0 / length
    back = scale * np.concatenate([np.cos(angle.T), -np.sin(angle.T)], 1)
    angle = turn * freq[:, None] * np.arange(lanes)[None, :] / length
    twiddle = np.concatenate([np.cos(angle), -np.sin(angle)], 1)
    angle = turn * (np.arange(lanes)[:, None] * np.arange(lanes)[None, :] % lanes) / lanes
    cosine, sine = np.cos(angle), np.sin(angle)
    inner = np.concatenate(
        [np.concatenate([cosine, -sine], 1), np.concatenate([sine, cosine], 1)], 0
    )
    outer_high, outer_low = halves(outer.astype(np.float32))
    back_high, back_low = halves(back.astype(np.float32))
    inner_high, inner_low = halves(inner.astype(np.float32))
    return (
        np.concatenate([outer_high, outer_low], 1),
        np.concatenate([back_high, back_low], 0),
        twiddle.astype(np.float32),
        np.stack([inner_high, inner_low]),
    )


def iotas(rows, cols):
    return (
        lax.broadcasted_iota(jnp.int32, (rows, cols), 0),
        lax.broadcasted_iota(jnp.int32, (rows, cols), 1),
    )


def ones_where(mask):
    return jnp.where(mask, 1.0, 0.0).astype(BF16)


def pair_order():
    row, col = iotas(256, 256)
    return ones_where((row // 16 == col % 128 // 8) & (row // 8 % 2 == col // 128) & (row % 8 == col % 8))


def unit():
    row, col = iotas(128, 128)
    return ones_where(row == col)


def place():
    index = lax.axis_index("ch")
    return index // 8, index // 2 % 4, index % 2


def partner(slot_y, slot_zc, step):
    z, y, core = place()
    z = (z + slot_zc // 2) % 2
    core = (core + slot_zc) % 2
    y = (y + 4 + step * slot_y) % 4
    return z * 8 + y * 2 + core


def entry_kernel(
    d_out_hbm,
    w_second_hbm,
    signal_hbm,
    filter_hbm,
    near_ref,
    far_ref,
    core_ref,
    signal_ref,
    filter_ref,
    d_out_ref,
    w_second_ref,
    sems,
):
    copies = [
        pltpu.make_async_copy(source, target, sems.at[index])
        for index, (source, target) in enumerate(
            (
                (w_second_hbm, w_second_ref),
                (d_out_hbm, d_out_ref),
                (signal_hbm, signal_ref),
                (filter_hbm, filter_ref),
            )
        )
    ]
    for copy in copies:
        copy.start()
    row, col = iotas(32, 128)
    copies_of = ones_where(row == col % 32)
    row, col = iotas(128, 128)
    keep = row // 32 == col // 32
    block = 2 * partner(row // 8 % 4, row // 32, 1) + row // 4 % 2
    order = ones_where((block == col % 32) & (row % 4 == col // 32))
    copies[0].wait()
    flat = w_second_ref[...].reshape(128, 32)
    spread = jnp.where(keep, dot(flat, copies_of), 0.0).astype(BF16)
    weights = dot(order, spread).astype(BF16)
    copies[1].wait()
    result = dot(weights, d_out_ref[...], NT).astype(BF16)
    near_ref[...] = result[0:32, :]
    far_ref[...] = result[64:96, :]
    core_ref[0:32, :] = result[32:64, :]
    core_ref[32:64, :] = result[96:128, :]
    copies[2].wait()
    copies[3].wait()


def pair_kernel(signal_ref, filter_ref, pair_ref):
    both = jnp.concatenate([signal_ref[...], filter_ref[...]], axis=1)
    pair_ref[...] = dot(pair_order(), both, NT).astype(BF16)


def far_kernel(far_ref, core_ref, message_ref):
    message_ref[0:32, :] = far_ref[...]
    message_ref[32:64, :] = core_ref[32:64, :]


def repack_kernel(near_ref, core_ref, far_ref, *outs):
    near, core, far = (ref[...].astype(F32) for ref in (near_ref, core_ref, far_ref))
    values = (near, core[0:32, :], far[0:32, :], far[32:64, :])
    for y, ref in enumerate(outs):
        ref[...] = jnp.concatenate([v[8 * y : 8 * y + 8, :] for v in values], axis=0).astype(BF16)


def source(col):
    return partner(col // 32, col // 8 % 4, -1)


def prepare_kernel(gate_ref, w_first_ref, gate_out_ref, blocks_ref, own_ref):
    flat = w_first_ref[...].reshape(128, 64)
    row, col = iotas(64, 128)
    keep_row, keep_col = iotas(128, 128)
    keep = keep_row // 64 == keep_col // 4 % 2
    for ref, group in ((blocks_ref, col // 8), (own_ref, source(col))):
        spread = dot(flat, ones_where(row == group * 4 + col % 4))
        ref[...] = jnp.where(keep, spread, 0.0).astype(BF16)
    gate_out_ref[...] = dot(unit(), gate_ref[...], NT)


def gate_kernel(near_ref, first_ref, second_ref, third_ref, own_ref, gate_ref, conv_ref, pair_ref, returned_ref):
    pieces = [ref[...] for ref in (near_ref, first_ref, second_ref, third_ref)]
    returned = jnp.concatenate(pieces, axis=0)
    returned_ref[...] = returned
    incoming = dot(own_ref[...], returned) * gate_ref[...]
    rows = []
    for p in range(16):
        pieces = [conv_ref[128 * th + 8 * p : 128 * th + 8 * p + 8, :] for th in range(4)]
        rows.append(jnp.concatenate(pieces, axis=1))
        rows.append(incoming[8 * p : 8 * p + 8, :])
    pair_ref[...] = jnp.concatenate(rows, axis=0).astype(BF16)


def split(value):
    high = value.astype(BF16)
    return high, (value - high.astype(F32)).astype(BF16)


def by_channel(wide_ref, first, stride):
    columns = [wide_ref[pl.ds(first + c, 64, stride=stride), :] for c in range(8)]
    return jnp.concatenate(columns, axis=1).astype(BF16)


def by_slab(wide_ref, value, first, stride):
    for c in range(8):
        wide_ref[pl.ds(first + c, 64, stride=stride), :] = value[:, 128 * c : 128 * c + 128]


def unroll(wide_ref, value):
    rows = value.shape[0]
    for th in range(4):
        wide_ref[rows * th : rows * th + rows, :] = value[:, 128 * th : 128 * th + 128].astype(F32)


def enroll(wide_ref):
    rows = wide_ref.shape[0] // 4
    pieces = [wide_ref[rows * th : rows * th + rows, :].astype(BF16) for th in range(4)]
    return jnp.concatenate(pieces, axis=1)


def transform(values, outer_ref, twiddle_ref, inner_ref):
    stage = dot(outer_ref[...], jnp.concatenate([values, values], axis=0))
    cosine, sine = twiddle_ref[:, 0:128], twiddle_ref[:, 128:256]
    rows = []
    for c in range(8):
        real = stage[0:64, 128 * c : 128 * c + 128]
        imag = stage[64:128, 128 * c : 128 * c + 128]
        rows.append(
            jnp.concatenate([real * cosine - imag * sine, real * sine + imag * cosine], axis=1)
        )
    high, low = split(jnp.concatenate(rows, axis=0))
    return dot(high, inner_ref[0]) + dot(low, inner_ref[0]) + dot(high, inner_ref[1])


def restore(real, imag, back_ref, twiddle_ref, inner_ref):
    high, low = split(jnp.concatenate([real, imag], axis=1))
    stage = dot(high, inner_ref[0], NT) + dot(low, inner_ref[0], NT) + dot(high, inner_ref[1], NT)
    cosine, sine = twiddle_ref[:, 0:128], twiddle_ref[:, 128:256]
    columns = []
    for c in range(8):
        real = stage[64 * c : 64 * c + 64, 0:128]
        imag = stage[64 * c : 64 * c + 64, 128:256]
        columns.append(
            jnp.concatenate([real * cosine + imag * sine, imag * cosine - real * sine], axis=0)
        )
    high, low = split(jnp.concatenate(columns, axis=1))
    both = dot(back_ref[...], high)
    return both[0:64, :] + both[64:128, :] + dot(back_ref[0:64, :], low)


def conv_kernel(pair_ref, outer_ref, back_ref, twiddle_ref, inner_ref, conv_ref, spectra_ref, wide_ref):
    unroll(wide_ref, pair_ref[...])
    signal = transform(by_channel(wide_ref, 0, 16), outer_ref, twiddle_ref, inner_ref)
    kernel = transform(by_channel(wide_ref, 8, 16), outer_ref, twiddle_ref, inner_ref)
    spectra_ref[0] = signal
    spectra_ref[1] = kernel
    sr, si = signal[:, 0:128], signal[:, 128:256]
    kr, ki = kernel[:, 0:128], kernel[:, 128:256]
    result = restore(sr * kr - si * ki, sr * ki + si * kr, back_ref, twiddle_ref, inner_ref)
    by_slab(conv_ref, result, 0, 8)


def adjoint_kernel(
    pair_ref, spectra_ref, outer_ref, back_ref, twiddle_ref, inner_ref, grads_ref, wide_ref, out_ref
):
    unroll(wide_ref, pair_ref[...])
    spectrum = transform(by_channel(wide_ref, 8, 16), outer_ref, twiddle_ref, inner_ref)
    gr, gi = spectrum[:, 0:128], spectrum[:, 128:256]
    for field in range(2):
        real, imag = spectra_ref[1 - field, :, 0:128], spectra_ref[1 - field, :, 128:256]
        result = restore(
            gr * real + gi * imag, gi * real - gr * imag, back_ref, twiddle_ref, inner_ref
        )
        by_slab(out_ref, result, 0, 8)
        grads_ref[:, 512 * field : 512 * field + 512] = enroll(out_ref)


def conv_rows(pair_ref):
    wide = pair_ref[...].astype(F32)
    return jnp.concatenate([wide[16 * p : 16 * p + 8, :] for p in range(16)], axis=0)


def mix_kernel(pair_ref, gate_ref, blocks_ref, mix_ref):
    product = (conv_rows(pair_ref) * gate_ref[...]).astype(BF16)
    mix_ref[...] = dot(blocks_ref[...], product, TN).astype(BF16)


def first_kernel(pair_ref, gate_ref, returned_ref, own_ref, grad_gate_ref, partial_ref):
    conv = conv_rows(pair_ref)
    product = (conv * gate_ref[...]).astype(BF16)
    returned = returned_ref[...]
    grad_gate = (dot(own_ref[...], returned) * conv).astype(BF16)
    grad_gate_ref[...] = dot(grad_gate, unit(), TN).astype(BF16)
    row, col = iotas(128, 128)
    grad = jnp.where(row // 64 == col // 4 % 2, dot(product, returned, NT), 0.0)
    order = ones_where(
        (row // 8 == col % 64 // 4) & (row // 4 % 2 == col // 64) & (row % 4 == col % 4)
    )
    row, col = iotas(128, 64)
    fold = ones_where(source(row) * 4 + row % 4 == col)
    partial_ref[...] = dot(order, dot(grad.astype(BF16), fold).astype(BF16))


def second_kernel(received_ref, d_out_ref, partial_ref, grads_ref, sums_ref):
    row, col = iotas(128, 128)
    grad = jnp.where(row % 4 == col // 32, dot(received_ref[...], d_out_ref[...]), 0.0)
    row, col = iotas(128, 32)
    fold = ones_where(row % 32 == col)
    pieces = [partial_ref[...]] + [dot(piece, fold) for piece in split(grad)]
    sums_ref[:, 0:1024] = grads_ref[...]
    sums_ref[:, 1024:1152] = jnp.concatenate(pieces, axis=1).astype(BF16)


def exit_kernel(
    sums_ref, signal_hbm, filter_hbm, first_hbm, second_hbm, both_ref, first_ref, second_ref, sems
):
    copies = []

    def leave(source, target):
        copies.append(pltpu.make_async_copy(source, target, sems.at[len(copies)]))
        copies[-1].start()

    square = unit()
    for field, target in enumerate((signal_hbm, filter_hbm)):
        values = sums_ref[:, 512 * field : 512 * field + 512]
        both_ref[field] = dot(values, square, TN).astype(BF16)
        leave(both_ref.at[field], target)
    wide = sums_ref[:, 1024:1152].astype(F32)
    total = wide[0:8, :]
    for p in range(1, 16):
        total = total + wide[8 * p : 8 * p + 8, :]
    second = total[:, 64:96] + total[:, 96:128]
    for i in range(2):
        first_ref[i] = total[4 * i : 4 * i + 4, 0:64]
        for k in range(4):
            second_ref[k, i : i + 1, :] = second[4 * i + k : 4 * i + k + 1, :]
    leave(first_ref, first_hbm)
    leave(second_ref, second_hbm)
    for copy in copies:
        copy.wait()


def call(body, outs, scratch=(), flops=1 << 26, moved=1 << 19, spaces=None):
    extra = {}
    if spaces is not None:
        extra["in_specs"], extra["out_specs"] = [
            [pl.BlockSpec(memory_space=space) for space in side] for side in spaces
        ]
    return pl.pallas_call(
        body,
        out_shape=[
            pltpu.VMEM(*out[:2]) if len(out) > 2 else jax.ShapeDtypeStruct(*out) for out in outs
        ],
        scratch_shapes=list(scratch),
        compiler_params=pltpu.CompilerParams(vmem_limit_bytes=32 << 20),
        cost_estimate=pl.CostEstimate(flops=flops, bytes_accessed=moved, transcendentals=0),
        **extra,
    )


def exchange(value, axis):
    rows, cols = value.shape
    pieces = value.reshape(16, rows // 16, cols)
    return lax.all_to_all(pieces, axis, split_axis=0, concat_axis=0, tiled=True).reshape(rows, cols)


def shift(value, y, zc):
    pairs = []
    for index in range(16):
        z, there, core = (index // 8 + zc // 2) % 2, (index // 2 + y) % 4, (index + zc) % 2
        pairs.append((index, z * 8 + there * 2 + core))
    return lax.ppermute(value, "ch", pairs)


def shards(signal, filter_raw, gate, d_out, w_first, w_second):
    rows, width = signal.shape
    outer, back, twiddle, inner = (jnp.asarray(t) for t in tables(lax.axis_size("seq"), rows))
    single, double = ((width, rows), BF16), ((2 * width, rows), BF16)
    slab = ((rows, width), BF16)
    quarter, half = ((width // 4, rows), BF16), ((width // 2, rows), BF16)
    held = [pltpu.with_memory_space_constraint(v, pltpu.HBM) for v in (d_out, w_second, signal, filter_raw)]
    near, far, core, signal, filter_raw = call(
        entry_kernel,
        [
            quarter + (True,),
            quarter + (True,),
            half + (True,),
            slab + (True,),
            slab + (True,),
        ],
        [
            pltpu.VMEM(d_out.shape, BF16),
            pltpu.VMEM(w_second.shape, BF16),
            pltpu.SemaphoreType.DMA((4,)),
        ],
        spaces=([pl.ANY] * 4, [pltpu.VMEM] * 5),
    )(*held)
    core = shift(core, 0, 1)
    pair = call(pair_kernel, [double])(signal, filter_raw)[0]
    far = call(far_kernel, [half])(far, core)[0]
    pair, far = lax.optimization_barrier((pair, far))
    far = shift(far, 0, 2)
    gate, w_first, far = lax.optimization_barrier((gate, w_first, far))
    pair = exchange(pair, "seq")
    near, *others = call(repack_kernel, [quarter] * 4, flops=1 << 35)(near, core, far)
    pair = lax.optimization_barrier((pair, near))[0]
    others = [shift(value, y, 0) for y, value in zip((1, 2, 3), others)]
    square = ((128, 128), BF16)
    gate, blocks, own = call(prepare_kernel, [((width, rows), F32), square, square])(gate, w_first)
    conv, spectra = call(
        conv_kernel,
        [((4 * width, 128), F32), ((2, 512, 256), F32)],
        [pltpu.VMEM((2 * width * 4, 128), F32)],
        flops=1 << 30,
    )(pair, outer, back, twiddle, inner)
    pair, returned = call(gate_kernel, [double, single])(near, *others, own, gate, conv)
    pair = exchange(pair, "seq")
    mix = call(mix_kernel, [single])(pair, gate, blocks)[0]
    received = exchange(mix, "ch")
    grads = call(
        adjoint_kernel,
        [((width, 2 * rows), BF16)],
        [pltpu.VMEM((2 * width * 4, 128), F32), pltpu.VMEM((width * 4, 128), F32)],
        flops=1 << 30,
    )(pair, spectra, outer, back, twiddle, inner)[0]
    grad_gate, partial = call(first_kernel, [slab, ((width, 64), F32)])(
        pair, gate, returned, own
    )
    sums = call(second_kernel, [((width, 2 * rows + 128), BF16)])(received, d_out, partial, grads)[0]
    sums = exchange(sums, "seq")
    grad_signal, grad_filter, grad_first, grad_second = call(
        exit_kernel,
        [slab, slab, ((2, 4, 64), F32), ((4, 2, 32), F32)],
        [
            pltpu.VMEM((2, rows, width), BF16),
            pltpu.VMEM((2, 4, 64), F32),
            pltpu.VMEM((4, 2, 32), F32),
            pltpu.SemaphoreType.DMA((4,)),
        ],
        spaces=([pltpu.VMEM], [pl.ANY] * 4),
    )(sums)
    return (grad_signal, grad_filter, grad_gate, grad_first, grad_second)


def solution(mesh):
    in_specs = (
        P("seq", "ch"),
        P("seq", "ch"),
        P("seq", "ch"),
        P("seq", "ch"),
        P("ch", None, None),
        P("ch", None, None),
    )
    out_specs = (
        P("seq", "ch"),
        P("seq", "ch"),
        P("seq", "ch"),
        P("ch", "seq", None),
        P("ch", "seq", None),
    )
    return jax.shard_map(shards, mesh=mesh, in_specs=in_specs, out_specs=out_specs, check_vma=False)
```

```python
import math

import jax
import jax.numpy as jnp
import numpy as np
from jax import lax
from jax.experimental import pallas as pl
from jax.experimental.pallas import tpu as pltpu
from jax.sharding import PartitionSpec as P

F32 = jnp.float32
BF16 = jnp.bfloat16
NN = (((1,), (0,)), ((), ()))
NT = (((1,), (1,)), ((), ()))
TN = (((0,), (0,)), ((), ()))


def dot(a, b, form=NN):
    return lax.dot_general(a, b, form, preferred_element_type=F32)


def halves(table):
    high = table.astype(BF16)
    return high, (table - high.astype(np.float32)).astype(BF16)


def tables(devices, rows):
    lanes = 128
    length = 2 * devices * rows
    steps = devices * rows // lanes
    split = rows // lanes
    place = (np.arange(steps) % devices) * split + np.arange(steps) // devices
    turn = 2.0 * math.pi
    freq = np.arange(steps) + 0.5
    angle = turn * freq[:, None] * place[None, :] / (2 * steps)
    outer = np.concatenate([np.cos(angle), -np.sin(angle)], 0)
    scale = float(devices * rows) ** -0.5 * 2.0 / length
    back = scale * np.concatenate([np.cos(angle.T), -np.sin(angle.T)], 1)
    angle = turn * freq[:, None] * np.arange(lanes)[None, :] / length
    twiddle = np.concatenate([np.cos(angle), -np.sin(angle)], 1)
    angle = turn * (np.arange(lanes)[:, None] * np.arange(lanes)[None, :] % lanes) / lanes
    cosine, sine = np.cos(angle), np.sin(angle)
    inner = np.concatenate(
        [np.concatenate([cosine, -sine], 1), np.concatenate([sine, cosine], 1)], 0
    )
    outer_high, outer_low = halves(outer.astype(np.float32))
    back_high, back_low = halves(back.astype(np.float32))
    inner_high, inner_low = halves(inner.astype(np.float32))
    return (
        np.concatenate([outer_high, outer_low], 1),
        np.concatenate([back_high, back_low], 0),
        twiddle.astype(np.float32),
        np.stack([inner_high, inner_low]),
    )


def iotas(rows, cols):
    return (
        lax.broadcasted_iota(jnp.int32, (rows, cols), 0),
        lax.broadcasted_iota(jnp.int32, (rows, cols), 1),
    )


def ones_where(mask):
    return jnp.where(mask, 1.0, 0.0).astype(BF16)


def pair_order():
    row, col = iotas(256, 256)
    return ones_where((row // 16 == col % 128 // 8) & (row // 8 % 2 == col // 128) & (row % 8 == col % 8))


def unit():
    row, col = iotas(128, 128)
    return ones_where(row == col)


def place():
    index = lax.axis_index("ch")
    return index // 8, index // 2 % 4, index % 2


def partner(slot_y, slot_zc, step):
    z, y, core = place()
    z = (z + slot_zc // 2) % 2
    core = (core + slot_zc) % 2
    y = (y + 4 + step * slot_y) % 4
    return z * 8 + y * 2 + core


def entry_kernel(
    d_out_hbm,
    w_second_hbm,
    signal_hbm,
    filter_hbm,
    near_ref,
    far_ref,
    pair_hbm,
    d_out_ref,
    w_second_ref,
    both_ref,
    pair_ref,
    sems,
):
    copies = [
        pltpu.make_async_copy(source, target, sems.at[index])
        for index, (source, target) in enumerate(
            (
                (signal_hbm, both_ref.at[0]),
                (filter_hbm, both_ref.at[1]),
                (w_second_hbm, w_second_ref),
                (d_out_hbm, d_out_ref),
            )
        )
    ]
    for copy in copies:
        copy.start()
    pairs = pair_order()
    row, col = iotas(32, 128)
    copies_of = ones_where(row == col % 32)
    row, col = iotas(128, 128)
    keep = row // 32 == col // 32
    block = 2 * partner(row // 16 % 4, row // 64 * 2 + row // 8 % 2, 1) + row // 4 % 2
    order = ones_where((block == col % 32) & (row % 4 == col // 32))
    copies[0].wait()
    copies[1].wait()
    both = jnp.concatenate([both_ref[0], both_ref[1]], axis=1)
    pair_ref[...] = dot(pairs, both, NT).astype(BF16)
    leave = pltpu.make_async_copy(pair_ref, pair_hbm, sems.at[4])
    leave.start()
    copies[2].wait()
    flat = w_second_ref[...].reshape(128, 32)
    spread = jnp.where(keep, dot(flat, copies_of), 0.0).astype(BF16)
    weights = dot(order, spread).astype(BF16)
    copies[3].wait()
    result = dot(weights, d_out_ref[...], NT).astype(BF16)
    near_ref[...] = result[0:64, :]
    far_ref[...] = result[64:128, :]
    leave.wait()


def y_kernel(near_ref, far_ref, *outs):
    for y, ref in enumerate(outs):
        ref[0:16, :] = near_ref[16 * y : 16 * y + 16, :]
        ref[16:32, :] = far_ref[16 * y : 16 * y + 16, :]


def core_kernel(*refs):
    values = [ref[...].astype(F32) for ref in refs[:4]]
    for core, ref in enumerate(refs[4:]):
        pieces = [v[16 * z + 8 * core : 16 * z + 8 * core + 8, :] for v in values for z in range(2)]
        ref[...] = jnp.concatenate(pieces, axis=0).astype(BF16)


def source(col):
    return partner(col // 16 % 4, col // 8 % 2 * 2 + col // 64, -1)


def prepare_kernel(gate_ref, w_first_ref, gate_out_ref, blocks_ref, own_ref):
    flat = w_first_ref[...].reshape(128, 64)
    row, col = iotas(64, 128)
    keep_row, keep_col = iotas(128, 128)
    keep = keep_row // 64 == keep_col // 4 % 2
    for ref, group in ((blocks_ref, col // 8), (own_ref, source(col))):
        spread = dot(flat, ones_where(row == group * 4 + col % 4))
        ref[...] = jnp.where(keep, spread, 0.0).astype(BF16)
    gate_out_ref[...] = dot(unit(), gate_ref[...], NT)


def gate_kernel(near_ref, core_ref, own_ref, gate_ref, conv_ref, pair_ref, returned_ref):
    returned = jnp.concatenate([near_ref[...], core_ref[...]], axis=0)
    returned_ref[...] = returned
    incoming = dot(own_ref[...], returned) * gate_ref[...]
    rows = []
    for p in range(16):
        pieces = [conv_ref[128 * th + 8 * p : 128 * th + 8 * p + 8, :] for th in range(4)]
        rows.append(jnp.concatenate(pieces, axis=1))
        rows.append(incoming[8 * p : 8 * p + 8, :])
    pair_ref[...] = jnp.concatenate(rows, axis=0).astype(BF16)


def split(value):
    high = value.astype(BF16)
    return high, (value - high.astype(F32)).astype(BF16)


def by_channel(wide_ref, first, stride):
    columns = [wide_ref[pl.ds(first + c, 64, stride=stride), :] for c in range(8)]
    return jnp.concatenate(columns, axis=1).astype(BF16)


def by_slab(wide_ref, value, first, stride):
    for c in range(8):
        wide_ref[pl.ds(first + c, 64, stride=stride), :] = value[:, 128 * c : 128 * c + 128]


def unroll(wide_ref, value):
    rows = value.shape[0]
    for th in range(4):
        wide_ref[rows * th : rows * th + rows, :] = value[:, 128 * th : 128 * th + 128].astype(F32)


def enroll(wide_ref):
    rows = wide_ref.shape[0] // 4
    pieces = [wide_ref[rows * th : rows * th + rows, :].astype(BF16) for th in range(4)]
    return jnp.concatenate(pieces, axis=1)


def transform(values, outer_ref, twiddle_ref, inner_ref):
    stage = dot(outer_ref[...], jnp.concatenate([values, values], axis=0))
    cosine, sine = twiddle_ref[:, 0:128], twiddle_ref[:, 128:256]
    rows = []
    for c in range(8):
        real = stage[0:64, 128 * c : 128 * c + 128]
        imag = stage[64:128, 128 * c : 128 * c + 128]
        rows.append(
            jnp.concatenate([real * cosine - imag * sine, real * sine + imag * cosine], axis=1)
        )
    high, low = split(jnp.concatenate(rows, axis=0))
    return dot(high, inner_ref[0]) + dot(low, inner_ref[0]) + dot(high, inner_ref[1])


def restore(real, imag, back_ref, twiddle_ref, inner_ref):
    high, low = split(jnp.concatenate([real, imag], axis=1))
    stage = dot(high, inner_ref[0], NT) + dot(low, inner_ref[0], NT) + dot(high, inner_ref[1], NT)
    cosine, sine = twiddle_ref[:, 0:128], twiddle_ref[:, 128:256]
    columns = []
    for c in range(8):
        real = stage[64 * c : 64 * c + 64, 0:128]
        imag = stage[64 * c : 64 * c + 64, 128:256]
        columns.append(
            jnp.concatenate([real * cosine + imag * sine, imag * cosine - real * sine], axis=0)
        )
    high, low = split(jnp.concatenate(columns, axis=1))
    both = dot(back_ref[...], high)
    return both[0:64, :] + both[64:128, :] + dot(back_ref[0:64, :], low)


def conv_kernel(pair_ref, outer_ref, back_ref, twiddle_ref, inner_ref, conv_ref, spectra_ref, wide_ref):
    unroll(wide_ref, pair_ref[...])
    signal = transform(by_channel(wide_ref, 0, 16), outer_ref, twiddle_ref, inner_ref)
    kernel = transform(by_channel(wide_ref, 8, 16), outer_ref, twiddle_ref, inner_ref)
    spectra_ref[0] = signal
    spectra_ref[1] = kernel
    sr, si = signal[:, 0:128], signal[:, 128:256]
    kr, ki = kernel[:, 0:128], kernel[:, 128:256]
    result = restore(sr * kr - si * ki, sr * ki + si * kr, back_ref, twiddle_ref, inner_ref)
    by_slab(conv_ref, result, 0, 8)


def adjoint_kernel(
    pair_ref, spectra_ref, outer_ref, back_ref, twiddle_ref, inner_ref, grads_ref, wide_ref, out_ref
):
    unroll(wide_ref, pair_ref[...])
    spectrum = transform(by_channel(wide_ref, 8, 16), outer_ref, twiddle_ref, inner_ref)
    gr, gi = spectrum[:, 0:128], spectrum[:, 128:256]
    for field in range(2):
        real, imag = spectra_ref[1 - field, :, 0:128], spectra_ref[1 - field, :, 128:256]
        result = restore(
            gr * real + gi * imag, gi * real - gr * imag, back_ref, twiddle_ref, inner_ref
        )
        by_slab(out_ref, result, 0, 8)
        grads_ref[:, 512 * field : 512 * field + 512] = enroll(out_ref)


def conv_rows(pair_ref):
    wide = pair_ref[...].astype(F32)
    return jnp.concatenate([wide[16 * p : 16 * p + 8, :] for p in range(16)], axis=0)


def mix_kernel(pair_ref, gate_ref, blocks_ref, mix_ref):
    product = (conv_rows(pair_ref) * gate_ref[...]).astype(BF16)
    mix_ref[...] = dot(blocks_ref[...], product, TN).astype(BF16)


def first_kernel(pair_ref, gate_ref, returned_ref, own_ref, grad_gate_ref, partial_ref):
    conv = conv_rows(pair_ref)
    product = (conv * gate_ref[...]).astype(BF16)
    returned = returned_ref[...]
    grad_gate = (dot(own_ref[...], returned) * conv).astype(BF16)
    grad_gate_ref[...] = dot(grad_gate, unit(), TN).astype(BF16)
    row, col = iotas(128, 128)
    grad = jnp.where(row // 64 == col // 4 % 2, dot(product, returned, NT), 0.0)
    order = ones_where(
        (row // 8 == col % 64 // 4) & (row // 4 % 2 == col // 64) & (row % 4 == col % 4)
    )
    row, col = iotas(128, 64)
    fold = ones_where(source(row) * 4 + row % 4 == col)
    partial_ref[...] = dot(order, dot(grad.astype(BF16), fold).astype(BF16))


def second_kernel(received_ref, d_out_ref, partial_ref, grads_ref, sums_ref):
    row, col = iotas(128, 128)
    grad = jnp.where(row % 4 == col // 32, dot(received_ref[...], d_out_ref[...]), 0.0)
    row, col = iotas(128, 32)
    fold = ones_where(row % 32 == col)
    pieces = [partial_ref[...]] + [dot(piece, fold) for piece in split(grad)]
    sums_ref[:, 0:1024] = grads_ref[...]
    sums_ref[:, 1024:1152] = jnp.concatenate(pieces, axis=1).astype(BF16)


def exit_kernel(
    sums_ref, signal_hbm, filter_hbm, first_hbm, second_hbm, both_ref, first_ref, second_ref, sems
):
    copies = []

    def leave(source, target):
        copies.append(pltpu.make_async_copy(source, target, sems.at[len(copies)]))
        copies[-1].start()

    square = unit()
    for field, target in enumerate((signal_hbm, filter_hbm)):
        values = sums_ref[:, 512 * field : 512 * field + 512]
        both_ref[field] = dot(values, square, TN).astype(BF16)
        leave(both_ref.at[field], target)
    wide = sums_ref[:, 1024:1152].astype(F32)
    total = wide[0:8, :]
    for p in range(1, 16):
        total = total + wide[8 * p : 8 * p + 8, :]
    second = total[:, 64:96] + total[:, 96:128]
    for i in range(2):
        first_ref[i] = total[4 * i : 4 * i + 4, 0:64]
        for k in range(4):
            second_ref[k, i : i + 1, :] = second[4 * i + k : 4 * i + k + 1, :]
    leave(first_ref, first_hbm)
    leave(second_ref, second_hbm)
    for copy in copies:
        copy.wait()


def call(body, outs, scratch=(), flops=1 << 26, moved=1 << 19, spaces=None):
    extra = {}
    if spaces is not None:
        extra["in_specs"], extra["out_specs"] = [
            [pl.BlockSpec(memory_space=space) for space in side] for side in spaces
        ]
    return pl.pallas_call(
        body,
        out_shape=[
            pltpu.VMEM(*out[:2]) if len(out) > 2 else jax.ShapeDtypeStruct(*out) for out in outs
        ],
        scratch_shapes=list(scratch),
        compiler_params=pltpu.CompilerParams(vmem_limit_bytes=32 << 20),
        cost_estimate=pl.CostEstimate(flops=flops, bytes_accessed=moved, transcendentals=0),
        **extra,
    )


def exchange(value, axis):
    rows, cols = value.shape
    pieces = value.reshape(16, rows // 16, cols)
    return lax.all_to_all(pieces, axis, split_axis=0, concat_axis=0, tiled=True).reshape(rows, cols)


def shift(value, y, zc):
    pairs = []
    for index in range(16):
        z, there, core = (index // 8 + zc // 2) % 2, (index // 2 + y) % 4, (index + zc) % 2
        pairs.append((index, z * 8 + there * 2 + core))
    return lax.ppermute(value, "ch", pairs)


def shards(signal, filter_raw, gate, d_out, w_first, w_second):
    rows, width = signal.shape
    outer, back, twiddle, inner = (jnp.asarray(t) for t in tables(lax.axis_size("seq"), rows))
    single, double = ((width, rows), BF16), ((2 * width, rows), BF16)
    slab = ((rows, width), BF16)
    quarter, half = ((width // 4, rows), BF16), ((width // 2, rows), BF16)
    held = [pltpu.with_memory_space_constraint(v, pltpu.HBM) for v in (d_out, w_second, signal, filter_raw)]
    near, far, pair = call(
        entry_kernel,
        [half + (True,), half + (True,), double],
        [
            pltpu.VMEM(d_out.shape, BF16),
            pltpu.VMEM(w_second.shape, BF16),
            pltpu.VMEM((2, rows, width), BF16),
            pltpu.VMEM((2 * width, rows), BF16),
            pltpu.SemaphoreType.DMA((5,)),
        ],
        spaces=([pl.ANY] * 4, [pltpu.VMEM] * 2 + [pl.ANY]),
    )(*held)
    far = shift(far, 0, 2)
    pair = exchange(pair, "seq")
    own, *others = call(y_kernel, [quarter] * 4, flops=1 << 35)(near, far)
    others = [shift(value, y, 0) for y, value in zip((1, 2, 3), others)]
    near, core = call(core_kernel, [half] * 2)(own, *others)
    pair = lax.optimization_barrier((pair, near))[0]
    core = shift(core, 0, 1)
    square = ((128, 128), BF16)
    gate, blocks, own = call(prepare_kernel, [((width, rows), F32), square, square])(gate, w_first)
    conv, spectra = call(
        conv_kernel,
        [((4 * width, 128), F32), ((2, 512, 256), F32)],
        [pltpu.VMEM((2 * width * 4, 128), F32)],
        flops=1 << 30,
    )(pair, outer, back, twiddle, inner)
    pair, returned = call(gate_kernel, [double, single])(near, core, own, gate, conv)
    pair = exchange(pair, "seq")
    mix = call(mix_kernel, [single])(pair, gate, blocks)[0]
    received = exchange(mix, "ch")
    grads = call(
        adjoint_kernel,
        [((width, 2 * rows), BF16)],
        [pltpu.VMEM((2 * width * 4, 128), F32), pltpu.VMEM((width * 4, 128), F32)],
        flops=1 << 30,
    )(pair, spectra, outer, back, twiddle, inner)[0]
    grad_gate, partial = call(first_kernel, [slab, ((width, 64), F32)])(
        pair, gate, returned, own
    )
    sums = call(second_kernel, [((width, 2 * rows + 128), BF16)])(received, d_out, partial, grads)[0]
    sums = exchange(sums, "seq")
    grad_signal, grad_filter, grad_first, grad_second = call(
        exit_kernel,
        [slab, slab, ((2, 4, 64), F32), ((4, 2, 32), F32)],
        [
            pltpu.VMEM((2, rows, width), BF16),
            pltpu.VMEM((2, 4, 64), F32),
            pltpu.VMEM((4, 2, 32), F32),
            pltpu.SemaphoreType.DMA((4,)),
        ],
        spaces=([pltpu.VMEM], [pl.ANY] * 4),
    )(sums)
    return (grad_signal, grad_filter, grad_gate, grad_first, grad_second)


def solution(mesh):
    in_specs = (
        P("seq", "ch"),
        P("seq", "ch"),
        P("seq", "ch"),
        P("seq", "ch"),
        P("ch", None, None),
        P("ch", None, None),
    )
    out_specs = (
        P("seq", "ch"),
        P("seq", "ch"),
        P("seq", "ch"),
        P("ch", "seq", None),
        P("ch", "seq", None),
    )
    return jax.shard_map(shards, mesh=mesh, in_specs=in_specs, out_specs=out_specs, check_vma=False)
```

```python
import math

import jax
import jax.numpy as jnp
import numpy as np
from jax import lax
from jax.experimental import pallas as pl
from jax.experimental.pallas import tpu as pltpu
from jax.sharding import PartitionSpec as P

F32 = jnp.float32
BF16 = jnp.bfloat16
NN = (((1,), (0,)), ((), ()))
NT = (((1,), (1,)), ((), ()))
TN = (((0,), (0,)), ((), ()))


def dot(a, b, form=NN):
    return lax.dot_general(a, b, form, preferred_element_type=F32)


def halves(table):
    high = table.astype(BF16)
    return high, (table - high.astype(np.float32)).astype(BF16)


def tables(devices, rows):
    lanes = 128
    length = 2 * devices * rows
    steps = devices * rows // lanes
    split = rows // lanes
    place = (np.arange(steps) % devices) * split + np.arange(steps) // devices
    turn = 2.0 * math.pi
    freq = np.arange(steps) + 0.5
    angle = turn * freq[:, None] * place[None, :] / (2 * steps)
    outer = np.concatenate([np.cos(angle), -np.sin(angle)], 0)
    scale = float(devices * rows) ** -0.5 * 2.0 / length
    back = scale * np.concatenate([np.cos(angle.T), -np.sin(angle.T)], 1)
    angle = turn * freq[:, None] * np.arange(lanes)[None, :] / length
    twiddle = np.concatenate([np.cos(angle), -np.sin(angle)], 1)
    angle = turn * (np.arange(lanes)[:, None] * np.arange(lanes)[None, :] % lanes) / lanes
    cosine, sine = np.cos(angle), np.sin(angle)
    inner = np.concatenate(
        [np.concatenate([cosine, -sine], 1), np.concatenate([sine, cosine], 1)], 0
    )
    outer_high, outer_low = halves(outer.astype(np.float32))
    back_high, back_low = halves(back.astype(np.float32))
    inner_high, inner_low = halves(inner.astype(np.float32))
    return (
        np.concatenate([outer_high, outer_low], 1),
        np.concatenate([back_high, back_low], 0),
        twiddle.astype(np.float32),
        np.stack([inner_high, inner_low]),
    )


def iotas(rows, cols):
    return (
        lax.broadcasted_iota(jnp.int32, (rows, cols), 0),
        lax.broadcasted_iota(jnp.int32, (rows, cols), 1),
    )


def ones_where(mask):
    return jnp.where(mask, 1.0, 0.0).astype(BF16)


def pair_order():
    row, col = iotas(256, 256)
    return ones_where((row // 16 == col % 128 // 8) & (row // 8 % 2 == col // 128) & (row % 8 == col % 8))


def unit():
    row, col = iotas(128, 128)
    return ones_where(row == col)


def place():
    index = lax.axis_index("ch")
    return index // 8, index // 2 % 4, index % 2


def partner(slot_y, slot_zc, step):
    z, y, core = place()
    z = (z + slot_zc // 2) % 2
    core = (core + slot_zc) % 2
    y = (y + 4 + step * slot_y) % 4
    return z * 8 + y * 2 + core


def entry_kernel(
    d_out_hbm,
    w_second_hbm,
    signal_hbm,
    filter_hbm,
    near_ref,
    core_ref,
    far_ref,
    pair_hbm,
    d_out_ref,
    w_second_ref,
    both_ref,
    pair_ref,
    sems,
):
    copies = [
        pltpu.make_async_copy(source, target, sems.at[index])
        for index, (source, target) in enumerate(
            (
                (signal_hbm, both_ref.at[0]),
                (filter_hbm, both_ref.at[1]),
                (w_second_hbm, w_second_ref),
                (d_out_hbm, d_out_ref),
            )
        )
    ]
    for copy in copies:
        copy.start()
    pairs = pair_order()
    row, col = iotas(32, 128)
    copies_of = ones_where(row == col % 32)
    row, col = iotas(128, 128)
    keep = row // 32 == col // 32
    block = 2 * partner(row // 8 % 4, row // 32, 1) + row // 4 % 2
    order = ones_where((block == col % 32) & (row % 4 == col // 32))
    copies[0].wait()
    copies[1].wait()
    both = jnp.concatenate([both_ref[0], both_ref[1]], axis=1)
    leaving = []
    for part in range(2):
        place_of = pl.ds(128 * part, 128)
        pair_ref[place_of, :] = dot(pairs[128 * part : 128 * part + 128, :], both, NT).astype(BF16)
        leaving.append(
            pltpu.make_async_copy(pair_ref.at[place_of], pair_hbm.at[place_of], sems.at[4 + part])
        )
        leaving[-1].start()
    copies[2].wait()
    flat = w_second_ref[...].reshape(128, 32)
    spread = jnp.where(keep, dot(flat, copies_of), 0.0).astype(BF16)
    weights = dot(order, spread).astype(BF16)
    copies[3].wait()
    result = dot(weights, d_out_ref[...], NT).astype(BF16)
    for ref, start in zip((near_ref, core_ref, far_ref), (0, 32, 64)):
        ref[...] = result[start : start + ref.shape[0], :]
    for copy in leaving:
        copy.wait()


def core_kernel(core_ref, far_ref, message_ref):
    message_ref[0:32, :] = core_ref[...]
    message_ref[32:64, :] = far_ref[32:64, :]


def repack_kernel(near_ref, core_ref, far_ref, *outs):
    near, core, far = (ref[...].astype(F32) for ref in (near_ref, core_ref, far_ref))
    values = (near, core[0:32, :], far[0:32, :], core[32:64, :])
    for y, ref in enumerate(outs):
        ref[...] = jnp.concatenate([v[8 * y : 8 * y + 8, :] for v in values], axis=0).astype(BF16)


def source(col):
    return partner(col // 32, col // 8 % 4, -1)


def prepare_kernel(gate_ref, w_first_ref, gate_out_ref, blocks_ref, own_ref):
    flat = w_first_ref[...].reshape(128, 64)
    row, col = iotas(64, 128)
    keep_row, keep_col = iotas(128, 128)
    keep = keep_row // 64 == keep_col // 4 % 2
    for ref, group in ((blocks_ref, col // 8), (own_ref, source(col))):
        spread = dot(flat, ones_where(row == group * 4 + col % 4))
        ref[...] = jnp.where(keep, spread, 0.0).astype(BF16)
    gate_out_ref[...] = dot(unit(), gate_ref[...], NT)


def gate_kernel(near_ref, first_ref, second_ref, third_ref, own_ref, gate_ref, conv_ref, pair_ref, returned_ref):
    pieces = [ref[...] for ref in (near_ref, first_ref, second_ref, third_ref)]
    returned = jnp.concatenate(pieces, axis=0)
    returned_ref[...] = returned
    incoming = dot(own_ref[...], returned) * gate_ref[...]
    rows = []
    for p in range(16):
        pieces = [conv_ref[128 * th + 8 * p : 128 * th + 8 * p + 8, :] for th in range(4)]
        rows.append(jnp.concatenate(pieces, axis=1))
        rows.append(incoming[8 * p : 8 * p + 8, :])
    pair_ref[...] = jnp.concatenate(rows, axis=0).astype(BF16)


def split(value):
    high = value.astype(BF16)
    return high, (value - high.astype(F32)).astype(BF16)


def by_channel(wide_ref, first, stride):
    columns = [wide_ref[pl.ds(first + c, 64, stride=stride), :] for c in range(8)]
    return jnp.concatenate(columns, axis=1).astype(BF16)


def by_slab(wide_ref, value, first, stride):
    for c in range(8):
        wide_ref[pl.ds(first + c, 64, stride=stride), :] = value[:, 128 * c : 128 * c + 128]


def unroll(wide_ref, value):
    rows = value.shape[0]
    for th in range(4):
        wide_ref[rows * th : rows * th + rows, :] = value[:, 128 * th : 128 * th + 128].astype(F32)


def enroll(wide_ref):
    rows = wide_ref.shape[0] // 4
    pieces = [wide_ref[rows * th : rows * th + rows, :].astype(BF16) for th in range(4)]
    return jnp.concatenate(pieces, axis=1)


def transform(values, outer_ref, twiddle_ref, inner_ref):
    stage = dot(outer_ref[...], jnp.concatenate([values, values], axis=0))
    cosine, sine = twiddle_ref[:, 0:128], twiddle_ref[:, 128:256]
    rows = []
    for c in range(8):
        real = stage[0:64, 128 * c : 128 * c + 128]
        imag = stage[64:128, 128 * c : 128 * c + 128]
        rows.append(
            jnp.concatenate([real * cosine - imag * sine, real * sine + imag * cosine], axis=1)
        )
    high, low = split(jnp.concatenate(rows, axis=0))
    return dot(high, inner_ref[0]) + dot(low, inner_ref[0]) + dot(high, inner_ref[1])


def restore(real, imag, back_ref, twiddle_ref, inner_ref):
    high, low = split(jnp.concatenate([real, imag], axis=1))
    stage = dot(high, inner_ref[0], NT) + dot(low, inner_ref[0], NT) + dot(high, inner_ref[1], NT)
    cosine, sine = twiddle_ref[:, 0:128], twiddle_ref[:, 128:256]
    columns = []
    for c in range(8):
        real = stage[64 * c : 64 * c + 64, 0:128]
        imag = stage[64 * c : 64 * c + 64, 128:256]
        columns.append(
            jnp.concatenate([real * cosine + imag * sine, imag * cosine - real * sine], axis=0)
        )
    high, low = split(jnp.concatenate(columns, axis=1))
    both = dot(back_ref[...], high)
    return both[0:64, :] + both[64:128, :] + dot(back_ref[0:64, :], low)


def conv_kernel(pair_ref, outer_ref, back_ref, twiddle_ref, inner_ref, conv_ref, spectra_ref, wide_ref):
    unroll(wide_ref, pair_ref[...])
    signal = transform(by_channel(wide_ref, 0, 16), outer_ref, twiddle_ref, inner_ref)
    kernel = transform(by_channel(wide_ref, 8, 16), outer_ref, twiddle_ref, inner_ref)
    spectra_ref[0] = signal
    spectra_ref[1] = kernel
    sr, si = signal[:, 0:128], signal[:, 128:256]
    kr, ki = kernel[:, 0:128], kernel[:, 128:256]
    result = restore(sr * kr - si * ki, sr * ki + si * kr, back_ref, twiddle_ref, inner_ref)
    by_slab(conv_ref, result, 0, 8)


def adjoint_kernel(
    pair_ref, spectra_ref, outer_ref, back_ref, twiddle_ref, inner_ref, grads_ref, wide_ref, out_ref
):
    unroll(wide_ref, pair_ref[...])
    spectrum = transform(by_channel(wide_ref, 8, 16), outer_ref, twiddle_ref, inner_ref)
    gr, gi = spectrum[:, 0:128], spectrum[:, 128:256]
    for field in range(2):
        real, imag = spectra_ref[1 - field, :, 0:128], spectra_ref[1 - field, :, 128:256]
        result = restore(
            gr * real + gi * imag, gi * real - gr * imag, back_ref, twiddle_ref, inner_ref
        )
        by_slab(out_ref, result, 0, 8)
        grads_ref[:, 512 * field : 512 * field + 512] = enroll(out_ref)


def conv_rows(pair_ref):
    wide = pair_ref[...].astype(F32)
    return jnp.concatenate([wide[16 * p : 16 * p + 8, :] for p in range(16)], axis=0)


def mix_kernel(pair_ref, gate_ref, blocks_ref, mix_hbm, mix_ref, sems):
    product = (conv_rows(pair_ref) * gate_ref[...]).astype(BF16)
    leaving = []
    for part in range(2):
        place_of = pl.ds(256 * part, 256)
        values = product[:, 256 * part : 256 * part + 256]
        mix_ref[:, place_of] = dot(blocks_ref[...], values, TN).astype(BF16)
        leaving.append(
            pltpu.make_async_copy(mix_ref.at[:, place_of], mix_hbm.at[:, place_of], sems.at[part])
        )
        leaving[-1].start()
    for copy in leaving:
        copy.wait()


def first_kernel(pair_ref, gate_ref, returned_ref, own_ref, grad_gate_ref, partial_ref):
    conv = conv_rows(pair_ref)
    product = (conv * gate_ref[...]).astype(BF16)
    returned = returned_ref[...]
    grad_gate = (dot(own_ref[...], returned) * conv).astype(BF16)
    grad_gate_ref[...] = dot(grad_gate, unit(), TN).astype(BF16)
    row, col = iotas(128, 128)
    grad = jnp.where(row // 64 == col // 4 % 2, dot(product, returned, NT), 0.0)
    order = ones_where(
        (row // 8 == col % 64 // 4) & (row // 4 % 2 == col // 64) & (row % 4 == col % 4)
    )
    row, col = iotas(128, 64)
    fold = ones_where(source(row) * 4 + row % 4 == col)
    partial_ref[...] = dot(order, dot(grad.astype(BF16), fold).astype(BF16))


def second_kernel(received_ref, d_out_ref, partial_ref, grads_ref, sums_ref):
    row, col = iotas(128, 128)
    grad = jnp.where(row % 4 == col // 32, dot(received_ref[...], d_out_ref[...]), 0.0)
    row, col = iotas(128, 32)
    fold = ones_where(row % 32 == col)
    pieces = [partial_ref[...]] + [dot(piece, fold) for piece in split(grad)]
    sums_ref[:, 0:1024] = grads_ref[...]
    sums_ref[:, 1024:1152] = jnp.concatenate(pieces, axis=1).astype(BF16)


def exit_kernel(
    sums_ref, signal_hbm, filter_hbm, first_hbm, second_hbm, both_ref, first_ref, second_ref, sems
):
    copies = []

    def leave(source, target):
        copies.append(pltpu.make_async_copy(source, target, sems.at[len(copies)]))
        copies[-1].start()

    square = unit()
    for field, target in enumerate((signal_hbm, filter_hbm)):
        values = sums_ref[:, 512 * field : 512 * field + 512]
        both_ref[field] = dot(values, square, TN).astype(BF16)
        leave(both_ref.at[field], target)
    wide = sums_ref[:, 1024:1152].astype(F32)
    total = wide[0:8, :]
    for p in range(1, 16):
        total = total + wide[8 * p : 8 * p + 8, :]
    second = total[:, 64:96] + total[:, 96:128]
    for i in range(2):
        first_ref[i] = total[4 * i : 4 * i + 4, 0:64]
        for k in range(4):
            second_ref[k, i : i + 1, :] = second[4 * i + k : 4 * i + k + 1, :]
    leave(first_ref, first_hbm)
    leave(second_ref, second_hbm)
    for copy in copies:
        copy.wait()


def call(body, outs, scratch=(), flops=1 << 26, moved=1 << 19, spaces=None):
    extra = {}
    if spaces is not None:
        extra["in_specs"], extra["out_specs"] = [
            [pl.BlockSpec(memory_space=space) for space in side] for side in spaces
        ]
    return pl.pallas_call(
        body,
        out_shape=[
            pltpu.VMEM(*out[:2]) if len(out) > 2 else jax.ShapeDtypeStruct(*out) for out in outs
        ],
        scratch_shapes=list(scratch),
        compiler_params=pltpu.CompilerParams(vmem_limit_bytes=32 << 20),
        cost_estimate=pl.CostEstimate(flops=flops, bytes_accessed=moved, transcendentals=0),
        **extra,
    )


def exchange(value, axis):
    rows, cols = value.shape
    pieces = value.reshape(16, rows // 16, cols)
    return lax.all_to_all(pieces, axis, split_axis=0, concat_axis=0, tiled=True).reshape(rows, cols)


def shift(value, y, zc):
    pairs = []
    for index in range(16):
        z, there, core = (index // 8 + zc // 2) % 2, (index // 2 + y) % 4, (index + zc) % 2
        pairs.append((index, z * 8 + there * 2 + core))
    return lax.ppermute(value, "ch", pairs)


def shards(signal, filter_raw, gate, d_out, w_first, w_second):
    rows, width = signal.shape
    outer, back, twiddle, inner = (jnp.asarray(t) for t in tables(lax.axis_size("seq"), rows))
    single, double = ((width, rows), BF16), ((2 * width, rows), BF16)
    slab = ((rows, width), BF16)
    quarter, half = ((width // 4, rows), BF16), ((width // 2, rows), BF16)
    held = [pltpu.with_memory_space_constraint(v, pltpu.HBM) for v in (d_out, w_second, signal, filter_raw)]
    near, core, far, pair = call(
        entry_kernel,
        [quarter + (True,), quarter + (True,), half + (True,), double],
        [
            pltpu.VMEM(d_out.shape, BF16),
            pltpu.VMEM(w_second.shape, BF16),
            pltpu.VMEM((2, rows, width), BF16),
            pltpu.VMEM((2 * width, rows), BF16),
            pltpu.SemaphoreType.DMA((6,)),
        ],
        spaces=([pl.ANY] * 4, [pltpu.VMEM] * 3 + [pl.ANY]),
    )(*held)
    far = shift(far, 0, 2)
    pair = exchange(pair, "seq")
    core = shift(call(core_kernel, [half], flops=1 << 35)(core, far)[0], 0, 1)
    near, *others = call(repack_kernel, [quarter] * 4)(near, core, far)
    pair = lax.optimization_barrier((pair, near))[0]
    others = [shift(value, y, 0) for y, value in zip((1, 2, 3), others)]
    square = ((128, 128), BF16)
    gate, blocks, own = call(prepare_kernel, [((width, rows), F32), square, square])(gate, w_first)
    conv, spectra = call(
        conv_kernel,
        [((4 * width, 128), F32), ((2, 512, 256), F32)],
        [pltpu.VMEM((2 * width * 4, 128), F32)],
        flops=1 << 30,
    )(pair, outer, back, twiddle, inner)
    pair, returned = call(gate_kernel, [double, single])(near, *others, own, gate, conv)
    pair = exchange(pair, "seq")
    mix = call(
        mix_kernel,
        [single],
        [pltpu.VMEM((width, rows), BF16), pltpu.SemaphoreType.DMA((2,))],
        spaces=([pltpu.VMEM] * 3, [pl.ANY]),
    )(pair, gate, blocks)[0]
    received = exchange(mix, "ch")
    grads = call(
        adjoint_kernel,
        [((width, 2 * rows), BF16)],
        [pltpu.VMEM((2 * width * 4, 128), F32), pltpu.VMEM((width * 4, 128), F32)],
        flops=1 << 30,
    )(pair, spectra, outer, back, twiddle, inner)[0]
    grad_gate, partial = call(first_kernel, [slab, ((width, 64), F32)])(
        pair, gate, returned, own
    )
    sums = call(second_kernel, [((width, 2 * rows + 128), BF16)])(received, d_out, partial, grads)[0]
    sums = exchange(sums, "seq")
    grad_signal, grad_filter, grad_first, grad_second = call(
        exit_kernel,
        [slab, slab, ((2, 4, 64), F32), ((4, 2, 32), F32)],
        [
            pltpu.VMEM((2, rows, width), BF16),
            pltpu.VMEM((2, 4, 64), F32),
            pltpu.VMEM((4, 2, 32), F32),
            pltpu.SemaphoreType.DMA((4,)),
        ],
        spaces=([pltpu.VMEM], [pl.ANY] * 4),
    )(sums)
    return (grad_signal, grad_filter, grad_gate, grad_first, grad_second)


def solution(mesh):
    in_specs = (
        P("seq", "ch"),
        P("seq", "ch"),
        P("seq", "ch"),
        P("seq", "ch"),
        P("ch", None, None),
        P("ch", None, None),
    )
    out_specs = (
        P("seq", "ch"),
        P("seq", "ch"),
        P("seq", "ch"),
        P("ch", "seq", None),
        P("ch", "seq", None),
    )
    return jax.shard_map(shards, mesh=mesh, in_specs=in_specs, out_specs=out_specs, check_vma=False)
```

```python
import math

import jax
import jax.numpy as jnp
import numpy as np
from jax import lax
from jax.experimental import pallas as pl
from jax.experimental.pallas import tpu as pltpu
from jax.sharding import PartitionSpec as P

F32 = jnp.float32
BF16 = jnp.bfloat16
NN = (((1,), (0,)), ((), ()))
NT = (((1,), (1,)), ((), ()))
TN = (((0,), (0,)), ((), ()))


def dot(a, b, form=NN):
    return lax.dot_general(a, b, form, preferred_element_type=F32)


def halves(table):
    high = table.astype(BF16)
    return high, (table - high.astype(np.float32)).astype(BF16)


def tables(devices, rows):
    lanes = 128
    length = 2 * devices * rows
    steps = devices * rows // lanes
    split = rows // lanes
    place = (np.arange(steps) % devices) * split + np.arange(steps) // devices
    turn = 2.0 * math.pi
    freq = np.arange(steps) + 0.5
    angle = turn * freq[:, None] * place[None, :] / (2 * steps)
    outer = np.concatenate([np.cos(angle), -np.sin(angle)], 0)
    scale = float(devices * rows) ** -0.5 * 2.0 / length
    back = scale * np.concatenate([np.cos(angle.T), -np.sin(angle.T)], 1)
    angle = turn * freq[:, None] * np.arange(lanes)[None, :] / length
    twiddle = np.concatenate([np.cos(angle), -np.sin(angle)], 1)
    angle = turn * (np.arange(lanes)[:, None] * np.arange(lanes)[None, :] % lanes) / lanes
    cosine, sine = np.cos(angle), np.sin(angle)
    inner = np.concatenate(
        [np.concatenate([cosine, -sine], 1), np.concatenate([sine, cosine], 1)], 0
    )
    outer_high, outer_low = halves(outer.astype(np.float32))
    back_high, back_low = halves(back.astype(np.float32))
    inner_high, inner_low = halves(inner.astype(np.float32))
    return (
        np.concatenate([outer_high, outer_low], 1),
        np.stack([back_high, back_low]),
        twiddle.astype(np.float32),
        np.stack([inner_high, inner_low]),
    )


def iotas(rows, cols):
    return (
        lax.broadcasted_iota(jnp.int32, (rows, cols), 0),
        lax.broadcasted_iota(jnp.int32, (rows, cols), 1),
    )


def ones_where(mask):
    return jnp.where(mask, 1.0, 0.0).astype(BF16)


def pair_order():
    row, col = iotas(256, 256)
    return ones_where((row // 16 == col % 128 // 8) & (row // 8 % 2 == col // 128) & (row % 8 == col % 8))


def unit():
    row, col = iotas(128, 128)
    return ones_where(row == col)


def place():
    index = lax.axis_index("ch")
    return index // 8, index // 2 % 4, index % 2


def partner(slot_y, slot_zc, step):
    z, y, core = place()
    z = (z + slot_zc // 2) % 2
    core = (core + slot_zc) % 2
    y = (y + 4 + step * slot_y) % 4
    return z * 8 + y * 2 + core


def entry_kernel(
    d_out_hbm,
    w_second_hbm,
    signal_hbm,
    filter_hbm,
    near_ref,
    core_ref,
    far_ref,
    pair_hbm,
    d_out_ref,
    w_second_ref,
    both_ref,
    pair_ref,
    sems,
):
    copies = [
        pltpu.make_async_copy(source, target, sems.at[index])
        for index, (source, target) in enumerate(
            (
                (signal_hbm, both_ref.at[0]),
                (filter_hbm, both_ref.at[1]),
                (w_second_hbm, w_second_ref),
                (d_out_hbm, d_out_ref),
            )
        )
    ]
    for copy in copies:
        copy.start()
    pairs = pair_order()
    row, col = iotas(32, 128)
    copies_of = ones_where(row == col % 32)
    row, col = iotas(128, 128)
    keep = row // 32 == col // 32
    block = 2 * partner(row // 8 % 4, row // 32, 1) + row // 4 % 2
    order = ones_where((block == col % 32) & (row % 4 == col // 32))
    copies[0].wait()
    copies[1].wait()
    both = jnp.concatenate([both_ref[0], both_ref[1]], axis=1)
    pair_ref[...] = dot(pairs, both, NT).astype(BF16)
    leave = pltpu.make_async_copy(pair_ref, pair_hbm, sems.at[4])
    leave.start()
    copies[2].wait()
    flat = w_second_ref[...].reshape(128, 32)
    spread = jnp.where(keep, dot(flat, copies_of), 0.0).astype(BF16)
    weights = dot(order, spread).astype(BF16)
    copies[3].wait()
    result = dot(weights, d_out_ref[...], NT).astype(BF16)
    for ref, start in zip((near_ref, core_ref, far_ref), (0, 32, 64)):
        ref[...] = result[start : start + ref.shape[0], :]
    leave.wait()


def core_kernel(core_ref, far_ref, message_ref):
    message_ref[0:32, :] = core_ref[...]
    message_ref[32:64, :] = far_ref[32:64, :]


def repack_kernel(near_ref, core_ref, far_ref, *outs):
    near, core, far = (ref[...].astype(F32) for ref in (near_ref, core_ref, far_ref))
    values = (near, core[0:32, :], far[0:32, :], core[32:64, :])
    for y, ref in enumerate(outs):
        ref[...] = jnp.concatenate([v[8 * y : 8 * y + 8, :] for v in values], axis=0).astype(BF16)


def source(col):
    return partner(col // 32, col // 8 % 4, -1)


def prepare_kernel(gate_ref, w_first_ref, gate_out_ref, blocks_ref, own_ref):
    flat = w_first_ref[...].reshape(128, 64)
    row, col = iotas(64, 128)
    keep_row, keep_col = iotas(128, 128)
    keep = keep_row // 64 == keep_col // 4 % 2
    for ref, group in ((blocks_ref, col // 8), (own_ref, source(col))):
        spread = dot(flat, ones_where(row == group * 4 + col % 4))
        ref[...] = jnp.where(keep, spread, 0.0).astype(BF16)
    gate_out_ref[...] = dot(unit(), gate_ref[...], NT)


def gate_kernel(near_ref, first_ref, second_ref, third_ref, own_ref, gate_ref, conv_ref, pair_ref, returned_ref):
    pieces = [ref[...] for ref in (near_ref, first_ref, second_ref, third_ref)]
    returned = jnp.concatenate(pieces, axis=0)
    returned_ref[...] = returned
    incoming = dot(own_ref[...], returned) * gate_ref[...]
    rows = []
    for p in range(16):
        pieces = [conv_ref[128 * th + 8 * p : 128 * th + 8 * p + 8, :] for th in range(4)]
        rows.append(jnp.concatenate(pieces, axis=1))
        rows.append(incoming[8 * p : 8 * p + 8, :])
    pair_ref[...] = jnp.concatenate(rows, axis=0).astype(BF16)


def split(value):
    high = value.astype(BF16)
    return high, (value - high.astype(F32)).astype(BF16)


def by_channel(wide_ref, first, stride):
    columns = [wide_ref[pl.ds(first + c, 64, stride=stride), :] for c in range(8)]
    return jnp.concatenate(columns, axis=1).astype(BF16)


def by_slab(wide_ref, value, first, stride):
    for c in range(8):
        wide_ref[pl.ds(first + c, 64, stride=stride), :] = value[:, 128 * c : 128 * c + 128]


def unroll(wide_ref, value):
    rows = value.shape[0]
    for th in range(4):
        wide_ref[rows * th : rows * th + rows, :] = value[:, 128 * th : 128 * th + 128].astype(F32)


def enroll(wide_ref):
    rows = wide_ref.shape[0] // 4
    pieces = [wide_ref[rows * th : rows * th + rows, :].astype(BF16) for th in range(4)]
    return jnp.concatenate(pieces, axis=1)


def transform(values, outer_ref, twiddle_ref, inner_ref):
    stage = dot(outer_ref[...], jnp.concatenate([values, values], axis=0))
    cosine, sine = twiddle_ref[:, 0:128], twiddle_ref[:, 128:256]
    rows = []
    for c in range(8):
        real = stage[0:64, 128 * c : 128 * c + 128]
        imag = stage[64:128, 128 * c : 128 * c + 128]
        rows.append(
            jnp.concatenate([real * cosine - imag * sine, real * sine + imag * cosine], axis=1)
        )
    high, low = split(jnp.concatenate(rows, axis=0))
    return dot(high, inner_ref[0]) + dot(low, inner_ref[0]) + dot(high, inner_ref[1])


def restore(real, imag, back_ref, twiddle_ref, inner_ref):
    high, low = split(jnp.concatenate([real, imag], axis=1))
    stage = dot(high, inner_ref[0], NT) + dot(low, inner_ref[0], NT) + dot(high, inner_ref[1], NT)
    cosine, sine = twiddle_ref[:, 0:128], twiddle_ref[:, 128:256]
    columns = []
    for c in range(8):
        real = stage[64 * c : 64 * c + 64, 0:128]
        imag = stage[64 * c : 64 * c + 64, 128:256]
        columns.append(
            jnp.concatenate([real * cosine + imag * sine, imag * cosine - real * sine], axis=0)
        )
    high, low = split(jnp.concatenate(columns, axis=1))
    return dot(back_ref[0], high) + dot(back_ref[0], low) + dot(back_ref[1], high)


def conv_kernel(pair_ref, outer_ref, back_ref, twiddle_ref, inner_ref, conv_ref, spectra_ref, wide_ref):
    unroll(wide_ref, pair_ref[...])
    signal = transform(by_channel(wide_ref, 0, 16), outer_ref, twiddle_ref, inner_ref)
    kernel = transform(by_channel(wide_ref, 8, 16), outer_ref, twiddle_ref, inner_ref)
    spectra_ref[0] = signal
    spectra_ref[1] = kernel
    sr, si = signal[:, 0:128], signal[:, 128:256]
    kr, ki = kernel[:, 0:128], kernel[:, 128:256]
    result = restore(sr * kr - si * ki, sr * ki + si * kr, back_ref, twiddle_ref, inner_ref)
    by_slab(conv_ref, result, 0, 8)


def adjoint_kernel(
    pair_ref, spectra_ref, outer_ref, back_ref, twiddle_ref, inner_ref, grads_ref, wide_ref, out_ref
):
    unroll(wide_ref, pair_ref[...])
    spectrum = transform(by_channel(wide_ref, 8, 16), outer_ref, twiddle_ref, inner_ref)
    gr, gi = spectrum[:, 0:128], spectrum[:, 128:256]
    for field in range(2):
        real, imag = spectra_ref[1 - field, :, 0:128], spectra_ref[1 - field, :, 128:256]
        result = restore(
            gr * real + gi * imag, gi * real - gr * imag, back_ref, twiddle_ref, inner_ref
        )
        by_slab(out_ref, result, 0, 8)
        grads_ref[:, 512 * field : 512 * field + 512] = enroll(out_ref)


def conv_rows(pair_ref):
    wide = pair_ref[...].astype(F32)
    return jnp.concatenate([wide[16 * p : 16 * p + 8, :] for p in range(16)], axis=0)


def mix_kernel(pair_ref, gate_ref, blocks_ref, mix_ref):
    product = (conv_rows(pair_ref) * gate_ref[...]).astype(BF16)
    mix_ref[...] = dot(blocks_ref[...], product, TN).astype(BF16)


def first_kernel(pair_ref, gate_ref, returned_ref, own_ref, grad_gate_ref, partial_ref):
    conv = conv_rows(pair_ref)
    product = (conv * gate_ref[...]).astype(BF16)
    returned = returned_ref[...]
    grad_gate = (dot(own_ref[...], returned) * conv).astype(BF16)
    grad_gate_ref[...] = dot(grad_gate, unit(), TN).astype(BF16)
    row, col = iotas(128, 128)
    grad = jnp.where(row // 64 == col // 4 % 2, dot(product, returned, NT), 0.0)
    order = ones_where(
        (row // 8 == col % 64 // 4) & (row // 4 % 2 == col // 64) & (row % 4 == col % 4)
    )
    row, col = iotas(128, 64)
    fold = ones_where(source(row) * 4 + row % 4 == col)
    partial_ref[...] = dot(order, dot(grad.astype(BF16), fold).astype(BF16))


def second_kernel(received_ref, d_out_ref, partial_ref, grads_ref, sums_ref):
    row, col = iotas(128, 128)
    grad = jnp.where(row % 4 == col // 32, dot(received_ref[...], d_out_ref[...]), 0.0)
    row, col = iotas(128, 32)
    fold = ones_where(row % 32 == col)
    pieces = [partial_ref[...]] + [dot(piece, fold) for piece in split(grad)]
    sums_ref[:, 0:1024] = grads_ref[...]
    sums_ref[:, 1024:1152] = jnp.concatenate(pieces, axis=1).astype(BF16)


def exit_kernel(
    sums_ref, signal_hbm, filter_hbm, first_hbm, second_hbm, both_ref, first_ref, second_ref, sems
):
    copies = []

    def leave(source, target):
        copies.append(pltpu.make_async_copy(source, target, sems.at[len(copies)]))
        copies[-1].start()

    for field, target in enumerate((signal_hbm, filter_hbm)):
        values = sums_ref[:, 512 * field : 512 * field + 512]
        both_ref[field] = values.T
        leave(both_ref.at[field], target)
    wide = sums_ref[:, 1024:1152].astype(F32)
    total = wide[0:8, :]
    for p in range(1, 16):
        total = total + wide[8 * p : 8 * p + 8, :]
    second = total[:, 64:96] + total[:, 96:128]
    for i in range(2):
        first_ref[i] = total[4 * i : 4 * i + 4, 0:64]
        for k in range(4):
            second_ref[k, i : i + 1, :] = second[4 * i + k : 4 * i + k + 1, :]
    leave(first_ref, first_hbm)
    leave(second_ref, second_hbm)
    for copy in copies:
        copy.wait()


def call(body, outs, scratch=(), flops=1 << 26, moved=1 << 19, spaces=None):
    extra = {}
    if spaces is not None:
        extra["in_specs"], extra["out_specs"] = [
            [pl.BlockSpec(memory_space=space) for space in side] for side in spaces
        ]
    return pl.pallas_call(
        body,
        out_shape=[
            pltpu.VMEM(*out[:2]) if len(out) > 2 else jax.ShapeDtypeStruct(*out) for out in outs
        ],
        scratch_shapes=list(scratch),
        compiler_params=pltpu.CompilerParams(vmem_limit_bytes=32 << 20),
        cost_estimate=pl.CostEstimate(flops=flops, bytes_accessed=moved, transcendentals=0),
        **extra,
    )


def exchange(value, axis):
    rows, cols = value.shape
    pieces = value.reshape(16, rows // 16, cols)
    return lax.all_to_all(pieces, axis, split_axis=0, concat_axis=0, tiled=True).reshape(rows, cols)


def shift(value, y, zc):
    pairs = []
    for index in range(16):
        z, there, core = (index // 8 + zc // 2) % 2, (index // 2 + y) % 4, (index + zc) % 2
        pairs.append((index, z * 8 + there * 2 + core))
    return lax.ppermute(value, "ch", pairs)


def shards(signal, filter_raw, gate, d_out, w_first, w_second):
    rows, width = signal.shape
    outer, back, twiddle, inner = (jnp.asarray(t) for t in tables(lax.axis_size("seq"), rows))
    single, double = ((width, rows), BF16), ((2 * width, rows), BF16)
    slab = ((rows, width), BF16)
    quarter, half = ((width // 4, rows), BF16), ((width // 2, rows), BF16)
    held = [pltpu.with_memory_space_constraint(v, pltpu.HBM) for v in (d_out, w_second, signal, filter_raw)]
    near, core, far, pair = call(
        entry_kernel,
        [quarter + (True,), quarter + (True,), half + (True,), double],
        [
            pltpu.VMEM(d_out.shape, BF16),
            pltpu.VMEM(w_second.shape, BF16),
            pltpu.VMEM((2, rows, width), BF16),
            pltpu.VMEM((2 * width, rows), BF16),
            pltpu.SemaphoreType.DMA((5,)),
        ],
        spaces=([pl.ANY] * 4, [pltpu.VMEM] * 3 + [pl.ANY]),
    )(*held)
    far = shift(far, 0, 2)
    pair = exchange(pair, "seq")
    core = shift(call(core_kernel, [half], flops=1 << 35)(core, far)[0], 0, 1)
    near, *others = call(repack_kernel, [quarter] * 4)(near, core, far)
    pair = lax.optimization_barrier((pair, near))[0]
    others = [shift(value, y, 0) for y, value in zip((1, 2, 3), others)]
    square = ((128, 128), BF16)
    gate, blocks, own = call(prepare_kernel, [((width, rows), F32), square, square])(gate, w_first)
    conv, spectra = call(
        conv_kernel,
        [((4 * width, 128), F32), ((2, 512, 256), F32)],
        [pltpu.VMEM((2 * width * 4, 128), F32)],
        flops=1 << 30,
    )(pair, outer, back, twiddle, inner)
    pair, returned = call(gate_kernel, [double, single])(near, *others, own, gate, conv)
    pair = exchange(pair, "seq")
    mix = call(mix_kernel, [single])(pair, gate, blocks)[0]
    received = exchange(mix, "ch")
    grads = call(
        adjoint_kernel,
        [((width, 2 * rows), BF16)],
        [pltpu.VMEM((2 * width * 4, 128), F32), pltpu.VMEM((width * 4, 128), F32)],
        flops=1 << 30,
    )(pair, spectra, outer, back, twiddle, inner)[0]
    grad_gate, partial = call(first_kernel, [slab, ((width, 64), F32)])(
        pair, gate, returned, own
    )
    sums = call(second_kernel, [((width, 2 * rows + 128), BF16)])(received, d_out, partial, grads)[0]
    sums = exchange(sums, "seq")
    grad_signal, grad_filter, grad_first, grad_second = call(
        exit_kernel,
        [slab, slab, ((2, 4, 64), F32), ((4, 2, 32), F32)],
        [
            pltpu.VMEM((2, rows, width), BF16),
            pltpu.VMEM((2, 4, 64), F32),
            pltpu.VMEM((4, 2, 32), F32),
            pltpu.SemaphoreType.DMA((4,)),
        ],
        spaces=([pltpu.VMEM], [pl.ANY] * 4),
    )(sums)
    return (grad_signal, grad_filter, grad_gate, grad_first, grad_second)


def solution(mesh):
    in_specs = (
        P("seq", "ch"),
        P("seq", "ch"),
        P("seq", "ch"),
        P("seq", "ch"),
        P("ch", None, None),
        P("ch", None, None),
    )
    out_specs = (
        P("seq", "ch"),
        P("seq", "ch"),
        P("seq", "ch"),
        P("ch", "seq", None),
        P("ch", "seq", None),
    )
    return jax.shard_map(shards, mesh=mesh, in_specs=in_specs, out_specs=out_specs, check_vma=False)
```

```python
import math

import jax
import jax.numpy as jnp
import numpy as np
from jax import lax
from jax.experimental import pallas as pl
from jax.experimental.pallas import tpu as pltpu
from jax.sharding import PartitionSpec as P

F32 = jnp.float32
BF16 = jnp.bfloat16
NN = (((1,), (0,)), ((), ()))
NT = (((1,), (1,)), ((), ()))
TN = (((0,), (0,)), ((), ()))


def dot(a, b, form=NN):
    return lax.dot_general(a, b, form, preferred_element_type=F32)


def halves(table):
    high = table.astype(BF16)
    return high, (table - high.astype(np.float32)).astype(BF16)


def tables(devices, rows):
    lanes = 128
    length = 2 * devices * rows
    steps = devices * rows // lanes
    split = rows // lanes
    place = (np.arange(steps) % devices) * split + np.arange(steps) // devices
    turn = 2.0 * math.pi
    freq = np.arange(steps) + 0.5
    angle = turn * freq[:, None] * place[None, :] / (2 * steps)
    outer = np.concatenate([np.cos(angle), -np.sin(angle)], 0)
    scale = float(devices * rows) ** -0.5 * 2.0 / length
    back = scale * np.concatenate([np.cos(angle.T), -np.sin(angle.T)], 1)
    angle = turn * freq[:, None] * np.arange(lanes)[None, :] / length
    twiddle = np.concatenate([np.cos(angle), -np.sin(angle)], 1)
    angle = turn * (np.arange(lanes)[:, None] * np.arange(lanes)[None, :] % lanes) / lanes
    cosine, sine = np.cos(angle), np.sin(angle)
    inner = np.concatenate(
        [np.concatenate([cosine, -sine], 1), np.concatenate([sine, cosine], 1)], 0
    )
    outer_high, outer_low = halves(outer.astype(np.float32))
    back_high, back_low = halves(back.astype(np.float32))
    inner_high, inner_low = halves(inner.astype(np.float32))
    return (
        np.concatenate([outer_high, outer_low], 1),
        np.concatenate([back_high, back_low], 0),
        twiddle.astype(np.float32),
        np.stack([inner_high, inner_low]),
    )


def iotas(rows, cols):
    return (
        lax.broadcasted_iota(jnp.int32, (rows, cols), 0),
        lax.broadcasted_iota(jnp.int32, (rows, cols), 1),
    )


def ones_where(mask):
    return jnp.where(mask, 1.0, 0.0).astype(BF16)


def pair_order():
    row, col = iotas(256, 256)
    return ones_where((row // 16 == col % 128 // 8) & (row // 8 % 2 == col // 128) & (row % 8 == col % 8))


def unit():
    row, col = iotas(128, 128)
    return ones_where(row == col)


def place():
    index = lax.axis_index("ch")
    return index // 8, index // 2 % 4, index % 2


def partner(slot_y, slot_zc, step):
    z, y, core = place()
    z = (z + slot_zc // 2) % 2
    core = (core + slot_zc) % 2
    y = (y + 4 + step * slot_y) % 4
    return z * 8 + y * 2 + core


def entry_kernel(
    d_out_hbm,
    w_second_hbm,
    signal_hbm,
    filter_hbm,
    near_ref,
    core_ref,
    far_ref,
    pair_hbm,
    d_out_ref,
    w_second_ref,
    both_ref,
    pair_ref,
    sems,
):
    copies = [
        pltpu.make_async_copy(source, target, sems.at[index])
        for index, (source, target) in enumerate(
            (
                (signal_hbm, both_ref.at[0]),
                (filter_hbm, both_ref.at[1]),
                (w_second_hbm, w_second_ref),
                (d_out_hbm, d_out_ref),
            )
        )
    ]
    for copy in copies:
        copy.start()
    pairs = pair_order()
    row, col = iotas(32, 128)
    copies_of = ones_where(row == col % 32)
    row, col = iotas(128, 128)
    keep = row // 32 == col // 32
    block = 2 * partner(row // 8 % 4, row // 32, 1) + row // 4 % 2
    order = ones_where((block == col % 32) & (row % 4 == col // 32))
    copies[0].wait()
    copies[1].wait()
    both = jnp.concatenate([both_ref[0], both_ref[1]], axis=1)
    pair_ref[...] = dot(pairs, both, NT).astype(BF16)
    leave = pltpu.make_async_copy(pair_ref, pair_hbm, sems.at[4])
    leave.start()
    copies[2].wait()
    flat = w_second_ref[...].reshape(128, 32)
    spread = jnp.where(keep, dot(flat, copies_of), 0.0).astype(BF16)
    weights = dot(order, spread).astype(BF16)
    copies[3].wait()
    result = dot(weights, d_out_ref[...], NT).astype(BF16)
    for ref, start in zip((near_ref, core_ref, far_ref), (0, 32, 64)):
        ref[...] = result[start : start + ref.shape[0], :]
    leave.wait()


def core_kernel(core_ref, far_ref, message_ref):
    message_ref[0:32, :] = core_ref[...]
    message_ref[32:64, :] = far_ref[32:64, :]


def repack_kernel(near_ref, core_ref, far_ref, *outs):
    near, core, far = (ref[...].astype(F32) for ref in (near_ref, core_ref, far_ref))
    values = (near, core[0:32, :], far[0:32, :], core[32:64, :])
    for y, ref in enumerate(outs):
        ref[...] = jnp.concatenate([v[8 * y : 8 * y + 8, :] for v in values], axis=0).astype(BF16)


def source(col):
    return partner(col // 32, col // 8 % 4, -1)


def prepare_kernel(gate_ref, w_first_ref, gate_out_ref, blocks_ref, own_ref):
    flat = w_first_ref[...].reshape(128, 64)
    row, col = iotas(64, 128)
    keep_row, keep_col = iotas(128, 128)
    keep = keep_row // 64 == keep_col // 4 % 2
    for ref, group in ((blocks_ref, col // 8), (own_ref, source(col))):
        spread = dot(flat, ones_where(row == group * 4 + col % 4))
        ref[...] = jnp.where(keep, spread, 0.0).astype(BF16)
    gate_out_ref[...] = dot(unit(), gate_ref[...], NT)


def gate_kernel(near_ref, first_ref, second_ref, third_ref, own_ref, gate_ref, conv_ref, pair_ref, returned_ref):
    pieces = [ref[...] for ref in (near_ref, first_ref, second_ref, third_ref)]
    returned = jnp.concatenate(pieces, axis=0)
    returned_ref[...] = returned
    incoming = dot(own_ref[...], returned) * gate_ref[...]
    rows = []
    for p in range(16):
        pieces = [conv_ref[128 * th + 8 * p : 128 * th + 8 * p + 8, :] for th in range(4)]
        rows.append(jnp.concatenate(pieces, axis=1))
        rows.append(incoming[8 * p : 8 * p + 8, :])
    pair_ref[...] = jnp.concatenate(rows, axis=0).astype(BF16)


def split(value):
    high = value.astype(BF16)
    return high, (value - high.astype(F32)).astype(BF16)


def by_channel(wide_ref, first, stride):
    columns = [wide_ref[pl.ds(first + c, 64, stride=stride), :] for c in range(8)]
    return jnp.concatenate(columns, axis=1).astype(BF16)


def by_slab(wide_ref, value, first, stride):
    for c in range(8):
        wide_ref[pl.ds(first + c, 64, stride=stride), :] = value[:, 128 * c : 128 * c + 128]


def unroll(wide_ref, value):
    rows = value.shape[0]
    for th in range(4):
        wide_ref[rows * th : rows * th + rows, :] = value[:, 128 * th : 128 * th + 128].astype(F32)


def enroll(wide_ref):
    rows = wide_ref.shape[0] // 4
    pieces = [wide_ref[rows * th : rows * th + rows, :].astype(BF16) for th in range(4)]
    return jnp.concatenate(pieces, axis=1)


def transform(values, outer_ref, twiddle_ref, inner_ref):
    stage = dot(outer_ref[...], jnp.concatenate([values, values], axis=0))
    cosine, sine = twiddle_ref[:, 0:128], twiddle_ref[:, 128:256]
    rows = []
    for c in range(8):
        real = stage[0:64, 128 * c : 128 * c + 128]
        imag = stage[64:128, 128 * c : 128 * c + 128]
        rows.append(
            jnp.concatenate([real * cosine - imag * sine, real * sine + imag * cosine], axis=1)
        )
    high, low = split(jnp.concatenate(rows, axis=0))
    return dot(high, inner_ref[0]) + dot(low, inner_ref[0]) + dot(high, inner_ref[1])


def restore(real, imag, back_ref, twiddle_ref, inner_ref):
    high, low = split(jnp.concatenate([real, imag], axis=1))
    stage = dot(high, inner_ref[0], NT) + dot(low, inner_ref[0], NT) + dot(high, inner_ref[1], NT)
    cosine, sine = twiddle_ref[:, 0:128], twiddle_ref[:, 128:256]
    columns = []
    for c in range(8):
        real = stage[64 * c : 64 * c + 64, 0:128]
        imag = stage[64 * c : 64 * c + 64, 128:256]
        columns.append(
            jnp.concatenate([real * cosine + imag * sine, imag * cosine - real * sine], axis=0)
        )
    high, low = split(jnp.concatenate(columns, axis=1))
    both = dot(back_ref[...], high)
    return both[0:64, :] + both[64:128, :] + dot(back_ref[0:64, :], low)


def conv_kernel(pair_ref, outer_ref, back_ref, twiddle_ref, inner_ref, conv_ref, spectra_ref, wide_ref):
    unroll(wide_ref, pair_ref[...])
    signal = transform(by_channel(wide_ref, 0, 16), outer_ref, twiddle_ref, inner_ref)
    kernel = transform(by_channel(wide_ref, 8, 16), outer_ref, twiddle_ref, inner_ref)
    spectra_ref[0] = signal
    spectra_ref[1] = kernel
    sr, si = signal[:, 0:128], signal[:, 128:256]
    kr, ki = kernel[:, 0:128], kernel[:, 128:256]
    result = restore(sr * kr - si * ki, sr * ki + si * kr, back_ref, twiddle_ref, inner_ref)
    by_slab(conv_ref, result, 0, 8)


def adjoint_kernel(
    pair_ref, spectra_ref, outer_ref, back_ref, twiddle_ref, inner_ref, grads_ref, wide_ref, out_ref
):
    unroll(wide_ref, pair_ref[...])
    spectrum = transform(by_channel(wide_ref, 8, 16), outer_ref, twiddle_ref, inner_ref)
    gr, gi = spectrum[:, 0:128], spectrum[:, 128:256]
    for field in range(2):
        real, imag = spectra_ref[1 - field, :, 0:128], spectra_ref[1 - field, :, 128:256]
        result = restore(
            gr * real + gi * imag, gi * real - gr * imag, back_ref, twiddle_ref, inner_ref
        )
        by_slab(out_ref, result, 0, 8)
        grads_ref[:, 512 * field : 512 * field + 512] = enroll(out_ref)


def conv_rows(pair_ref):
    wide = pair_ref[...].astype(F32)
    return jnp.concatenate([wide[16 * p : 16 * p + 8, :] for p in range(16)], axis=0)


def mix_kernel(pair_ref, gate_ref, blocks_ref, mix_ref):
    product = (conv_rows(pair_ref) * gate_ref[...]).astype(BF16)
    mix_ref[...] = dot(blocks_ref[...], product, TN).astype(BF16)


def first_kernel(pair_ref, gate_ref, returned_ref, own_ref, grad_gate_ref, partial_ref):
    conv = conv_rows(pair_ref)
    product = (conv * gate_ref[...]).astype(BF16)
    returned = returned_ref[...]
    grad_gate = (dot(own_ref[...], returned) * conv).astype(BF16)
    grad_gate_ref[...] = dot(grad_gate, unit(), TN).astype(BF16)
    row, col = iotas(128, 128)
    grad = jnp.where(row // 64 == col // 4 % 2, dot(product, returned, NT), 0.0)
    order = ones_where(
        (row // 8 == col % 64 // 4) & (row // 4 % 2 == col // 64) & (row % 4 == col % 4)
    )
    row, col = iotas(128, 64)
    fold = ones_where(source(row) * 4 + row % 4 == col)
    partial_ref[...] = dot(order, dot(grad.astype(BF16), fold).astype(BF16))


def second_kernel(received_ref, d_out_ref, partial_ref, grads_ref, sums_ref):
    row, col = iotas(128, 128)
    grad = jnp.where(row % 4 == col // 32, dot(received_ref[...], d_out_ref[...]), 0.0)
    row, col = iotas(128, 32)
    fold = ones_where(row % 32 == col)
    pieces = [partial_ref[...]] + [dot(piece, fold) for piece in split(grad)]
    sums_ref[:, 0:1024] = grads_ref[...]
    sums_ref[:, 1024:1152] = jnp.concatenate(pieces, axis=1).astype(BF16)


def exit_kernel(
    sums_ref, signal_hbm, filter_hbm, first_hbm, second_hbm, both_ref, first_ref, second_ref, sems
):
    copies = []

    def leave(source, target):
        copies.append(pltpu.make_async_copy(source, target, sems.at[len(copies)]))
        copies[-1].start()

    square = unit()
    for field, target in enumerate((signal_hbm, filter_hbm)):
        values = sums_ref[:, 512 * field : 512 * field + 512]
        both_ref[field] = dot(values, square, TN).astype(BF16)
        leave(both_ref.at[field], target)
    wide = sums_ref[:, 1024:1152].astype(F32)
    total = wide[0:8, :]
    for p in range(1, 16):
        total = total + wide[8 * p : 8 * p + 8, :]
    second = total[:, 64:96] + total[:, 96:128]
    for i in range(2):
        first_ref[i] = total[4 * i : 4 * i + 4, 0:64]
        for k in range(4):
            second_ref[k, i : i + 1, :] = second[4 * i + k : 4 * i + k + 1, :]
    leave(first_ref, first_hbm)
    leave(second_ref, second_hbm)
    for copy in copies:
        copy.wait()


def call(body, outs, scratch=(), flops=1 << 26, moved=1 << 19, spaces=None):
    extra = {}
    if spaces is not None:
        extra["in_specs"], extra["out_specs"] = [
            [pl.BlockSpec(memory_space=space) for space in side] for side in spaces
        ]
    return pl.pallas_call(
        body,
        out_shape=[
            pltpu.VMEM(*out[:2]) if len(out) > 2 else jax.ShapeDtypeStruct(*out) for out in outs
        ],
        scratch_shapes=list(scratch),
        compiler_params=pltpu.CompilerParams(vmem_limit_bytes=32 << 20),
        cost_estimate=pl.CostEstimate(flops=flops, bytes_accessed=moved, transcendentals=0),
        **extra,
    )


def exchange(value, axis):
    rows, cols = value.shape
    pieces = value.reshape(16, rows // 16, cols)
    return lax.all_to_all(pieces, axis, split_axis=0, concat_axis=0, tiled=True).reshape(rows, cols)


def shift(value, y, zc):
    pairs = []
    for index in range(16):
        z, there, core = (index // 8 + zc // 2) % 2, (index // 2 + y) % 4, (index + zc) % 2
        pairs.append((index, z * 8 + there * 2 + core))
    return lax.ppermute(value, "ch", pairs)


def shards(signal, filter_raw, gate, d_out, w_first, w_second):
    rows, width = signal.shape
    outer, back, twiddle, inner = (jnp.asarray(t) for t in tables(lax.axis_size("seq"), rows))
    single, double = ((width, rows), BF16), ((2 * width, rows), BF16)
    slab = ((rows, width), BF16)
    quarter, half = ((width // 4, rows), BF16), ((width // 2, rows), BF16)
    held = [pltpu.with_memory_space_constraint(v, pltpu.HBM) for v in (d_out, w_second, signal, filter_raw)]
    near, core, far, pair = call(
        entry_kernel,
        [quarter + (True,), quarter + (True,), half + (True,), double],
        [
            pltpu.VMEM(d_out.shape, BF16),
            pltpu.VMEM(w_second.shape, BF16),
            pltpu.VMEM((2, rows, width), BF16),
            pltpu.VMEM((2 * width, rows), BF16),
            pltpu.SemaphoreType.DMA((5,)),
        ],
        spaces=([pl.ANY] * 4, [pltpu.VMEM] * 3 + [pl.ANY]),
    )(*held)
    far = shift(far, 0, 2)
    pair = exchange(pair, "seq")
    core = shift(call(core_kernel, [half], flops=1 << 35)(core, far)[0], 0, 1)
    near, *others = call(repack_kernel, [quarter] * 4)(near, core, far)
    pair = lax.optimization_barrier((pair, near))[0]
    others = [shift(value, y, 0) for y, value in zip((1, 2, 3), others)]
    square = ((128, 128), BF16)
    gate, blocks, own = call(prepare_kernel, [((width, rows), F32), square, square])(gate, w_first)
    conv, spectra = call(
        conv_kernel,
        [((4 * width, 128), F32), ((2, 512, 256), F32)],
        [pltpu.VMEM((2 * width * 4, 128), F32)],
        flops=1 << 30,
    )(pair, outer, back, twiddle, inner)
    pair, returned = call(gate_kernel, [double, single])(near, *others, own, gate, conv)
    pair = exchange(pair, "seq")
    mix = call(mix_kernel, [single])(pair, gate, blocks)[0]
    received = exchange(mix, "ch")
    grads = call(
        adjoint_kernel,
        [((width, 2 * rows), BF16)],
        [pltpu.VMEM((2 * width * 4, 128), F32), pltpu.VMEM((width * 4, 128), F32)],
        flops=1 << 30,
    )(pair, spectra, outer, back, twiddle, inner)[0]
    grad_gate, partial = call(first_kernel, [slab, ((width, 64), F32)])(
        pair, gate, returned, own
    )
    sums = call(second_kernel, [((width, 2 * rows + 128), BF16)])(received, d_out, partial, grads)[0]
    sums = exchange(sums, "seq")
    grad_signal, grad_filter, grad_first, grad_second = call(
        exit_kernel,
        [slab, slab, ((2, 4, 64), F32), ((4, 2, 32), F32)],
        [
            pltpu.VMEM((2, rows, width), BF16),
            pltpu.VMEM((2, 4, 64), F32),
            pltpu.VMEM((4, 2, 32), F32),
            pltpu.SemaphoreType.DMA((4,)),
        ],
        spaces=([pltpu.VMEM], [pl.ANY] * 4),
    )(sums)
    return (grad_signal, grad_filter, grad_gate, grad_first, grad_second)


def solution(mesh):
    in_specs = (
        P("seq", "ch"),
        P("seq", "ch"),
        P("seq", "ch"),
        P("seq", "ch"),
        P("ch", None, None),
        P("ch", None, None),
    )
    out_specs = (
        P("seq", "ch"),
        P("seq", "ch"),
        P("seq", "ch"),
        P("ch", "seq", None),
        P("ch", "seq", None),
    )
    return jax.shard_map(shards, mesh=mesh, in_specs=in_specs, out_specs=out_specs, check_vma=False)
```
